512 devices in a mesh: strip: 128 (over x, z, y_hi), cells: 4 (over y_lo, core).
Axes of the slice: x: 4, y: 4 (y_hi: 2, y_lo: 2; y = y_hi * 2 + y_lo), z: 16, core: 2. Of those that a mesh axis runs over, the one named last changes fastest.
Arguments:
- pin_rows: int32 [2097152], P(('strip', 'cells')), may hold values from 0 to 2
- pin_cols: int32 [2097152], P(('strip', 'cells')), may hold values from 0 to 2558
- pin_fracs: float32 [2, 2097152], P(None, ('strip', 'cells')), may hold values from 0 to 1
- pin_weights: float32 [2097152], P(('strip', 'cells')), may hold values from 0.5 to 1.5
- capacity: int32 [512, 2560], P('strip', 'cells'), may hold values from 1 to 4
- blockage: float32 [512, 2560], P('strip', 'cells'), may hold values from 0 to 0.5
- row_blocks: float32 [20, 128, 128], P('cells'), may hold values from -0.002 to 0.15
- col_blocks: float32 [4, 128, 128], replicated, may hold values from -0.002 to 0.15
Outputs:
- final_density: float32 [512, 2560], P('strip', 'cells')
- pin_velocity: float32 [2, 2097152], P(None, ('strip', 'cells'))
The draws below stay inside these ranges and needn't reach their ends.
All inputs are finite; a program needn't handle non-finite values.
Results may differ from the reference program's by a relative error of at most 0.0052.
Values may be sent and summed in bfloat16 or wider, within the bound.
A program may use at most 64 MiB of HBM per device.

```python
import jax
import jax.numpy as jnp
from jax import lax

RD = 4
BLK = 128
SWEEPS = 3
STEPS = 2
NROW = 512
NCOL = 2560
PINS_STRIP = 16384
PINS = 2097152
BLKY = 128
NBX = 20
NBY = 4


coupling = 2.0


def block_inverses(key, block_count, block_size):
    first_key, second_key = jax.random.split(key)
    reference_level = jnp.exp(jax.random.uniform(first_key, (block_count, 1, 1), jnp.float32, jnp.log(4.0), jnp.log(6.0)))
    shift_rate = reference_level / coupling
    cosh_value = 1.0 + 0.5 * shift_rate
    angle_rate = jnp.log(cosh_value + jnp.sqrt(cosh_value * cosh_value - 1.0))
    positions = jnp.arange(1, block_size + 1).astype(jnp.float32)
    row_pos = positions[None, :, None]
    col_pos = positions[None, None, :]
    spread = jnp.abs(row_pos - col_pos)
    position_sum = row_pos + col_pos
    far_ends = 2.0 * (block_size + 1)
    numerator = jnp.exp(-spread * angle_rate) - jnp.exp(-(far_ends - position_sum) * angle_rate) - jnp.exp(-position_sum * angle_rate) + jnp.exp(-(far_ends - spread) * angle_rate)
    denominator = 2.0 * jnp.sinh(angle_rate) * (1.0 - jnp.exp(-far_ends * angle_rate)) * coupling
    noise = jax.random.uniform(second_key, (block_count, block_size, block_size), jnp.float32, -0.002, 0.002)
    return numerator / denominator + noise


def draw_row_blocks(key, part):
    return block_inverses(jax.random.fold_in(key, 11), NBX, BLK)


def draw_col_blocks(key, part):
    return block_inverses(jax.random.fold_in(key, 23), NBY, BLKY)


def set_ends(drawn, stream_key, low, largest):
    extent = drawn.shape
    index_at = [jax.random.randint(jax.random.fold_in(stream_key, axis), (), 0, extent[axis]) for axis in range(len(extent))]
    drawn = drawn.at[tuple(index_at)].set(low)
    longest = extent.index(max(extent))
    index_at[longest] = (index_at[longest] + 1) % extent[longest]
    return drawn.at[tuple(index_at)].set(largest)


def levels(own_key, dims, cuts, smallest, high):
    loudness, own = 1.0, jax.random.fold_in(own_key, 6)
    for position, blocks in cuts:
        steps = jnp.exp(jax.random.uniform(jax.random.fold_in(own, position), (blocks,), jnp.float32, smallest / len(cuts), high / len(cuts)))
        loudness = loudness * jnp.repeat(steps, dims[position] // blocks).reshape([-1 if axis == position else 1 for axis in range(len(dims))])
    return loudness


def setup_inputs(seed: int = 0) -> dict:
    arg_keys = jax.random.split(jax.random.key(seed), 9)
    pin_rows = set_ends(jax.random.randint(arg_keys[0], (PINS,), 0, RD - 1), jax.random.fold_in(arg_keys[0], 1), 0, (RD - 1) - 1).astype(jnp.int32)
    pin_cols = set_ends(jax.random.randint(arg_keys[1], (PINS,), 0, NCOL - 1), jax.random.fold_in(arg_keys[1], 1), 0, (NCOL - 1) - 1).astype(jnp.int32)
    pin_fracs = jnp.clip(1.0 * jax.random.uniform(arg_keys[2], (2, PINS), jnp.float32) ** levels(arg_keys[2], (2, PINS), ((1, 512),), -0.2, 0.2), 0.0, 1.0)
    pin_weights = jnp.clip(0.5 + 1.0 * jax.random.uniform(arg_keys[3], (PINS,), jnp.float32) ** levels(arg_keys[3], (PINS,), ((0, 512),), -0.2, 0.2), 0.5, 1.5)
    capacity = set_ends(jax.random.randint(arg_keys[4], (NROW, NCOL), 1, 5), jax.random.fold_in(arg_keys[4], 1), 1, 4).astype(jnp.int32)
    blockage = jnp.clip(0.5 * jax.random.uniform(arg_keys[5], (NROW, NCOL), jnp.float32) ** levels(arg_keys[5], (NROW, NCOL), ((0, 128), (1, 4)), -0.2, 0.2), 0.0, 0.5)
    row_blocks = draw_row_blocks(jax.random.fold_in(arg_keys[8], 71), 0)
    col_blocks = draw_col_blocks(jax.random.fold_in(arg_keys[8], 71), 0)
    return dict(pin_rows=pin_rows, pin_cols=pin_cols, pin_fracs=pin_fracs, pin_weights=pin_weights, capacity=capacity, blockage=blockage, row_blocks=row_blocks, col_blocks=col_blocks)


coupling = 2.0
floor_level = 0.5
highest = lax.Precision.HIGHEST


def along_lines(values):
    padded = jnp.pad(values, ((0, 0), (1, 1)), mode="edge")
    return 2.0 * values - padded[:, :-2] - padded[:, 2:]


def across_lines(values):
    padded = jnp.pad(values, ((1, 1), (0, 0)), mode="edge")
    return 2.0 * values - padded[:-2] - padded[2:]


def blockwise(residual, blocks):
    leading = residual.shape[0]
    pieces = residual.reshape(leading, blocks.shape[0], blocks.shape[1])
    result = jnp.einsum("rnj,nij->rni", pieces, blocks, precision=highest)
    return result.reshape(leading, blocks.shape[0] * blocks.shape[1])


def line_solve(source, weights, start_iterate, blocks):
    iterate = start_iterate
    for sweep_index in range(SWEEPS):
        residual = source - (weights * iterate + coupling * along_lines(iterate))
        iterate = iterate + blockwise(residual, blocks)
    return iterate


def rounded(values):
    return lax.optimization_barrier(values.astype(jnp.bfloat16)).astype(jnp.float32)


def reference(pin_rows, pin_cols, pin_fracs, pin_weights, capacity, blockage, row_blocks, col_blocks):
    weights = capacity.astype(jnp.float32) * (1.0 - blockage)
    strip_of = (jnp.arange(PINS) // PINS_STRIP).astype(jnp.int32)
    global_rows = strip_of * RD + pin_rows
    near_y = 1.0 - pin_fracs[0]
    near_x = 1.0 - pin_fracs[1]
    splat_rows = [rounded(pin_weights * near_y), rounded(pin_weights * pin_fracs[0])]
    look_rows = [rounded(near_y), rounded(pin_fracs[0])]
    col_factors = [rounded(near_x), rounded(pin_fracs[1])]
    density = jnp.zeros((NROW, NCOL), jnp.float32)
    for row_offset in range(2):
        for col_offset in range(2):
            density = density.at[global_rows + row_offset, pin_cols + col_offset].add(
                splat_rows[row_offset] * col_factors[col_offset])
    current = density / weights
    source = weights * current - coupling * across_lines(current)
    for step_index in range(STEPS):
        current = line_solve(source, weights, current, row_blocks)
        middle = weights * current - coupling * along_lines(current)
        current = line_solve(middle.T, weights.T, current.T, col_blocks).T
        if step_index + 1 < STEPS:
            source = weights * current - coupling * across_lines(current)
    padded_cols = jnp.pad(current, ((0, 0), (1, 1)), mode="edge")
    padded_rows = jnp.pad(current, ((1, 1), (0, 0)), mode="edge")
    scale = jnp.maximum(current, floor_level)
    velocity_x = rounded(-(0.5 * (padded_cols[:, 2:] - padded_cols[:, :-2])) / scale)
    velocity_y = rounded(-(0.5 * (padded_rows[2:] - padded_rows[:-2])) / scale)
    total_y = jnp.zeros((PINS,), jnp.float32)
    total_x = jnp.zeros((PINS,), jnp.float32)
    for row_offset in range(2):
        for col_offset in range(2):
            factor = look_rows[row_offset] * col_factors[col_offset]
            total_y = total_y + factor * velocity_y[global_rows + row_offset, pin_cols + col_offset]
            total_x = total_x + factor * velocity_x[global_rows + row_offset, pin_cols + col_offset]
    return current, jnp.stack([total_y, total_x])
```

```python
import functools

import jax
import jax.numpy as jnp
from jax import lax
from jax.experimental import pallas as pl
from jax.experimental.pallas import tpu as pltpu
from jax.sharding import PartitionSpec as P

SWEEPS = 3
STEPS = 2
coupling = 2.0
floor_level = 0.5
f32 = jnp.float32
bf16 = jnp.bfloat16


def exact_parts(values):
    high = values.astype(bf16)
    return high, (values - high.astype(f32)).astype(bf16)


def row_product(values, high_ref, low_ref):
    pieces = []
    for n in range(high_ref.shape[0]):
        high, low = exact_parts(values[:, 128 * n : 128 * (n + 1)])
        dims = (((1,), (1,)), ((), ()))
        dot = functools.partial(lax.dot_general, dimension_numbers=dims, preferred_element_type=f32)
        pieces.append(
            dot(high, high_ref[n]) + (dot(low, high_ref[n]) + dot(high, low_ref[n]))
        )
    return jnp.concatenate(pieces, axis=1)


def col_product(matrix, values):
    high, low = exact_parts(values)
    dot = functools.partial(jnp.dot, preferred_element_type=f32)
    return dot(matrix[0], high) + (dot(matrix[0], low) + dot(matrix[1], high))


def adi_kernel(
    sizes,
    part_ref,
    cap_ref,
    blk_ref,
    rowb_ref,
    colb_ref,
    density_ref,
    vel_ref,
    edge_part,
    part_recv,
    edge_recv,
    wedge_send,
    wedge_recv,
    w_send,
    w_plane,
    w_block,
    rowb_high,
    rowb_low,
    colb_parts,
    rim_send,
    rim_recv,
    field_send,
    field_plane,
    field_block,
    padded,
    answer_send,
    answer_near,
    near_send,
    near,
    still_send,
    still_recv,
    still_all,
    tops_send,
    tops_recv,
    tops_all,
    inflow,
    last_send,
    last_recv,
    send_sem,
    recv_sem,
):
    K, Q, C, RD, NC, BL = sizes
    strips = K * Q
    HC = w_send.shape[2]
    cut = NC - HC
    depth = Q // 2
    strip = lax.axis_index("strip")
    cell = lax.axis_index("cells")
    plane = strip // Q
    place = strip % Q
    half = strip % 2
    first_cell, last_cell = cell == 0, cell == C - 1
    first_plane, last_plane = plane == 0, plane == K - 1

    def at(strip_id, cell_id):
        return (strip_id, cell_id)

    cell_peers = [at(strip, (cell + d) % C) for d in range(1, C)]
    above_strip, below_strip = (strip + strips - 1) % strips, (strip + 1) % strips
    offsets = [(dz, dy) for dz in range(depth) for dy in range(2) if (dz, dy) != (0, 0)]
    offsets.sort(key=lambda o: -(min(o[0], depth - o[0]) + 2 * o[1]))
    plane_peers = []
    for dz, dy in offsets:
        other = ((place // 2 + dz) % depth) * 2 + (place % 2 + dy) % 2
        plane_peers.append((at(plane * Q + other, cell), (half + dy) % 2))
    partner = at(strip + 1 - 2 * half, cell)
    shifts = [(dk, dy) for dk in range(K) for dy in range(2) if (dk, dy) != (0, 0)]
    shifts.sort(key=lambda o: -(min(o[0], K - o[0]) + 2 * o[1]))
    plane_cross = [
        at(((plane + dk) % K) * Q + place + dy * (1 - 2 * half), cell) for dk, dy in shifts
    ]
    slot = 2 * plane + half
    row_peers = [at(s, (cell + d) % C) for s in (above_strip, below_strip) for d in range(C)]

    barrier = pltpu.get_barrier_semaphore()
    greeted = cell_peers + [p for p, _ in plane_peers] + plane_cross + row_peers
    for peer in greeted:
        pl.semaphore_signal(barrier, 1, device_id=peer, device_id_type=pl.DeviceIdType.MESH)

    sent = []

    def send(group, source, target, peer):
        pltpu.make_async_remote_copy(
            src_ref=source,
            dst_ref=target,
            send_sem=send_sem.at[group],
            recv_sem=recv_sem.at[group],
            device_id=peer,
            device_id_type=pl.DeviceIdType.MESH,
        ).start()

    def arrived(group, span):
        sent.append((group, span))
        pltpu.make_async_copy(span, span, recv_sem.at[group]).wait()

    weights = cap_ref[...].astype(f32) * (1.0 - blk_ref[...])
    w_send[0] = weights[:, :HC]
    w_send[1] = weights[:, cut:]
    w_plane[place] = w_send[half]
    wedge_send[0] = weights[:1]
    wedge_send[1] = weights[RD - 1 :]
    for c in range(C):
        edge_part[0, c] = part_ref[c, :1]
        edge_part[1, c] = part_ref[c, RD - 1 :]
    pl.semaphore_wait(barrier, len(greeted))

    for d in range(C):
        other = (cell + d) % C
        send(1, edge_part.at[0, other], edge_recv.at[1, cell], at(above_strip, other))
        send(1, edge_part.at[1, other], edge_recv.at[0, cell], at(below_strip, other))
    send(2, wedge_send.at[0], wedge_recv.at[1], at(above_strip, cell))
    send(2, wedge_send.at[1], wedge_recv.at[0], at(below_strip, cell))
    for d in range(1, C):
        other = (cell + d) % C
        send(0, part_ref.at[other], part_recv.at[C - 1 - d], at(strip, other))
    for peer, other_half in plane_peers:
        send(3, w_send.at[other_half], w_plane.at[place], peer)

    for n in range(rowb_ref.shape[0]):
        high, low = exact_parts(rowb_ref[n])
        rowb_high[n] = high
        rowb_low[n] = low
    high, low = exact_parts(colb_ref[plane])
    colb_parts[0] = high
    colb_parts[1] = low

    end = lax.broadcasted_iota(jnp.int32, (RD, HC), 1)

    def along_inside(values):
        left = pltpu.roll(values, 1, 1)
        right = pltpu.roll(values, NC - 1, 1)
        spot = lax.broadcasted_iota(jnp.int32, values.shape, 1)
        left = jnp.where(spot == 0, jnp.where(first_cell, values, 0.0), left)
        right = jnp.where(spot == NC - 1, jnp.where(last_cell, values, 0.0), right)
        return 2.0 * values - left - right

    weights_two = jnp.concatenate([weights, weights], axis=0)
    spot = lax.broadcasted_iota(jnp.int32, (2 * RD, NC), 1)
    row = lax.broadcasted_iota(jnp.int32, (2 * RD, NC), 0)
    unit = jnp.where(spot == jnp.where(row < RD, 0, NC - 1), coupling, 0.0)
    pulse = row_product(unit, rowb_high, rowb_low)
    pulses = [pulse]
    for _ in range(SWEEPS - 1):
        back = weights_two * pulse + coupling * along_inside(pulse)
        pulse = pulse - row_product(back, rowb_high, rowb_low)
        pulses.append(pulse)

    arrived(1, edge_recv)
    arrived(2, wedge_recv)
    arrived(0, part_recv.at[0 : C - 1])
    density = part_ref[cell]
    for d in range(C - 1):
        density = density + part_recv[d]
    current = density / weights
    row_above = edge_recv[0, 0]
    row_below = edge_recv[1, 0]
    for c in range(1, C):
        row_above = row_above + edge_recv[0, c]
        row_below = row_below + edge_recv[1, c]
    row_above = row_above / wedge_recv[0]
    row_below = row_below / wedge_recv[1]
    row_above = jnp.where(strip == 0, current[:1], row_above)
    row_below = jnp.where(strip == strips - 1, current[RD - 1 :], row_below)

    def frames():
        base = pl.multiple_of(RD * 2 * (place // 2), 2 * RD)
        inner = padded[pl.ds(base + 8, 2 * RD), :]
        over = padded[pl.ds(base + 7, 1), :]
        under = padded[pl.ds(base + 8 + 2 * RD, 1), :]
        fill = jnp.zeros((6 - RD, HC), f32)
        upper = jnp.concatenate([over, inner[: RD + 1], fill], axis=0)
        lower = jnp.concatenate([inner[RD - 1 :], under, fill], axis=0)
        return jnp.where(half == 0, upper, lower), jnp.where(half == 0, lower, upper)

    small = lax.broadcasted_iota(jnp.int32, (RD, 128), 1)

    def clamp_rows(values):
        shape = values.shape
        spot = lax.broadcasted_iota(jnp.int32, shape, 0)
        up = pltpu.roll(values, 1, 0)
        down = pltpu.roll(values, shape[0] - 1, 0)
        up = jnp.where(spot == 0, jnp.where(first_plane, values, 0.0), up)
        down = jnp.where(spot == shape[0] - 1, jnp.where(last_plane, values, 0.0), down)
        return 2.0 * values - up - down

    for step in range(STEPS):
        up = jnp.concatenate([row_above, current[: RD - 1]], axis=0)
        down = jnp.concatenate([current[1:], row_below], axis=0)
        source = weights * current - coupling * (2.0 * current - up - down)
        iterate = current
        levels = [iterate]
        for _ in range(SWEEPS):
            left_over = source - (weights * iterate + coupling * along_inside(iterate))
            iterate = iterate + row_product(left_over, rowb_high, rowb_low)
            levels.append(iterate)
        for side, column in ((0, 0), (1, NC - 1)):
            message = jnp.zeros((RD, 128), f32)
            for j in range(SWEEPS + 1):
                message = jnp.where(small == j, levels[j][:, column : column + 1], message)
            for m in range(SWEEPS):
                mine = pulses[m][side * RD : (side + 1) * RD, column : column + 1]
                message = jnp.where(small == SWEEPS + 1 + m, mine, message)
            rim_send[step, side] = message
        group = 4 + 4 * step
        send(group, rim_send.at[step, 0], rim_recv.at[step, 1], at(strip, (cell + C - 1) % C))
        send(group, rim_send.at[step, 1], rim_recv.at[step, 0], at(strip, (cell + 1) % C))

        if step == 0:
            arrived(3, w_plane.at[0 : Q - 1])
            for i in range(Q):
                w_block[RD * i : RD * (i + 1), :] = w_plane[i]
            padded[0:8, :] = jnp.zeros((8, HC), f32)
            padded[BL + 8 :, :] = jnp.zeros((8, HC), f32)
            for side, column in ((0, 0), (1, BL - 1)):
                answer = coupling * jnp.broadcast_to(
                    colb_ref[plane][:, column : column + 1], (BL, HC)
                )
                for m in range(SWEEPS):
                    if m > 0:
                        back = w_block[...] * answer + coupling * clamp_rows(answer)
                        answer = answer - col_product(colb_parts, back)
                    padded[8 : BL + 8, :] = answer
                    own, other = frames()
                    answer_near[half, m, side] = own
                    answer_send[m, side] = other
                    still_send[m, side, 0:1, :] = answer[:1]
                    still_send[m, side, 1:2, :] = answer[BL - 1 :]
            still_recv[slot] = still_send[...]
            for peer in plane_cross:
                send(5, still_send, still_recv.at[slot], peer)
            send(9, answer_send, answer_near.at[half], partner)

        arrived(group, rim_recv.at[step])
        edges = []
        for side in range(2):
            own = [rim_send[step, side][:, i : i + 1] for i in range(2 * SWEEPS + 1)]
            far = [rim_recv[step, side][:, i : i + 1] for i in range(2 * SWEEPS + 1)]
            mine, theirs = [], []
            for j in range(SWEEPS + 1):
                a, b = own[j], far[j]
                for i in range(j):
                    a = a + own[SWEEPS + j - i] * theirs[i]
                    b = b + far[SWEEPS + j - i] * mine[i]
                mine.append(a)
                theirs.append(b)
            edges.append(theirs)
        left_in = [jnp.where(first_cell, 0.0, e) for e in edges[0]]
        right_in = [jnp.where(last_cell, 0.0, e) for e in edges[1]]
        for i in range(SWEEPS):
            iterate = iterate + (
                pulses[SWEEPS - 1 - i][:RD] * left_in[i] + pulses[SWEEPS - 1 - i][RD:] * right_in[i]
            )
        halo_left = jnp.where(first_cell, iterate[:, :1], left_in[SWEEPS])
        halo_right = jnp.where(last_cell, iterate[:, NC - 1 :], right_in[SWEEPS])
        field_send[step, 0] = jnp.where(end == HC - 1, halo_left, iterate[:, :HC])
        field_send[step, 1] = jnp.where(end == 0, halo_right, iterate[:, cut:])
        field_plane[step, place] = field_send[step, half]
        for peer, other_half in plane_peers:
            send(group + 2, field_send.at[step, other_half], field_plane.at[step, place], peer)
        arrived(group + 2, field_plane.at[step, 0 : Q - 1])
        for i in range(Q):
            field_block[RD * i : RD * (i + 1), :] = field_plane[step, i]

        start = field_block[...]
        beside = pltpu.roll(start, 1, 1) + pltpu.roll(start, HC - 1, 1)
        middle = w_block[...] * start - coupling * (2.0 * start - beside)
        iterate = start
        for j in range(SWEEPS + 1):
            if j > 0:
                left_over = middle - (w_block[...] * iterate + coupling * clamp_rows(iterate))
                iterate = iterate + col_product(colb_parts, left_over)
            tops_send[step, j, 0:1, :] = iterate[:1]
            tops_send[step, j, 1:2, :] = iterate[BL - 1 :]
        for peer in plane_cross:
            send(group + 3, tops_send.at[step], tops_recv.at[step, slot], peer)
        padded[8 : BL + 8, :] = iterate
        own, other = frames()
        near_send[step] = other
        near[step, half] = own
        send(13 + step, near_send.at[step], near.at[step, half], partner)
        tops_recv[step, slot] = tops_send[step]

        if step == 0:
            arrived(5, still_recv.at[0 : 2 * K - 1])
            arrived(9, answer_near.at[0])
            for k in range(K):
                for m in range(SWEEPS):
                    for side in range(2):
                        for h in range(2):
                            still_all[h, m, side, 2 * k : 2 * k + 2, :] = still_recv[
                                2 * k + h, m, side
                            ]
        arrived(group + 3, tops_recv.at[step, 0 : 2 * K - 1])
        for k in range(K):
            for j in range(SWEEPS + 1):
                for h in range(2):
                    tops_all[h, j, 2 * k : 2 * k + 2, :] = tops_recv[step, 2 * k + h, j]
        arrived(13 + step, near.at[step, 0])
        spot = lax.broadcasted_iota(jnp.int32, (2 * K, HC), 0)
        even = spot % 2 == 0
        mine = pl.ds(2 * plane, 1)
        halves = []
        for h in range(2):
            from_above, from_below = [], []
            for j in range(SWEEPS + 1):
                value = tops_all[h, j]
                for i in range(j):
                    value = value + still_all[h, j - i - 1, 0] * from_above[i]
                    value = value + still_all[h, j - i - 1, 1] * from_below[i]
                over = jnp.where(even, pltpu.roll(value, 1, 0), pltpu.roll(value, 2, 0))
                under = jnp.where(
                    even, pltpu.roll(value, 2 * K - 2, 0), pltpu.roll(value, 2 * K - 1, 0)
                )
                from_above.append(jnp.where(spot < 2, 0.0, over))
                from_below.append(jnp.where(spot >= 2 * K - 2, 0.0, under))
                inflow[h, j, 0] = from_above[j]
                inflow[h, j, 1] = from_below[j]
            nearby = near[step, h]
            for i in range(SWEEPS):
                m = SWEEPS - 1 - i
                nearby = nearby + (
                    answer_near[h, m, 0] * inflow[h, i, 0, mine, :]
                    + answer_near[h, m, 1] * inflow[h, i, 1, mine, :]
                )
            above, below = nearby[:1], nearby[1 + RD : 2 + RD]
            above = jnp.where(place == 0, inflow[h, SWEEPS, 0, mine, :], above)
            below = jnp.where(place == Q - 1, inflow[h, SWEEPS, 1, mine, :], below)
            halves.append((above, nearby[1 : 1 + RD], below))

        def joined(first, second):
            over = HC - cut
            lanes = lax.broadcasted_iota(jnp.int32, (first.shape[0], over), 1)
            both = jnp.where(lanes < over // 2, first[:, cut:], second[:, :over])
            return jnp.concatenate([first[:, :cut], both, second[:, over:]], axis=1)

        row_above, current, row_below = (joined(a, b) for a, b in zip(*halves))
        row_above = jnp.where(strip == 0, current[:1], row_above)
        row_below = jnp.where(strip == strips - 1, current[RD - 1 :], row_below)

    density_ref[...] = current
    last_send[0:1, :] = row_above
    last_send[1 : 1 + RD, :] = current
    last_send[1 + RD : 2 + RD, :] = row_below
    last_send[2 + RD : 8, :] = jnp.zeros((6 - RD, NC), f32)
    last_recv[cell] = last_send[...]
    for peer in cell_peers:
        send(12, last_send, last_recv.at[cell], peer)
    arrived(12, last_recv.at[0 : C - 1])
    field = jnp.concatenate([last_recv[c] for c in range(C)], axis=1)
    centre = field[1 : 1 + RD]
    spot = lax.broadcasted_iota(jnp.int32, (RD, C * NC), 1)
    left = jnp.where(spot == 0, centre, pltpu.roll(centre, 1, 1))
    right = jnp.where(spot == C * NC - 1, centre, pltpu.roll(centre, C * NC - 1, 1))
    scale = jnp.maximum(centre, floor_level)
    vel_ref[0] = -(0.5 * (field[2 : 2 + RD] - field[:RD])) / scale
    vel_ref[1] = -(0.5 * (right - left)) / scale
    for group, span in sent:
        pltpu.make_async_copy(span, span, send_sem.at[group]).wait()


def diffuse(part, capacity, blockage, row_blocks, col_blocks):
    strips = lax.axis_size("strip")
    C = lax.axis_size("cells")
    RD, NC = capacity.shape
    NB = row_blocks.shape[0]
    K, BL = col_blocks.shape[:2]
    Q = strips // K
    HC = 128 * ((NB + 1) // 2)
    vmem = pl.BlockSpec(memory_space=pltpu.VMEM)
    shapes = [
        ((2, C, 1, NC), f32),
        ((C, RD, NC), f32),
        ((2, C, 1, NC), f32),
        ((2, 1, NC), f32),
        ((2, 1, NC), f32),
        ((2, RD, HC), f32),
        ((Q, RD, HC), f32),
        ((BL, HC), f32),
        ((NB, 128, 128), bf16),
        ((NB, 128, 128), bf16),
        ((2, BL, BL), bf16),
        ((STEPS, 2, RD, 128), f32),
        ((STEPS, 2, RD, 128), f32),
        ((STEPS, 2, RD, HC), f32),
        ((STEPS, Q, RD, HC), f32),
        ((BL, HC), f32),
        ((BL + 16, HC), f32),
        ((SWEEPS, 2, 8, HC), f32),
        ((2, SWEEPS, 2, 8, HC), f32),
        ((STEPS, 8, HC), f32),
        ((STEPS, 2, 8, HC), f32),
        ((SWEEPS, 2, 2, HC), f32),
        ((2 * K, SWEEPS, 2, 2, HC), f32),
        ((2, SWEEPS, 2, 2 * K, HC), f32),
        ((STEPS, SWEEPS + 1, 2, HC), f32),
        ((STEPS, 2 * K, SWEEPS + 1, 2, HC), f32),
        ((2, SWEEPS + 1, 2 * K, HC), f32),
        ((2, SWEEPS + 1, 2, 2 * K, HC), f32),
        ((8, NC), f32),
        ((C, 8, NC), f32),
    ]
    return pl.pallas_call(
        functools.partial(adi_kernel, (K, Q, C, RD, NC, BL)),
        out_shape=(
            jax.ShapeDtypeStruct((RD, NC), f32),
            jax.ShapeDtypeStruct((2, RD, C * NC), f32),
        ),
        in_specs=[vmem] * 5,
        out_specs=(vmem, vmem),
        scratch_shapes=[pltpu.VMEM(shape, dtype) for shape, dtype in shapes]
        + [pltpu.SemaphoreType.DMA((15,)), pltpu.SemaphoreType.DMA((15,))],
        compiler_params=pltpu.CompilerParams(
            collective_id=0, has_side_effects=True, vmem_limit_bytes=48 << 20
        ),
        name="adi",
    )(part, capacity, blockage, row_blocks, col_blocks)


def pin_tables(block_rows, block_cols, row_near, row_far, col_near, col_far, rows_dev, hi_count):
    block_size = block_rows.shape[0]
    zero_value = jnp.zeros((), jnp.bfloat16)
    row_index = lax.broadcasted_iota(jnp.int32, (block_size, rows_dev), 1)
    row_table = jnp.where(
        row_index == block_rows[:, None], row_near[:, None], zero_value
    ) + jnp.where(row_index == block_rows[:, None] + 1, row_far[:, None], zero_value)
    high_index = lax.broadcasted_iota(jnp.int32, (block_size, 1, hi_count), 2)
    low_index = lax.broadcasted_iota(jnp.int32, (block_size, 128), 1)
    bin_tables = []
    lane_tables = []
    for offset, factor in ((0, col_near), (1, col_far)):
        column = block_cols + offset
        high_part = column // 128
        low_part = column - high_part * 128
        chosen = (high_index == high_part[:, None, None]).astype(jnp.bfloat16)
        bin_tables.append((row_table[:, :, None] * chosen).reshape(block_size, rows_dev * hi_count))
        lane_tables.append(jnp.where(low_index == low_part[:, None], factor[:, None], zero_value))
    return (jnp.concatenate(bin_tables, 0), jnp.concatenate(lane_tables, 0))


def pin_factors(pin_rows, pin_cols, row_near, row_far, col_near, col_far):
    block_size = min(2048, pin_rows.shape[0])
    return (
        block_size,
        tuple(
            (
                item.reshape(-1, block_size)
                for item in (pin_rows, pin_cols, row_near, row_far, col_near, col_far)
            )
        ),
    )


def splat(pin_rows, pin_cols, pin_fracs, pin_weights, rows_dev, hi_count):
    near_y = 1.0 - pin_fracs[0]
    near_x = 1.0 - pin_fracs[1]
    block_size, pieces = pin_factors(
        pin_rows,
        pin_cols,
        (pin_weights * near_y).astype(jnp.bfloat16),
        (pin_weights * pin_fracs[0]).astype(jnp.bfloat16),
        near_x.astype(jnp.bfloat16),
        pin_fracs[1].astype(jnp.bfloat16),
    )

    def add_block(total, block):
        bins, lane_table = pin_tables(
            block[0], block[1], block[2], block[3], block[4], block[5], rows_dev, hi_count
        )
        part_sum = lax.dot_general(
            bins, lane_table, (((0,), (0,)), ((), ())), preferred_element_type=jnp.float32
        )
        return (total + part_sum, None)

    total, unused = lax.scan(add_block, jnp.zeros((rows_dev * hi_count, 128), jnp.float32), pieces)
    return total.reshape(rows_dev, hi_count * 128)


def interpolate(pin_rows, pin_cols, pin_fracs, velocity_y, velocity_x, rows_dev, hi_count):
    stacked = jnp.concatenate(
        [
            velocity_y.reshape(rows_dev * hi_count, 128),
            velocity_x.reshape(rows_dev * hi_count, 128),
        ],
        1,
    )
    npins = pin_rows.shape[0]
    block_size, pieces = pin_factors(
        pin_rows,
        pin_cols,
        (1.0 - pin_fracs[0]).astype(jnp.bfloat16),
        pin_fracs[0].astype(jnp.bfloat16),
        (1.0 - pin_fracs[1]).astype(jnp.bfloat16),
        pin_fracs[1].astype(jnp.bfloat16),
    )

    def one_block(carry, block):
        bins, lane_table = pin_tables(
            block[0], block[1], block[2], block[3], block[4], block[5], rows_dev, hi_count
        )
        sampled = jnp.dot(bins, stacked, preferred_element_type=jnp.float32)
        lane_values = lane_table.astype(jnp.float32)
        both_y = jnp.sum(sampled[:, :128] * lane_values, axis=1)
        both_x = jnp.sum(sampled[:, 128:] * lane_values, axis=1)
        result = jnp.stack(
            [both_y[:block_size] + both_y[block_size:], both_x[:block_size] + both_x[block_size:]]
        )
        return (carry, result)

    unused, outputs = lax.scan(one_block, jnp.zeros((), jnp.float32), pieces)
    return jnp.transpose(outputs, (1, 0, 2)).reshape(2, npins)


def local(pin_rows, pin_cols, pin_fracs, pin_weights, capacity, blockage, row_blocks, col_blocks):
    rows_dev, cols_dev = capacity.shape
    cells = lax.axis_size("cells")
    hi_count = cols_dev * cells // 128
    part = splat(pin_rows, pin_cols, pin_fracs, pin_weights, rows_dev, hi_count)
    part = jnp.transpose(part.reshape(rows_dev, cells, cols_dev), (1, 0, 2))
    current, velocity = diffuse(part, capacity, blockage, row_blocks, col_blocks)
    velocity = velocity.astype(bf16)
    pin_velocity = interpolate(
        pin_rows, pin_cols, pin_fracs, velocity[0], velocity[1], rows_dev, hi_count
    )
    return (current, pin_velocity)


def solution(mesh):
    placed = (
        P(("strip", "cells")),
        P(("strip", "cells")),
        P(None, ("strip", "cells")),
        P(("strip", "cells")),
        P("strip", "cells"),
        P("strip", "cells"),
        P("cells", None, None),
        P(),
    )
    return jax.shard_map(
        local,
        mesh=mesh,
        in_specs=placed,
        out_specs=(P("strip", "cells"), P(None, ("strip", "cells"))),
        check_vma=False,
    )
```

```python
import functools

import jax
import jax.numpy as jnp
from jax import lax
from jax.experimental import pallas as pl
from jax.experimental.pallas import tpu as pltpu
from jax.sharding import PartitionSpec as P

SWEEPS = 3
STEPS = 2
coupling = 2.0
floor_level = 0.5
f32 = jnp.float32
bf16 = jnp.bfloat16


def exact_parts(values):
    high = values.astype(bf16)
    return high, (values - high.astype(f32)).astype(bf16)


def row_product(values, blocks_ref):
    pieces = []
    for n in range(blocks_ref.shape[0]):
        high, low = exact_parts(values[:, 128 * n : 128 * (n + 1)])
        pieces.append(
            lax.dot_general(
                jnp.concatenate([high, low, high], axis=1),
                blocks_ref[n],
                (((1,), (1,)), ((), ())),
                preferred_element_type=f32,
            )
        )
    return jnp.concatenate(pieces, axis=1)


def col_product(matrix_ref, values):
    high, low = exact_parts(values)
    parts = jnp.concatenate([high, low, high], axis=0)
    return jnp.dot(matrix_ref[...], parts, preferred_element_type=f32)


def table(index, first, second, count):
    spot = lax.broadcasted_iota(jnp.int32, (count, index.shape[1]), 0)
    return jnp.where(spot == index, first, jnp.where(spot == index + 1, second, 0.0))


def adi_kernel(
    sizes,
    rows_hbm,
    cols_hbm,
    fracs_hbm,
    pinw_hbm,
    cap_hbm,
    blk_hbm,
    rowb_hbm,
    colb_hbm,
    density_ref,
    pinv_ref,
    rows_ref,
    cols_ref,
    pinw_ref,
    fracs_ref,
    cap_ref,
    blk_ref,
    rowb_ref,
    colb_ref,
    bin_sums,
    part_ref,
    look,
    spread,
    vel_bins,
    edge_part,
    part_recv,
    edge_recv,
    wedge_send,
    wedge_recv,
    w_send,
    w_plane,
    w_block,
    rowb_parts,
    colb_parts,
    rim_send,
    rim_recv,
    field_send,
    field_plane,
    field_block,
    padded,
    answer_send,
    answer_near,
    near_send,
    near,
    still_send,
    still_recv,
    still_all,
    tops_send,
    tops_recv,
    tops_all,
    inflow,
    last_send,
    last_recv,
    send_sem,
    recv_sem,
    load_sem,
):
    K, Q, C, RD, NC, BL = sizes
    strips = K * Q
    HC = w_send.shape[2]
    cut = NC - HC
    strip = lax.axis_index("strip")
    cell = lax.axis_index("cells")
    plane = strip // Q
    place = strip % Q
    depth = Q // 2
    half = (place // 2) % 2
    strip_side = place % 2
    first_cell, last_cell = cell == 0, cell == C - 1
    first_plane, last_plane = plane == 0, plane == K - 1

    def at(strip_id, cell_id):
        return (strip_id, cell_id)

    cell_peers = [at(strip, (cell + d) % C) for d in range(1, C)]
    above_strip, below_strip = (strip + strips - 1) % strips, (strip + 1) % strips
    offsets = [(dz, dy) for dz in range(depth) for dy in range(2) if (dz, dy) != (0, 0)]
    offsets.sort(key=lambda o: -(min(o[0], depth - o[0]) + 2 * o[1]))
    plane_peers = []
    for dz, dy in offsets:
        other = ((place // 2 + dz) % depth) * 2 + (place % 2 + dy) % 2
        plane_peers.append((at(plane * Q + other, cell), (half + dz) % 2))
    partner = at(strip + 2 - 4 * half, cell)
    shifts = [(dk, dz) for dk in range(K) for dz in range(2) if (dk, dz) != (0, 0)]
    shifts.sort(key=lambda o: -(min(o[0], K - o[0]) + o[1]))
    plane_cross = [
        at(((plane + dk) % K) * Q + place + dz * (2 - 4 * half), cell) for dk, dz in shifts
    ]
    slot = 2 * plane + half
    row_peers = [at(s, (cell + d) % C) for s in (above_strip, below_strip) for d in range(C)]

    barrier = pltpu.get_barrier_semaphore()
    greeted = cell_peers + [p for p, _ in plane_peers] + plane_cross + row_peers
    for peer in greeted:
        pl.semaphore_signal(barrier, 1, device_id=peer, device_id_type=pl.DeviceIdType.MESH)

    sent = []

    def send(group, source, target, peer):
        pltpu.make_async_remote_copy(
            src_ref=source,
            dst_ref=target,
            send_sem=send_sem.at[group],
            recv_sem=recv_sem.at[group],
            device_id=peer,
            device_id_type=pl.DeviceIdType.MESH,
        ).start()

    def arrived(group, span):
        sent.append((group, span))
        pltpu.make_async_copy(span, span, recv_sem.at[group]).wait()

    loads = [
        pltpu.make_async_copy(source, target, load_sem.at[i])
        for i, (source, target) in enumerate(
            (
                (rows_hbm, rows_ref),
                (cols_hbm, cols_ref),
                (pinw_hbm, pinw_ref),
                (fracs_hbm, fracs_ref),
                (cap_hbm, cap_ref),
                (blk_hbm, blk_ref),
                (rowb_hbm, rowb_ref),
                (colb_hbm.at[plane], colb_ref),
            )
        )
    ]
    for load in loads:
        load.start()
    for load in loads:
        load.wait()

    chunks = rows_ref.shape[0]
    bins = bin_sums.shape[0]

    def pins_of(i):
        span = pl.ds(pl.multiple_of(128 * i, 128), 128)
        down, across = fracs_ref[0:1, span], fracs_ref[1:2, span]
        column = cols_ref[pl.ds(i, 1), :]
        tile = lax.shift_right_logical(column, 7)
        return down, across, tile * RD + rows_ref[pl.ds(i, 1), :], column - tile * 128

    def rounded(values):
        return values.astype(bf16).astype(f32)

    def add_pins(i, total):
        down, across, index, lane = pins_of(i)
        heavy = pinw_ref[pl.ds(i, 1), :]
        where_down = table(index, rounded(heavy * (1.0 - down)), rounded(heavy * down), bins)
        where_across = table(lane, rounded(1.0 - across), rounded(across), 136)
        return total + lax.dot_general(
            where_down.astype(bf16),
            where_across.astype(bf16),
            (((1,), (1,)), ((), ())),
            preferred_element_type=f32,
        )

    total = lax.fori_loop(0, chunks, add_pins, jnp.zeros((bins, 136), f32), unroll=4)
    spot = lax.broadcasted_iota(jnp.int32, (bins, 128), 1)
    past = jnp.where(spot == 0, total[:, 128:129], 0.0)
    bin_sums[...] = total[:, :128] + pltpu.roll(past, RD, 0)
    for c in range(C):
        for n in range(NC // 128):
            tile = c * (NC // 128) + n
            part_ref[c, :, 128 * n : 128 * (n + 1)] = bin_sums[RD * tile : RD * (tile + 1), :]

    weights = cap_ref[...].astype(f32) * (1.0 - blk_ref[...])
    w_send[0] = weights[:, :HC]
    w_send[1] = weights[:, cut:]
    w_plane[place] = w_send[half]
    wedge_send[0] = weights[:1]
    wedge_send[1] = weights[RD - 1 :]
    for c in range(C):
        edge_part[0, c] = part_ref[c, :1]
        edge_part[1, c] = part_ref[c, RD - 1 :]
    pl.semaphore_wait(barrier, len(greeted))

    for d in range(C):
        other = (cell + d) % C
        send(1, edge_part.at[0, other], edge_recv.at[1, cell], at(above_strip, other))
        send(1, edge_part.at[1, other], edge_recv.at[0, cell], at(below_strip, other))
    send(2, wedge_send.at[0], wedge_recv.at[1], at(above_strip, cell))
    send(2, wedge_send.at[1], wedge_recv.at[0], at(below_strip, cell))
    for d in range(1, C):
        other = (cell + d) % C
        send(0, part_ref.at[other], part_recv.at[C - 1 - d], at(strip, other))
    for peer, other_half in plane_peers:
        send(3, w_send.at[other_half], w_plane.at[place], peer)

    for n in range(rowb_ref.shape[0]):
        high, low = exact_parts(rowb_ref[n])
        rowb_parts[n] = jnp.concatenate([high, high, low], axis=1)
    high, low = exact_parts(colb_ref[...])
    colb_parts[...] = jnp.concatenate([high, high, low], axis=1)

    end = lax.broadcasted_iota(jnp.int32, (RD, HC), 1)

    def along_inside(values):
        left = pltpu.roll(values, 1, 1)
        right = pltpu.roll(values, NC - 1, 1)
        spot = lax.broadcasted_iota(jnp.int32, values.shape, 1)
        left = jnp.where(spot == 0, jnp.where(first_cell, values, 0.0), left)
        right = jnp.where(spot == NC - 1, jnp.where(last_cell, values, 0.0), right)
        return 2.0 * values - left - right

    weights_two = jnp.concatenate([weights, weights], axis=0)
    spot = lax.broadcasted_iota(jnp.int32, (2 * RD, NC), 1)
    row = lax.broadcasted_iota(jnp.int32, (2 * RD, NC), 0)
    unit = jnp.where(spot == jnp.where(row < RD, 0, NC - 1), coupling, 0.0)
    pulse = row_product(unit, rowb_parts)
    pulses = [pulse]
    for _ in range(SWEEPS - 1):
        back = weights_two * pulse + coupling * along_inside(pulse)
        pulse = pulse - row_product(back, rowb_parts)
        pulses.append(pulse)

    arrived(1, edge_recv)
    arrived(2, wedge_recv)
    arrived(0, part_recv.at[0 : C - 1])
    density = part_ref[cell]
    for d in range(C - 1):
        density = density + part_recv[d]
    current = density / weights
    row_above = edge_recv[0, 0]
    row_below = edge_recv[1, 0]
    for c in range(1, C):
        row_above = row_above + edge_recv[0, c]
        row_below = row_below + edge_recv[1, c]
    row_above = row_above / wedge_recv[0]
    row_below = row_below / wedge_recv[1]
    row_above = jnp.where(strip == 0, current[:1], row_above)
    row_below = jnp.where(strip == strips - 1, current[RD - 1 :], row_below)

    def frame(pair):
        base = pl.multiple_of(RD * 2 * pair, 2 * RD)
        inner = padded[pl.ds(base + 8, 2 * RD), :]
        over = padded[pl.ds(base + 7, 1), :]
        under = padded[pl.ds(base + 8 + 2 * RD, 1), :]
        fill = jnp.zeros((6 - RD, HC), f32)
        upper = jnp.concatenate([over, inner[: RD + 1], fill], axis=0)
        lower = jnp.concatenate([inner[RD - 1 :], under, fill], axis=0)
        return jnp.where(strip_side == 0, upper, lower)

    def frames():
        return frame(place // 2), frame(place // 2 + 1 - 2 * half)

    small = lax.broadcasted_iota(jnp.int32, (RD, 128), 1)

    def clamp_rows(values):
        shape = values.shape
        spot = lax.broadcasted_iota(jnp.int32, shape, 0)
        up = pltpu.roll(values, 1, 0)
        down = pltpu.roll(values, shape[0] - 1, 0)
        up = jnp.where(spot == 0, jnp.where(first_plane, values, 0.0), up)
        down = jnp.where(spot == shape[0] - 1, jnp.where(last_plane, values, 0.0), down)
        return 2.0 * values - up - down

    for step in range(STEPS):
        up = jnp.concatenate([row_above, current[: RD - 1]], axis=0)
        down = jnp.concatenate([current[1:], row_below], axis=0)
        source = weights * current - coupling * (2.0 * current - up - down)
        iterate = current
        levels = [iterate]
        for _ in range(SWEEPS):
            left_over = source - (weights * iterate + coupling * along_inside(iterate))
            iterate = iterate + row_product(left_over, rowb_parts)
            levels.append(iterate)
        for side, column in ((0, 0), (1, NC - 1)):
            message = jnp.zeros((RD, 128), f32)
            for j in range(SWEEPS + 1):
                message = jnp.where(small == j, levels[j][:, column : column + 1], message)
            for m in range(SWEEPS):
                mine = pulses[m][side * RD : (side + 1) * RD, column : column + 1]
                message = jnp.where(small == SWEEPS + 1 + m, mine, message)
            rim_send[step, side] = message
        group = 4 + 4 * step
        send(group, rim_send.at[step, 0], rim_recv.at[step, 1], at(strip, (cell + C - 1) % C))
        send(group, rim_send.at[step, 1], rim_recv.at[step, 0], at(strip, (cell + 1) % C))

        arrived(group, rim_recv.at[step])
        edges = []
        for side in range(2):
            own = [rim_send[step, side][:, i : i + 1] for i in range(2 * SWEEPS + 1)]
            far = [rim_recv[step, side][:, i : i + 1] for i in range(2 * SWEEPS + 1)]
            mine, theirs = [], []
            for j in range(SWEEPS + 1):
                a, b = own[j], far[j]
                for i in range(j):
                    a = a + own[SWEEPS + j - i] * theirs[i]
                    b = b + far[SWEEPS + j - i] * mine[i]
                mine.append(a)
                theirs.append(b)
            edges.append(theirs)
        left_in = [jnp.where(first_cell, 0.0, e) for e in edges[0]]
        right_in = [jnp.where(last_cell, 0.0, e) for e in edges[1]]
        for i in range(SWEEPS):
            iterate = iterate + (
                pulses[SWEEPS - 1 - i][:RD] * left_in[i] + pulses[SWEEPS - 1 - i][RD:] * right_in[i]
            )
        halo_left = jnp.where(first_cell, iterate[:, :1], left_in[SWEEPS])
        halo_right = jnp.where(last_cell, iterate[:, NC - 1 :], right_in[SWEEPS])
        field_send[step, 0] = jnp.where(end == HC - 1, halo_left, iterate[:, :HC])
        field_send[step, 1] = jnp.where(end == 0, halo_right, iterate[:, cut:])
        field_plane[step, place] = field_send[step, half]
        for peer, other_half in plane_peers:
            send(group + 2, field_send.at[step, other_half], field_plane.at[step, place], peer)
        if step == 0:
            arrived(3, w_plane.at[0 : Q - 1])
            for i in range(Q):
                w_block[RD * i : RD * (i + 1), :] = w_plane[i]
            padded[0:8, :] = jnp.zeros((8, HC), f32)
            padded[BL + 8 :, :] = jnp.zeros((8, HC), f32)
            for side, column in ((0, 0), (1, BL - 1)):
                answer = coupling * jnp.broadcast_to(
                    colb_ref[:, column : column + 1], (BL, HC)
                )
                for m in range(SWEEPS):
                    if m > 0:
                        back = w_block[...] * answer + coupling * clamp_rows(answer)
                        answer = answer - col_product(colb_parts, back)
                    padded[8 : BL + 8, :] = answer
                    own, other = frames()
                    answer_near[half, m, side] = own
                    answer_send[m, side] = other
                    still_send[m, side, 0:1, :] = answer[:1]
                    still_send[m, side, 1:2, :] = answer[BL - 1 :]
            still_recv[slot] = still_send[...]
            for peer in plane_cross:
                send(5, still_send, still_recv.at[slot], peer)
            send(9, answer_send, answer_near.at[half], partner)
        else:

            def prepare(i, carry):
                down, across, index, lane = pins_of(i)
                look[i] = table(index, rounded(1.0 - down), rounded(down), 128).astype(bf16)
                spread[i] = table(lane, rounded(1.0 - across), rounded(across), 136)
                return carry

            lax.fori_loop(0, chunks, prepare, 0, unroll=2)

        arrived(group + 2, field_plane.at[step, 0 : Q - 1])
        for i in range(Q):
            field_block[RD * i : RD * (i + 1), :] = field_plane[step, i]

        start = field_block[...]
        beside = pltpu.roll(start, 1, 1) + pltpu.roll(start, HC - 1, 1)
        middle = w_block[...] * start - coupling * (2.0 * start - beside)
        iterate = start
        for j in range(SWEEPS + 1):
            if j > 0:
                left_over = middle - (w_block[...] * iterate + coupling * clamp_rows(iterate))
                iterate = iterate + col_product(colb_parts, left_over)
            tops_send[step, j, 0:1, :] = iterate[:1]
            tops_send[step, j, 1:2, :] = iterate[BL - 1 :]
        for peer in plane_cross:
            send(group + 3, tops_send.at[step], tops_recv.at[step, slot], peer)
        padded[8 : BL + 8, :] = iterate
        own, other = frames()
        near_send[step] = other
        near[step, half] = own
        send(13 + step, near_send.at[step], near.at[step, half], partner)
        tops_recv[step, slot] = tops_send[step]

        if step == 0:
            arrived(5, still_recv.at[0 : 2 * K - 1])
            arrived(9, answer_near.at[0])
            for k in range(K):
                for m in range(SWEEPS):
                    for side in range(2):
                        for h in range(2):
                            still_all[h, m, side, 2 * k : 2 * k + 2, :] = still_recv[
                                2 * k + h, m, side
                            ]
        arrived(group + 3, tops_recv.at[step, 0 : 2 * K - 1])
        for k in range(K):
            for j in range(SWEEPS + 1):
                for h in range(2):
                    tops_all[h, j, 2 * k : 2 * k + 2, :] = tops_recv[step, 2 * k + h, j]
        arrived(13 + step, near.at[step, 0])
        spot = lax.broadcasted_iota(jnp.int32, (2 * K, HC), 0)
        even = spot % 2 == 0
        mine = pl.ds(2 * plane, 1)
        halves = []
        for h in range(2):
            from_above, from_below = [], []
            for j in range(SWEEPS + 1):
                value = tops_all[h, j]
                for i in range(j):
                    value = value + still_all[h, j - i - 1, 0] * from_above[i]
                    value = value + still_all[h, j - i - 1, 1] * from_below[i]
                over = jnp.where(even, pltpu.roll(value, 1, 0), pltpu.roll(value, 2, 0))
                under = jnp.where(
                    even, pltpu.roll(value, 2 * K - 2, 0), pltpu.roll(value, 2 * K - 1, 0)
                )
                from_above.append(jnp.where(spot < 2, 0.0, over))
                from_below.append(jnp.where(spot >= 2 * K - 2, 0.0, under))
                inflow[h, j, 0] = from_above[j]
                inflow[h, j, 1] = from_below[j]
            nearby = near[step, h]
            for i in range(SWEEPS):
                m = SWEEPS - 1 - i
                nearby = nearby + (
                    answer_near[h, m, 0] * inflow[h, i, 0, mine, :]
                    + answer_near[h, m, 1] * inflow[h, i, 1, mine, :]
                )
            above, below = nearby[:1], nearby[1 + RD : 2 + RD]
            above = jnp.where(place == 0, inflow[h, SWEEPS, 0, mine, :], above)
            below = jnp.where(place == Q - 1, inflow[h, SWEEPS, 1, mine, :], below)
            halves.append((above, nearby[1 : 1 + RD], below))

        def joined(first, second):
            over = HC - cut
            lanes = lax.broadcasted_iota(jnp.int32, (first.shape[0], over), 1)
            both = jnp.where(lanes < over // 2, first[:, cut:], second[:, :over])
            return jnp.concatenate([first[:, :cut], both, second[:, over:]], axis=1)

        row_above, current, row_below = (joined(a, b) for a, b in zip(*halves))
        row_above = jnp.where(strip == 0, current[:1], row_above)
        row_below = jnp.where(strip == strips - 1, current[RD - 1 :], row_below)

    density_ref[...] = current
    last_send[0:1, :] = row_above
    last_send[1 : 1 + RD, :] = current
    last_send[1 + RD : 2 + RD, :] = row_below
    last_send[2 + RD : 8, :] = jnp.zeros((6 - RD, NC), f32)
    last_recv[cell] = last_send[...]
    for peer in cell_peers:
        send(12, last_send, last_recv.at[cell], peer)
    arrived(12, last_recv.at[0 : C - 1])
    field = jnp.concatenate([last_recv[c] for c in range(C)], axis=1)
    centre = field[1 : 1 + RD]
    spot = lax.broadcasted_iota(jnp.int32, (RD, C * NC), 1)
    left = jnp.where(spot == 0, centre, pltpu.roll(centre, 1, 1))
    right = jnp.where(spot == C * NC - 1, centre, pltpu.roll(centre, C * NC - 1, 1))
    scale = jnp.maximum(centre, floor_level)
    velocity_y = -(0.5 * (field[2 : 2 + RD] - field[:RD])) / scale
    velocity_x = -(0.5 * (right - left)) / scale
    tables = []
    for i, velocity in enumerate((velocity_y, velocity_x)):
        vel_bins[i, bins:, :] = jnp.zeros((128 - bins, 128), f32)
        for n in range(bins // RD):
            vel_bins[i, RD * n : RD * (n + 1), :] = velocity[:, 128 * n : 128 * (n + 1)]
        turned = jnp.transpose(vel_bins[i])
        past = jnp.broadcast_to(pltpu.roll(turned[:8], 128 - RD, 1)[:1], (8, 128))
        tables += [turned.astype(bf16), past.astype(bf16)]
    tables = jnp.concatenate(tables, axis=0)

    def sample(i, carry):
        sampled = jnp.dot(tables, look[i], preferred_element_type=f32)
        across = spread[i]
        out_y = jnp.sum(sampled[:136] * across, axis=0, keepdims=True)
        out_x = jnp.sum(sampled[136:] * across, axis=0, keepdims=True)
        span = pl.ds(pl.multiple_of(128 * i, 128), 128)
        pinv_ref[:, span] = jnp.concatenate([out_y, out_x], axis=0)
        return carry

    lax.fori_loop(0, chunks, sample, 0, unroll=4)
    for group, span in sent:
        pltpu.make_async_copy(span, span, send_sem.at[group]).wait()


def diffuse(pin_rows, pin_cols, pin_fracs, pin_weights, capacity, blockage, row_blocks, col_blocks):
    pins = pin_rows.shape[0]
    chunks = pins // 128
    strips = lax.axis_size("strip")
    C = lax.axis_size("cells")
    RD, NC = capacity.shape
    NB = row_blocks.shape[0]
    K, BL = col_blocks.shape[:2]
    Q = strips // K
    HC = 128 * ((NB + 1) // 2)
    vmem = pl.BlockSpec(memory_space=pltpu.VMEM)
    bins = RD * C * NC // 128
    shapes = [
        ((chunks, 128), jnp.int32),
        ((chunks, 128), jnp.int32),
        ((chunks, 128), f32),
        ((2, pins), f32),
        ((RD, NC), jnp.int32),
        ((RD, NC), f32),
        ((NB, 128, 128), f32),
        ((BL, BL), f32),
        ((bins, 128), f32),
        ((C, RD, NC), f32),
        ((chunks, 128, 128), bf16),
        ((chunks, 136, 128), f32),
        ((2, 128, 128), f32),
        ((2, C, 1, NC), f32),
        ((C, RD, NC), f32),
        ((2, C, 1, NC), f32),
        ((2, 1, NC), f32),
        ((2, 1, NC), f32),
        ((2, RD, HC), f32),
        ((Q, RD, HC), f32),
        ((BL, HC), f32),
        ((NB, 128, 384), bf16),
        ((BL, 3 * BL), bf16),
        ((STEPS, 2, RD, 128), f32),
        ((STEPS, 2, RD, 128), f32),
        ((STEPS, 2, RD, HC), f32),
        ((STEPS, Q, RD, HC), f32),
        ((BL, HC), f32),
        ((BL + 16, HC), f32),
        ((SWEEPS, 2, 8, HC), f32),
        ((2, SWEEPS, 2, 8, HC), f32),
        ((STEPS, 8, HC), f32),
        ((STEPS, 2, 8, HC), f32),
        ((SWEEPS, 2, 2, HC), f32),
        ((2 * K, SWEEPS, 2, 2, HC), f32),
        ((2, SWEEPS, 2, 2 * K, HC), f32),
        ((STEPS, SWEEPS + 1, 2, HC), f32),
        ((STEPS, 2 * K, SWEEPS + 1, 2, HC), f32),
        ((2, SWEEPS + 1, 2 * K, HC), f32),
        ((2, SWEEPS + 1, 2, 2 * K, HC), f32),
        ((8, NC), f32),
        ((C, 8, NC), f32),
    ]
    return pl.pallas_call(
        functools.partial(adi_kernel, (K, Q, C, RD, NC, BL)),
        out_shape=(
            jax.ShapeDtypeStruct((RD, NC), f32),
            jax.ShapeDtypeStruct((2, pins), f32),
        ),
        in_specs=[pl.BlockSpec(memory_space=pl.ANY)] * 8,
        out_specs=(vmem, vmem),
        scratch_shapes=[pltpu.VMEM(shape, dtype) for shape, dtype in shapes]
        + [pltpu.SemaphoreType.DMA((n,)) for n in (15, 15, 8)],
        compiler_params=pltpu.CompilerParams(
            collective_id=0, has_side_effects=True, vmem_limit_bytes=48 << 20
        ),
        name="adi",
    )(
        pin_rows.reshape(chunks, 128),
        pin_cols.reshape(chunks, 128),
        pin_fracs,
        pin_weights.reshape(chunks, 128),
        capacity,
        blockage,
        row_blocks,
        col_blocks,
    )


def solution(mesh):
    placed = (
        P(("strip", "cells")),
        P(("strip", "cells")),
        P(None, ("strip", "cells")),
        P(("strip", "cells")),
        P("strip", "cells"),
        P("strip", "cells"),
        P("cells", None, None),
        P(),
    )
    return jax.shard_map(
        diffuse,
        mesh=mesh,
        in_specs=placed,
        out_specs=(P("strip", "cells"), P(None, ("strip", "cells"))),
        check_vma=False,
    )
```

```python
import functools

import jax
import jax.numpy as jnp
from jax import lax
from jax.experimental import pallas as pl
from jax.experimental.pallas import tpu as pltpu
from jax.sharding import PartitionSpec as P

SWEEPS = 3
STEPS = 2
coupling = 2.0
floor_level = 0.5
w_steps = 8191.0
f32 = jnp.float32
bf16 = jnp.bfloat16


def exact_parts(values):
    high = values.astype(bf16)
    return high, (values - high.astype(f32)).astype(bf16)


def row_product(values, blocks_ref):
    pieces = []
    for n in range(blocks_ref.shape[0]):
        high, low = exact_parts(values[:, 128 * n : 128 * (n + 1)])
        pieces.append(
            lax.dot_general(
                jnp.concatenate([high, low, high], axis=1),
                blocks_ref[n],
                (((1,), (1,)), ((), ())),
                preferred_element_type=f32,
            )
        )
    return jnp.concatenate(pieces, axis=1)


def col_product(matrix_ref, values):
    high, low = exact_parts(values)
    parts = jnp.concatenate([high, low, high], axis=0)
    return jnp.dot(matrix_ref[...], parts, preferred_element_type=f32)


def table(index, first, second, count):
    spot = lax.broadcasted_iota(jnp.int32, (count, index.shape[1]), 0)
    return jnp.where(spot == index, first, jnp.where(spot == index + 1, second, 0.0))


def adi_kernel(
    sizes,
    rows_hbm,
    cols_hbm,
    fracs_hbm,
    pinw_hbm,
    cap_hbm,
    blk_hbm,
    rowb_hbm,
    colb_hbm,
    density_ref,
    pinv_ref,
    rows_ref,
    cols_ref,
    pinw_ref,
    fracs_ref,
    cap_ref,
    blk_ref,
    rowb_ref,
    colb_ref,
    bin_sums,
    part_ref,
    look,
    spread,
    vel_bins,
    edge_part,
    part_recv,
    edge_recv,
    wedge_send,
    wedge_recv,
    w_send,
    w_plane,
    w_block,
    rowb_parts,
    colb_parts,
    rim_send,
    rim_recv,
    field_send,
    field_plane,
    field_block,
    padded,
    answer_send,
    answer_near,
    near_send,
    near,
    still_send,
    still_recv,
    still_all,
    tops_send,
    tops_recv,
    tops_all,
    inflow,
    last_send,
    last_recv,
    send_sem,
    recv_sem,
    load_sem,
):
    K, Q, C, RD, NC, BL = sizes
    strips = K * Q
    HC = w_send.shape[2]
    cut = NC - HC
    strip = lax.axis_index("strip")
    cell = lax.axis_index("cells")
    plane = strip // Q
    place = strip % Q
    depth = Q // 2
    half = (place // 2) % 2
    strip_side = place % 2
    first_cell, last_cell = cell == 0, cell == C - 1
    first_plane, last_plane = plane == 0, plane == K - 1

    def at(strip_id, cell_id):
        return (strip_id, cell_id)

    cell_peers = [at(strip, (cell + d) % C) for d in range(1, C)]
    above_strip, below_strip = (strip + strips - 1) % strips, (strip + 1) % strips
    offsets = [(dz, dy) for dz in range(depth) for dy in range(2) if (dz, dy) != (0, 0)]
    offsets.sort(key=lambda o: -(min(o[0], depth - o[0]) + 2 * o[1]))
    plane_peers = []
    for dz, dy in offsets:
        other = ((place // 2 + dz) % depth) * 2 + (place % 2 + dy) % 2
        plane_peers.append((at(plane * Q + other, cell), (half + dz) % 2))
    partner = at(strip + 2 - 4 * half, cell)
    shifts = [(dk, dz) for dk in range(K) for dz in range(2) if (dk, dz) != (0, 0)]
    shifts.sort(key=lambda o: -(min(o[0], K - o[0]) + o[1]))
    plane_cross = [
        at(((plane + dk) % K) * Q + place + dz * (2 - 4 * half), cell) for dk, dz in shifts
    ]
    slot = 2 * plane + half
    row_peers = [at(s, (cell + d) % C) for s in (above_strip, below_strip) for d in range(C)]

    barrier = pltpu.get_barrier_semaphore()
    greeted = cell_peers + [p for p, _ in plane_peers] + plane_cross + row_peers
    for peer in greeted:
        pl.semaphore_signal(barrier, 1, device_id=peer, device_id_type=pl.DeviceIdType.MESH)

    sent = []

    def send(group, source, target, peer):
        pltpu.make_async_remote_copy(
            src_ref=source,
            dst_ref=target,
            send_sem=send_sem.at[group],
            recv_sem=recv_sem.at[group],
            device_id=peer,
            device_id_type=pl.DeviceIdType.MESH,
        ).start()

    def arrived(group, span):
        sent.append((group, span))
        pltpu.make_async_copy(span, span, recv_sem.at[group]).wait()

    loads = [
        pltpu.make_async_copy(source, target, load_sem.at[i])
        for i, (source, target) in enumerate(
            (
                (rows_hbm, rows_ref),
                (cols_hbm, cols_ref),
                (pinw_hbm, pinw_ref),
                (fracs_hbm, fracs_ref),
                (cap_hbm, cap_ref),
                (blk_hbm, blk_ref),
                (rowb_hbm, rowb_ref),
                (colb_hbm.at[plane], colb_ref),
            )
        )
    ]
    for load in loads:
        load.start()
    for load in loads:
        load.wait()

    chunks = rows_ref.shape[0]
    bins = bin_sums.shape[0]

    def pins_of(i):
        span = pl.ds(pl.multiple_of(128 * i, 128), 128)
        down, across = fracs_ref[0:1, span], fracs_ref[1:2, span]
        column = cols_ref[pl.ds(i, 1), :]
        tile = lax.shift_right_logical(column, 7)
        return down, across, tile * RD + rows_ref[pl.ds(i, 1), :], column - tile * 128

    def rounded(values):
        return values.astype(bf16).astype(f32)

    def add_pins(i, total):
        down, across, index, lane = pins_of(i)
        heavy = pinw_ref[pl.ds(i, 1), :]
        where_down = table(index, rounded(heavy * (1.0 - down)), rounded(heavy * down), bins)
        where_across = table(lane, rounded(1.0 - across), rounded(across), 136)
        return total + lax.dot_general(
            where_down.astype(bf16),
            where_across.astype(bf16),
            (((1,), (1,)), ((), ())),
            preferred_element_type=f32,
        )

    total = lax.fori_loop(0, chunks, add_pins, jnp.zeros((bins, 136), f32), unroll=4)
    spot = lax.broadcasted_iota(jnp.int32, (bins, 128), 1)
    past = jnp.where(spot == 0, total[:, 128:129], 0.0)
    bin_sums[...] = total[:, :128] + pltpu.roll(past, RD, 0)
    for c in range(C):
        for n in range(NC // 128):
            tile = c * (NC // 128) + n
            part_ref[c, :, 128 * n : 128 * (n + 1)] = bin_sums[RD * tile : RD * (tile + 1), :]

    weights = cap_ref[...].astype(f32) * (1.0 - blk_ref[...])
    whole = jnp.round(weights * w_steps).astype(jnp.int32).astype(jnp.int16)
    w_send[0] = whole[:, :HC]
    w_send[1] = whole[:, cut:]
    w_plane[place] = w_send[half]
    wedge_send[0] = weights[:1]
    wedge_send[1] = weights[RD - 1 :]
    for c in range(C):
        edge_part[0, c] = part_ref[c, :1]
        edge_part[1, c] = part_ref[c, RD - 1 :]
    pl.semaphore_wait(barrier, len(greeted))

    for d in range(C):
        other = (cell + d) % C
        send(1, edge_part.at[0, other], edge_recv.at[1, cell], at(above_strip, other))
        send(1, edge_part.at[1, other], edge_recv.at[0, cell], at(below_strip, other))
    send(2, wedge_send.at[0], wedge_recv.at[1], at(above_strip, cell))
    send(2, wedge_send.at[1], wedge_recv.at[0], at(below_strip, cell))
    for d in range(1, C):
        other = (cell + d) % C
        send(0, part_ref.at[other], part_recv.at[C - 1 - d], at(strip, other))
    for peer, other_half in plane_peers:
        send(3, w_send.at[other_half], w_plane.at[place], peer)

    for n in range(rowb_ref.shape[0]):
        high, low = exact_parts(rowb_ref[n])
        rowb_parts[n] = jnp.concatenate([high, high, low], axis=1)
    high, low = exact_parts(colb_ref[...])
    colb_parts[...] = jnp.concatenate([high, high, low], axis=1)

    end = lax.broadcasted_iota(jnp.int32, (RD, HC), 1)

    def along_inside(values):
        left = pltpu.roll(values, 1, 1)
        right = pltpu.roll(values, NC - 1, 1)
        spot = lax.broadcasted_iota(jnp.int32, values.shape, 1)
        left = jnp.where(spot == 0, jnp.where(first_cell, values, 0.0), left)
        right = jnp.where(spot == NC - 1, jnp.where(last_cell, values, 0.0), right)
        return 2.0 * values - left - right

    weights_two = jnp.concatenate([weights, weights], axis=0)
    spot = lax.broadcasted_iota(jnp.int32, (2 * RD, NC), 1)
    row = lax.broadcasted_iota(jnp.int32, (2 * RD, NC), 0)
    unit = jnp.where(spot == jnp.where(row < RD, 0, NC - 1), coupling, 0.0)
    pulse = row_product(unit, rowb_parts)
    pulses = [pulse]
    for _ in range(SWEEPS - 1):
        back = weights_two * pulse + coupling * along_inside(pulse)
        pulse = pulse - row_product(back, rowb_parts)
        pulses.append(pulse)

    arrived(1, edge_recv)
    arrived(2, wedge_recv)
    arrived(0, part_recv.at[0 : C - 1])
    density = part_ref[cell]
    for d in range(C - 1):
        density = density + part_recv[d]
    current = density / weights
    row_above = edge_recv[0, 0]
    row_below = edge_recv[1, 0]
    for c in range(1, C):
        row_above = row_above + edge_recv[0, c]
        row_below = row_below + edge_recv[1, c]
    row_above = row_above / wedge_recv[0]
    row_below = row_below / wedge_recv[1]
    row_above = jnp.where(strip == 0, current[:1], row_above)
    row_below = jnp.where(strip == strips - 1, current[RD - 1 :], row_below)

    def frame(pair):
        base = pl.multiple_of(RD * 2 * pair, 2 * RD)
        inner = padded[pl.ds(base + 8, 2 * RD), :]
        over = padded[pl.ds(base + 7, 1), :]
        under = padded[pl.ds(base + 8 + 2 * RD, 1), :]
        fill = jnp.zeros((6 - RD, HC), f32)
        upper = jnp.concatenate([over, inner[: RD + 1], fill], axis=0)
        lower = jnp.concatenate([inner[RD - 1 :], under, fill], axis=0)
        return jnp.where(strip_side == 0, upper, lower)

    def frames():
        return frame(place // 2), frame(place // 2 + 1 - 2 * half)

    small = lax.broadcasted_iota(jnp.int32, (RD, 128), 1)

    def clamp_rows(values):
        shape = values.shape
        spot = lax.broadcasted_iota(jnp.int32, shape, 0)
        up = pltpu.roll(values, 1, 0)
        down = pltpu.roll(values, shape[0] - 1, 0)
        up = jnp.where(spot == 0, jnp.where(first_plane, values, 0.0), up)
        down = jnp.where(spot == shape[0] - 1, jnp.where(last_plane, values, 0.0), down)
        return 2.0 * values - up - down

    for step in range(STEPS):
        up = jnp.concatenate([row_above, current[: RD - 1]], axis=0)
        down = jnp.concatenate([current[1:], row_below], axis=0)
        source = weights * current - coupling * (2.0 * current - up - down)
        iterate = current
        levels = [iterate]
        for _ in range(SWEEPS):
            left_over = source - (weights * iterate + coupling * along_inside(iterate))
            iterate = iterate + row_product(left_over, rowb_parts)
            levels.append(iterate)
        for side, column in ((0, 0), (1, NC - 1)):
            message = jnp.zeros((RD, 128), f32)
            for j in range(SWEEPS + 1):
                message = jnp.where(small == j, levels[j][:, column : column + 1], message)
            for m in range(SWEEPS):
                mine = pulses[m][side * RD : (side + 1) * RD, column : column + 1]
                message = jnp.where(small == SWEEPS + 1 + m, mine, message)
            rim_send[step, side] = message
        group = 4 + 4 * step
        send(group, rim_send.at[step, 0], rim_recv.at[step, 1], at(strip, (cell + C - 1) % C))
        send(group, rim_send.at[step, 1], rim_recv.at[step, 0], at(strip, (cell + 1) % C))

        arrived(group, rim_recv.at[step])
        edges = []
        for side in range(2):
            own = [rim_send[step, side][:, i : i + 1] for i in range(2 * SWEEPS + 1)]
            far = [rim_recv[step, side][:, i : i + 1] for i in range(2 * SWEEPS + 1)]
            mine, theirs = [], []
            for j in range(SWEEPS + 1):
                a, b = own[j], far[j]
                for i in range(j):
                    a = a + own[SWEEPS + j - i] * theirs[i]
                    b = b + far[SWEEPS + j - i] * mine[i]
                mine.append(a)
                theirs.append(b)
            edges.append(theirs)
        left_in = [jnp.where(first_cell, 0.0, e) for e in edges[0]]
        right_in = [jnp.where(last_cell, 0.0, e) for e in edges[1]]
        for i in range(SWEEPS):
            iterate = iterate + (
                pulses[SWEEPS - 1 - i][:RD] * left_in[i] + pulses[SWEEPS - 1 - i][RD:] * right_in[i]
            )
        halo_left = jnp.where(first_cell, iterate[:, :1], left_in[SWEEPS])
        halo_right = jnp.where(last_cell, iterate[:, NC - 1 :], right_in[SWEEPS])
        field_send[step, 0] = jnp.where(end == HC - 1, halo_left, iterate[:, :HC])
        field_send[step, 1] = jnp.where(end == 0, halo_right, iterate[:, cut:])
        field_plane[step, place] = field_send[step, half]
        for peer, other_half in plane_peers:
            send(group + 2, field_send.at[step, other_half], field_plane.at[step, place], peer)
        if step == 0:
            arrived(3, w_plane.at[0 : Q - 1])
            for i in range(Q):
                stepped = w_plane[i].astype(jnp.int32).astype(f32)
                w_block[RD * i : RD * (i + 1), :] = stepped * (1.0 / w_steps)
            padded[0:8, :] = jnp.zeros((8, HC), f32)
            padded[BL + 8 :, :] = jnp.zeros((8, HC), f32)
            for side, column in ((0, 0), (1, BL - 1)):
                answer = coupling * jnp.broadcast_to(
                    colb_ref[:, column : column + 1], (BL, HC)
                )
                for m in range(SWEEPS):
                    if m > 0:
                        back = w_block[...] * answer + coupling * clamp_rows(answer)
                        answer = answer - col_product(colb_parts, back)
                    padded[8 : BL + 8, :] = answer
                    own, other = frames()
                    answer_near[half, m, side] = own
                    answer_send[m, side] = other
                    still_send[m, side, 0:1, :] = answer[:1]
                    still_send[m, side, 1:2, :] = answer[BL - 1 :]
            still_recv[slot] = still_send[...]
            for peer in plane_cross:
                send(5, still_send, still_recv.at[slot], peer)
            send(9, answer_send, answer_near.at[half], partner)
        else:

            def prepare(i, carry):
                down, across, index, lane = pins_of(i)
                look[i] = table(index, rounded(1.0 - down), rounded(down), 128).astype(bf16)
                spread[i] = table(lane, rounded(1.0 - across), rounded(across), 136)
                return carry

            lax.fori_loop(0, chunks, prepare, 0, unroll=2)

        arrived(group + 2, field_plane.at[step, 0 : Q - 1])
        for i in range(Q):
            field_block[RD * i : RD * (i + 1), :] = field_plane[step, i]

        start = field_block[...]
        beside = pltpu.roll(start, 1, 1) + pltpu.roll(start, HC - 1, 1)
        middle = w_block[...] * start - coupling * (2.0 * start - beside)
        iterate = start
        for j in range(SWEEPS + 1):
            if j > 0:
                left_over = middle - (w_block[...] * iterate + coupling * clamp_rows(iterate))
                iterate = iterate + col_product(colb_parts, left_over)
            tops_send[step, j, 0:1, :] = iterate[:1]
            tops_send[step, j, 1:2, :] = iterate[BL - 1 :]
        for peer in plane_cross:
            send(group + 3, tops_send.at[step], tops_recv.at[step, slot], peer)
        padded[8 : BL + 8, :] = iterate
        own, other = frames()
        near_send[step] = other
        near[step, half] = own
        send(13 + step, near_send.at[step], near.at[step, half], partner)
        tops_recv[step, slot] = tops_send[step]

        if step == 0:
            arrived(5, still_recv.at[0 : 2 * K - 1])
            arrived(9, answer_near.at[0])
            for k in range(K):
                for m in range(SWEEPS):
                    for side in range(2):
                        for h in range(2):
                            still_all[h, m, side, 2 * k : 2 * k + 2, :] = still_recv[
                                2 * k + h, m, side
                            ]
        arrived(group + 3, tops_recv.at[step, 0 : 2 * K - 1])
        for k in range(K):
            for j in range(SWEEPS + 1):
                for h in range(2):
                    tops_all[h, j, 2 * k : 2 * k + 2, :] = tops_recv[step, 2 * k + h, j]
        arrived(13 + step, near.at[step, 0])
        spot = lax.broadcasted_iota(jnp.int32, (2 * K, HC), 0)
        even = spot % 2 == 0
        mine = pl.ds(2 * plane, 1)
        halves = []
        for h in range(2):
            from_above, from_below = [], []
            for j in range(SWEEPS + 1):
                value = tops_all[h, j]
                for i in range(j):
                    value = value + still_all[h, j - i - 1, 0] * from_above[i]
                    value = value + still_all[h, j - i - 1, 1] * from_below[i]
                over = jnp.where(even, pltpu.roll(value, 1, 0), pltpu.roll(value, 2, 0))
                under = jnp.where(
                    even, pltpu.roll(value, 2 * K - 2, 0), pltpu.roll(value, 2 * K - 1, 0)
                )
                from_above.append(jnp.where(spot < 2, 0.0, over))
                from_below.append(jnp.where(spot >= 2 * K - 2, 0.0, under))
                inflow[h, j, 0] = from_above[j]
                inflow[h, j, 1] = from_below[j]
            nearby = near[step, h]
            for i in range(SWEEPS):
                m = SWEEPS - 1 - i
                nearby = nearby + (
                    answer_near[h, m, 0] * inflow[h, i, 0, mine, :]
                    + answer_near[h, m, 1] * inflow[h, i, 1, mine, :]
                )
            above, below = nearby[:1], nearby[1 + RD : 2 + RD]
            above = jnp.where(place == 0, inflow[h, SWEEPS, 0, mine, :], above)
            below = jnp.where(place == Q - 1, inflow[h, SWEEPS, 1, mine, :], below)
            halves.append((above, nearby[1 : 1 + RD], below))

        def joined(first, second):
            over = HC - cut
            lanes = lax.broadcasted_iota(jnp.int32, (first.shape[0], over), 1)
            both = jnp.where(lanes < over // 2, first[:, cut:], second[:, :over])
            return jnp.concatenate([first[:, :cut], both, second[:, over:]], axis=1)

        row_above, current, row_below = (joined(a, b) for a, b in zip(*halves))
        row_above = jnp.where(strip == 0, current[:1], row_above)
        row_below = jnp.where(strip == strips - 1, current[RD - 1 :], row_below)

    density_ref[...] = current
    last_send[0:1, :] = row_above
    last_send[1 : 1 + RD, :] = current
    last_send[1 + RD : 2 + RD, :] = row_below
    last_send[2 + RD : 8, :] = jnp.zeros((6 - RD, NC), f32)
    last_recv[cell] = last_send[...]
    for peer in cell_peers:
        send(12, last_send, last_recv.at[cell], peer)
    arrived(12, last_recv.at[0 : C - 1])
    field = jnp.concatenate([last_recv[c] for c in range(C)], axis=1)
    centre = field[1 : 1 + RD]
    spot = lax.broadcasted_iota(jnp.int32, (RD, C * NC), 1)
    left = jnp.where(spot == 0, centre, pltpu.roll(centre, 1, 1))
    right = jnp.where(spot == C * NC - 1, centre, pltpu.roll(centre, C * NC - 1, 1))
    scale = jnp.maximum(centre, floor_level)
    velocity_y = -(0.5 * (field[2 : 2 + RD] - field[:RD])) / scale
    velocity_x = -(0.5 * (right - left)) / scale
    tables = []
    for i, velocity in enumerate((velocity_y, velocity_x)):
        vel_bins[i, bins:, :] = jnp.zeros((128 - bins, 128), f32)
        for n in range(bins // RD):
            vel_bins[i, RD * n : RD * (n + 1), :] = velocity[:, 128 * n : 128 * (n + 1)]
        turned = jnp.transpose(vel_bins[i])
        past = jnp.broadcast_to(pltpu.roll(turned[:8], 128 - RD, 1)[:1], (8, 128))
        tables += [turned.astype(bf16), past.astype(bf16)]
    tables = jnp.concatenate(tables, axis=0)

    def sample(i, carry):
        sampled = jnp.dot(tables, look[i], preferred_element_type=f32)
        across = spread[i]
        out_y = jnp.sum(sampled[:136] * across, axis=0, keepdims=True)
        out_x = jnp.sum(sampled[136:] * across, axis=0, keepdims=True)
        span = pl.ds(pl.multiple_of(128 * i, 128), 128)
        pinv_ref[:, span] = jnp.concatenate([out_y, out_x], axis=0)
        return carry

    lax.fori_loop(0, chunks, sample, 0, unroll=4)
    for group, span in sent:
        pltpu.make_async_copy(span, span, send_sem.at[group]).wait()


def diffuse(pin_rows, pin_cols, pin_fracs, pin_weights, capacity, blockage, row_blocks, col_blocks):
    pins = pin_rows.shape[0]
    chunks = pins // 128
    strips = lax.axis_size("strip")
    C = lax.axis_size("cells")
    RD, NC = capacity.shape
    NB = row_blocks.shape[0]
    K, BL = col_blocks.shape[:2]
    Q = strips // K
    HC = 128 * ((NB + 1) // 2)
    vmem = pl.BlockSpec(memory_space=pltpu.VMEM)
    bins = RD * C * NC // 128
    shapes = [
        ((chunks, 128), jnp.int32),
        ((chunks, 128), jnp.int32),
        ((chunks, 128), f32),
        ((2, pins), f32),
        ((RD, NC), jnp.int32),
        ((RD, NC), f32),
        ((NB, 128, 128), f32),
        ((BL, BL), f32),
        ((bins, 128), f32),
        ((C, RD, NC), f32),
        ((chunks, 128, 128), bf16),
        ((chunks, 136, 128), f32),
        ((2, 128, 128), f32),
        ((2, C, 1, NC), f32),
        ((C, RD, NC), f32),
        ((2, C, 1, NC), f32),
        ((2, 1, NC), f32),
        ((2, 1, NC), f32),
        ((2, RD, HC), jnp.int16),
        ((Q, RD, HC), jnp.int16),
        ((BL, HC), f32),
        ((NB, 128, 384), bf16),
        ((BL, 3 * BL), bf16),
        ((STEPS, 2, RD, 128), f32),
        ((STEPS, 2, RD, 128), f32),
        ((STEPS, 2, RD, HC), f32),
        ((STEPS, Q, RD, HC), f32),
        ((BL, HC), f32),
        ((BL + 16, HC), f32),
        ((SWEEPS, 2, 8, HC), f32),
        ((2, SWEEPS, 2, 8, HC), f32),
        ((STEPS, 8, HC), f32),
        ((STEPS, 2, 8, HC), f32),
        ((SWEEPS, 2, 2, HC), f32),
        ((2 * K, SWEEPS, 2, 2, HC), f32),
        ((2, SWEEPS, 2, 2 * K, HC), f32),
        ((STEPS, SWEEPS + 1, 2, HC), f32),
        ((STEPS, 2 * K, SWEEPS + 1, 2, HC), f32),
        ((2, SWEEPS + 1, 2 * K, HC), f32),
        ((2, SWEEPS + 1, 2, 2 * K, HC), f32),
        ((8, NC), f32),
        ((C, 8, NC), f32),
    ]
    return pl.pallas_call(
        functools.partial(adi_kernel, (K, Q, C, RD, NC, BL)),
        out_shape=(
            jax.ShapeDtypeStruct((RD, NC), f32),
            jax.ShapeDtypeStruct((2, pins), f32),
        ),
        in_specs=[pl.BlockSpec(memory_space=pltpu.HBM)] * 8,
        out_specs=(vmem, vmem),
        scratch_shapes=[pltpu.VMEM(shape, dtype) for shape, dtype in shapes]
        + [pltpu.SemaphoreType.DMA((n,)) for n in (15, 15, 8)],
        compiler_params=pltpu.CompilerParams(
            collective_id=0, has_side_effects=True
        ),
        name="adi",
    )(
        pin_rows.reshape(chunks, 128),
        pin_cols.reshape(chunks, 128),
        pin_fracs,
        pin_weights.reshape(chunks, 128),
        capacity,
        blockage,
        row_blocks,
        col_blocks,
    )


def solution(mesh):
    placed = (
        P(("strip", "cells")),
        P(("strip", "cells")),
        P(None, ("strip", "cells")),
        P(("strip", "cells")),
        P("strip", "cells"),
        P("strip", "cells"),
        P("cells", None, None),
        P(),
    )
    return jax.shard_map(
        diffuse,
        mesh=mesh,
        in_specs=placed,
        out_specs=(P("strip", "cells"), P(None, ("strip", "cells"))),
        check_vma=False,
    )
```

```python
import functools

import jax
import jax.numpy as jnp
from jax import lax
from jax.experimental import pallas as pl
from jax.experimental.pallas import tpu as pltpu
from jax.sharding import PartitionSpec as P

SWEEPS = 3
STEPS = 2
coupling = 2.0
floor_level = 0.5
w_steps = 8191.0
f32 = jnp.float32
bf16 = jnp.bfloat16


def exact_parts(values):
    high = values.astype(bf16)
    return high, (values - high.astype(f32)).astype(bf16)


def row_product(values, blocks_ref, first=0):
    pieces = []
    for n in range(values.shape[1] // 128):
        high, low = exact_parts(values[:, 128 * n : 128 * (n + 1)])
        pieces.append(
            lax.dot_general(
                jnp.concatenate([high, low, high], axis=1),
                blocks_ref[first + n],
                (((1,), (1,)), ((), ())),
                preferred_element_type=f32,
            )
        )
    return jnp.concatenate(pieces, axis=1)


def col_product(matrix_ref, values):
    high, low = exact_parts(values)
    parts = jnp.concatenate([high, low, high], axis=0)
    return jnp.dot(matrix_ref[...], parts, preferred_element_type=f32)


def table(index, first, second, count):
    spot = lax.broadcasted_iota(jnp.int32, (count, index.shape[1]), 0)
    return jnp.where(spot == index, first, jnp.where(spot == index + 1, second, 0.0))


def adi_kernel(
    sizes,
    rows_hbm,
    cols_hbm,
    fracs_hbm,
    pinw_hbm,
    cap_hbm,
    blk_hbm,
    rowb_hbm,
    colb_hbm,
    density_ref,
    pinv_ref,
    rows_ref,
    cols_ref,
    pinw_ref,
    fracs_ref,
    cap_ref,
    blk_ref,
    rowb_ref,
    colb_ref,
    bin_sums,
    part_ref,
    look,
    spread,
    vel_bins,
    edge_part,
    part_recv,
    edge_recv,
    wedge_send,
    wedge_recv,
    w_send,
    w_plane,
    w_block,
    rowb_parts,
    colb_parts,
    rim_send,
    rim_recv,
    field_send,
    field_plane,
    field_block,
    inflow_send,
    inflow_plane,
    inflow_block,
    waves,
    padded,
    answer_send,
    answer_near,
    near_send,
    near,
    still_send,
    still_recv,
    still_all,
    tops_send,
    tops_recv,
    tops_all,
    inflow,
    last_send,
    last_recv,
    send_sem,
    recv_sem,
    load_sem,
):
    K, Q, C, RD, NC, BL = sizes
    strips = K * Q
    HC = w_send.shape[2]
    cut = NC - HC
    strip = lax.axis_index("strip")
    cell = lax.axis_index("cells")
    plane = strip // Q
    place = strip % Q
    depth = Q // 2
    half = (place // 2) % 2
    strip_side = place % 2
    first_cell, last_cell = cell == 0, cell == C - 1
    first_plane, last_plane = plane == 0, plane == K - 1

    def at(strip_id, cell_id):
        return (strip_id, cell_id)

    cell_peers = [at(strip, (cell + d) % C) for d in range(1, C)]
    above_strip, below_strip = (strip + strips - 1) % strips, (strip + 1) % strips
    offsets = [(dz, dy) for dz in range(depth) for dy in range(2) if (dz, dy) != (0, 0)]
    offsets.sort(key=lambda o: -(min(o[0], depth - o[0]) + 2 * o[1]))
    plane_peers = []
    for dz, dy in offsets:
        other = ((place // 2 + dz) % depth) * 2 + (place % 2 + dy) % 2
        plane_peers.append((at(plane * Q + other, cell), (half + dz) % 2))
    partner = at(strip + 2 - 4 * half, cell)
    shifts = [(dk, dz) for dk in range(K) for dz in range(2) if (dk, dz) != (0, 0)]
    shifts.sort(key=lambda o: -(min(o[0], K - o[0]) + o[1]))
    plane_cross = [
        at(((plane + dk) % K) * Q + place + dz * (2 - 4 * half), cell) for dk, dz in shifts
    ]
    slot = 2 * plane + half
    row_peers = [at(s, (cell + d) % C) for s in (above_strip, below_strip) for d in range(C)]

    barrier = pltpu.get_barrier_semaphore()
    greeted = cell_peers + [p for p, _ in plane_peers] + plane_cross + row_peers
    for peer in greeted:
        pl.semaphore_signal(barrier, 1, device_id=peer, device_id_type=pl.DeviceIdType.MESH)

    sent = []

    def send(group, source, target, peer):
        pltpu.make_async_remote_copy(
            src_ref=source,
            dst_ref=target,
            send_sem=send_sem.at[group],
            recv_sem=recv_sem.at[group],
            device_id=peer,
            device_id_type=pl.DeviceIdType.MESH,
        ).start()

    def arrived(group, span):
        sent.append((group, span))
        pltpu.make_async_copy(span, span, recv_sem.at[group]).wait()

    loads = [
        pltpu.make_async_copy(source, target, load_sem.at[i])
        for i, (source, target) in enumerate(
            (
                (rows_hbm, rows_ref),
                (cols_hbm, cols_ref),
                (pinw_hbm, pinw_ref),
                (fracs_hbm, fracs_ref),
                (cap_hbm, cap_ref),
                (blk_hbm, blk_ref),
                (rowb_hbm, rowb_ref),
                (colb_hbm.at[plane], colb_ref),
            )
        )
    ]
    for load in loads:
        load.start()
    for load in loads:
        load.wait()

    chunks = rows_ref.shape[0]
    bins = bin_sums.shape[0]

    def pins_of(i):
        span = pl.ds(pl.multiple_of(128 * i, 128), 128)
        down, across = fracs_ref[0:1, span], fracs_ref[1:2, span]
        column = cols_ref[pl.ds(i, 1), :]
        tile = lax.shift_right_logical(column, 7)
        return down, across, tile * RD + rows_ref[pl.ds(i, 1), :], column - tile * 128

    def rounded(values):
        return values.astype(bf16).astype(f32)

    def add_pins(i, total):
        down, across, index, lane = pins_of(i)
        heavy = pinw_ref[pl.ds(i, 1), :]
        where_down = table(index, rounded(heavy * (1.0 - down)), rounded(heavy * down), bins)
        where_across = table(lane, rounded(1.0 - across), rounded(across), 136)
        return total + lax.dot_general(
            where_down.astype(bf16),
            where_across.astype(bf16),
            (((1,), (1,)), ((), ())),
            preferred_element_type=f32,
        )

    total = lax.fori_loop(0, chunks, add_pins, jnp.zeros((bins, 136), f32), unroll=4)
    spot = lax.broadcasted_iota(jnp.int32, (bins, 128), 1)
    past = jnp.where(spot == 0, total[:, 128:129], 0.0)
    bin_sums[...] = total[:, :128] + pltpu.roll(past, RD, 0)
    for c in range(C):
        for n in range(NC // 128):
            tile = c * (NC // 128) + n
            part_ref[c, :, 128 * n : 128 * (n + 1)] = bin_sums[RD * tile : RD * (tile + 1), :]

    weights = cap_ref[...].astype(f32) * (1.0 - blk_ref[...])
    whole = jnp.round(weights * w_steps).astype(jnp.int32).astype(jnp.int16)
    w_send[0] = whole[:, :HC]
    w_send[1] = whole[:, cut:]
    w_plane[place] = w_send[half]
    wedge_send[0] = weights[:1]
    wedge_send[1] = weights[RD - 1 :]
    for c in range(C):
        edge_part[0, c] = part_ref[c, :1]
        edge_part[1, c] = part_ref[c, RD - 1 :]
    pl.semaphore_wait(barrier, len(greeted))

    for d in range(C):
        other = (cell + d) % C
        send(1, edge_part.at[0, other], edge_recv.at[1, cell], at(above_strip, other))
        send(1, edge_part.at[1, other], edge_recv.at[0, cell], at(below_strip, other))
    send(2, wedge_send.at[0], wedge_recv.at[1], at(above_strip, cell))
    send(2, wedge_send.at[1], wedge_recv.at[0], at(below_strip, cell))
    for d in range(1, C):
        other = (cell + d) % C
        send(0, part_ref.at[other], part_recv.at[C - 1 - d], at(strip, other))
    for peer, other_half in plane_peers:
        send(3, w_send.at[other_half], w_plane.at[place], peer)

    for n in range(rowb_ref.shape[0]):
        high, low = exact_parts(rowb_ref[n])
        rowb_parts[n] = jnp.concatenate([high, high, low], axis=1)
    high, low = exact_parts(colb_ref[...])
    colb_parts[...] = jnp.concatenate([high, high, low], axis=1)


    def along_inside(values):
        left = pltpu.roll(values, 1, 1)
        right = pltpu.roll(values, NC - 1, 1)
        spot = lax.broadcasted_iota(jnp.int32, values.shape, 1)
        left = jnp.where(spot == 0, jnp.where(first_cell, values, 0.0), left)
        right = jnp.where(spot == NC - 1, jnp.where(last_cell, values, 0.0), right)
        return 2.0 * values - left - right

    def along_half(values):
        left = pltpu.roll(values, 1, 1)
        right = pltpu.roll(values, HC - 1, 1)
        spot = lax.broadcasted_iota(jnp.int32, values.shape, 1)
        at_left = jnp.logical_and(half == 0, first_cell)
        at_right = jnp.logical_and(half == 1, last_cell)
        left = jnp.where(spot == 0, jnp.where(at_left, values, 0.0), left)
        right = jnp.where(spot == HC - 1, jnp.where(at_right, values, 0.0), right)
        return 2.0 * values - left - right

    weights_two = jnp.concatenate([weights, weights], axis=0)
    spot = lax.broadcasted_iota(jnp.int32, (2 * RD, NC), 1)
    row = lax.broadcasted_iota(jnp.int32, (2 * RD, NC), 0)
    unit = jnp.where(spot == jnp.where(row < RD, 0, NC - 1), coupling, 0.0)
    pulse = row_product(unit, rowb_parts)
    pulses = [pulse]
    for _ in range(SWEEPS - 1):
        back = weights_two * pulse + coupling * along_inside(pulse)
        pulse = pulse - row_product(back, rowb_parts)
        pulses.append(pulse)

    arrived(1, edge_recv)
    arrived(2, wedge_recv)
    arrived(0, part_recv.at[0 : C - 1])
    density = part_ref[cell]
    for d in range(C - 1):
        density = density + part_recv[d]
    current = density / weights
    row_above = edge_recv[0, 0]
    row_below = edge_recv[1, 0]
    for c in range(1, C):
        row_above = row_above + edge_recv[0, c]
        row_below = row_below + edge_recv[1, c]
    row_above = row_above / wedge_recv[0]
    row_below = row_below / wedge_recv[1]
    row_above = jnp.where(strip == 0, current[:1], row_above)
    row_below = jnp.where(strip == strips - 1, current[RD - 1 :], row_below)

    def frame(pair):
        base = pl.multiple_of(RD * 2 * pair, 2 * RD)
        inner = padded[pl.ds(base + 8, 2 * RD), :]
        over = padded[pl.ds(base + 7, 1), :]
        under = padded[pl.ds(base + 8 + 2 * RD, 1), :]
        fill = jnp.zeros((6 - RD, HC), f32)
        upper = jnp.concatenate([over, inner[: RD + 1], fill], axis=0)
        lower = jnp.concatenate([inner[RD - 1 :], under, fill], axis=0)
        return jnp.where(strip_side == 0, upper, lower)

    def frames():
        return frame(place // 2), frame(place // 2 + 1 - 2 * half)

    small = lax.broadcasted_iota(jnp.int32, (RD, 128), 1)

    def clamp_rows(values):
        shape = values.shape
        spot = lax.broadcasted_iota(jnp.int32, shape, 0)
        up = pltpu.roll(values, 1, 0)
        down = pltpu.roll(values, shape[0] - 1, 0)
        up = jnp.where(spot == 0, jnp.where(first_plane, values, 0.0), up)
        down = jnp.where(spot == shape[0] - 1, jnp.where(last_plane, values, 0.0), down)
        return 2.0 * values - up - down

    for step in range(STEPS):
        up = jnp.concatenate([row_above, current[: RD - 1]], axis=0)
        down = jnp.concatenate([current[1:], row_below], axis=0)
        source = weights * current - coupling * (2.0 * current - up - down)
        iterate = current
        levels = [iterate]
        for _ in range(SWEEPS):
            left_over = source - (weights * iterate + coupling * along_inside(iterate))
            iterate = iterate + row_product(left_over, rowb_parts)
            levels.append(iterate)
        for side, column in ((0, 0), (1, NC - 1)):
            message = jnp.zeros((RD, 128), f32)
            for j in range(SWEEPS + 1):
                message = jnp.where(small == j, levels[j][:, column : column + 1], message)
            for m in range(SWEEPS):
                mine = pulses[m][side * RD : (side + 1) * RD, column : column + 1]
                message = jnp.where(small == SWEEPS + 1 + m, mine, message)
            rim_send[step, side] = message
        group = 4 + 4 * step
        send(group, rim_send.at[step, 0], rim_recv.at[step, 1], at(strip, (cell + C - 1) % C))
        send(group, rim_send.at[step, 1], rim_recv.at[step, 0], at(strip, (cell + 1) % C))

        field_send[step, 0] = iterate[:, :HC]
        field_send[step, 1] = iterate[:, cut:]
        field_plane[step, place] = field_send[step, half]
        for peer, other_half in plane_peers:
            send(group + 2, field_send.at[step, other_half], field_plane.at[step, place], peer)
        arrived(group, rim_recv.at[step])
        edges = []
        for side in range(2):
            own = [rim_send[step, side][:, i : i + 1] for i in range(2 * SWEEPS + 1)]
            far = [rim_recv[step, side][:, i : i + 1] for i in range(2 * SWEEPS + 1)]
            mine, theirs = [], []
            for j in range(SWEEPS + 1):
                a, b = own[j], far[j]
                for i in range(j):
                    a = a + own[SWEEPS + j - i] * theirs[i]
                    b = b + far[SWEEPS + j - i] * mine[i]
                mine.append(a)
                theirs.append(b)
            edges.append(theirs)
        left_in = [jnp.where(first_cell, 0.0, e) for e in edges[0]]
        right_in = [jnp.where(last_cell, 0.0, e) for e in edges[1]]
        halo_left = jnp.where(first_cell, iterate[:, :1], left_in[SWEEPS])
        halo_right = jnp.where(last_cell, iterate[:, NC - 1 :], right_in[SWEEPS])
        far_left = pulses[1][:RD, cut - 1 : cut] * left_in[0]
        far_right = pulses[1][RD:, HC : HC + 1] * right_in[0]
        for h, entries in (
            (0, left_in[:SWEEPS] + [halo_left, far_right]),
            (1, right_in[:SWEEPS] + [halo_right, far_left]),
        ):
            message = jnp.zeros((RD, 128), f32)
            for i, entry in enumerate(entries):
                message = jnp.where(small == i, entry, message)
            packed = message[:1]
            for r in range(1, RD):
                packed = packed + pltpu.roll(message, 8 * r, 1)[r : r + 1]
            inflow_send[step, h] = packed
        inflow_plane[step, place] = inflow_send[step, half]
        for peer, other_half in plane_peers:
            send(15 + step, inflow_send.at[step, other_half], inflow_plane.at[step, place], peer)

        if step == 0:
            arrived(3, w_plane.at[0 : Q - 1])
            for i in range(Q):
                stepped = w_plane[i].astype(jnp.int32).astype(f32)
                w_block[RD * i : RD * (i + 1), :] = stepped * (1.0 / w_steps)
            padded[0:8, :] = jnp.zeros((8, HC), f32)
            padded[BL + 8 :, :] = jnp.zeros((8, HC), f32)
            for side, column in ((0, 0), (1, BL - 1)):
                answer = coupling * jnp.broadcast_to(
                    colb_ref[:, column : column + 1], (BL, HC)
                )
                for m in range(SWEEPS):
                    if m > 0:
                        back = w_block[...] * answer + coupling * clamp_rows(answer)
                        answer = answer - col_product(colb_parts, back)
                    padded[8 : BL + 8, :] = answer
                    own, other = frames()
                    answer_near[half, m, side] = own
                    answer_send[m, side] = other
                    still_send[m, side, 0:1, :] = answer[:1]
                    still_send[m, side, 1:2, :] = answer[BL - 1 :]
            still_recv[slot] = still_send[...]
            for peer in plane_cross:
                send(5, still_send, still_recv.at[slot], peer)
            send(9, answer_send, answer_near.at[half], partner)

            place_in_half = lax.broadcasted_iota(jnp.int32, (8, HC), 1)
            outer = jnp.where(half == 0, 0, HC - 1)
            unit = jnp.where(place_in_half == outer, coupling, 0.0)
            wave = row_product(unit, rowb_parts, 2 * half)[:1]
            wave = jnp.broadcast_to(wave, (BL, HC))
            waves[0] = wave
            for m in range(1, SWEEPS):
                back = w_block[...] * wave + coupling * along_half(wave)
                wave = wave - row_product(back, rowb_parts, 2 * half)
                waves[m] = wave
            unit = jnp.where(place_in_half == HC - 1 - outer, coupling, 0.0)
            inner_wave = row_product(unit, rowb_parts, 2 * half)[:1]
        else:

            def prepare(i, carry):
                down, across, index, lane = pins_of(i)
                look[i] = table(index, rounded(1.0 - down), rounded(down), 128).astype(bf16)
                spread[i] = table(lane, rounded(1.0 - across), rounded(across), 136)
                return carry

            lax.fori_loop(0, chunks, prepare, 0, unroll=2)

        arrived(group + 2, field_plane.at[step, 0 : Q - 1])
        for i in range(Q):
            field_block[RD * i : RD * (i + 1), :] = field_plane[step, i]

        arrived(15 + step, inflow_plane.at[step, 0 : Q - 1])
        for i in range(Q):
            inflow_block[RD * i : RD * (i + 1), :] = jnp.broadcast_to(
                inflow_plane[step, i], (RD, 128)
            )
        packed = inflow_block[...]
        turn = lax.broadcasted_iota(jnp.int32, (BL, 128), 0) % RD
        entries = packed
        for r in range(1, RD):
            entries = jnp.where(turn == r, pltpu.roll(packed, 128 - 8 * r, 1), entries)
        start = field_block[...] + inner_wave * entries[:, SWEEPS + 1 : SWEEPS + 2]
        for i in range(SWEEPS):
            start = start + waves[SWEEPS - 1 - i] * entries[:, i : i + 1]
        spot = lax.broadcasted_iota(jnp.int32, (BL, HC), 1)
        unused = jnp.where(half == 0, HC - 1, 0)
        start = jnp.where(spot == unused, entries[:, SWEEPS : SWEEPS + 1], start)
        beside = pltpu.roll(start, 1, 1) + pltpu.roll(start, HC - 1, 1)
        middle = w_block[...] * start - coupling * (2.0 * start - beside)
        iterate = start
        for j in range(SWEEPS + 1):
            if j > 0:
                left_over = middle - (w_block[...] * iterate + coupling * clamp_rows(iterate))
                iterate = iterate + col_product(colb_parts, left_over)
            tops_send[step, j, 0:1, :] = iterate[:1]
            tops_send[step, j, 1:2, :] = iterate[BL - 1 :]
        for peer in plane_cross:
            send(group + 3, tops_send.at[step], tops_recv.at[step, slot], peer)
        padded[8 : BL + 8, :] = iterate
        own, other = frames()
        near_send[step] = other
        near[step, half] = own
        send(13 + step, near_send.at[step], near.at[step, half], partner)
        tops_recv[step, slot] = tops_send[step]

        if step == 0:
            arrived(5, still_recv.at[0 : 2 * K - 1])
            arrived(9, answer_near.at[0])
            for k in range(K):
                for m in range(SWEEPS):
                    for side in range(2):
                        for h in range(2):
                            still_all[h, m, side, 2 * k : 2 * k + 2, :] = still_recv[
                                2 * k + h, m, side
                            ]
        arrived(group + 3, tops_recv.at[step, 0 : 2 * K - 1])
        for k in range(K):
            for j in range(SWEEPS + 1):
                for h in range(2):
                    tops_all[h, j, 2 * k : 2 * k + 2, :] = tops_recv[step, 2 * k + h, j]
        arrived(13 + step, near.at[step, 0])
        spot = lax.broadcasted_iota(jnp.int32, (2 * K, HC), 0)
        even = spot % 2 == 0
        mine = pl.ds(2 * plane, 1)
        halves = []
        for h in range(2):
            from_above, from_below = [], []
            for j in range(SWEEPS + 1):
                value = tops_all[h, j]
                for i in range(j):
                    value = value + still_all[h, j - i - 1, 0] * from_above[i]
                    value = value + still_all[h, j - i - 1, 1] * from_below[i]
                over = jnp.where(even, pltpu.roll(value, 1, 0), pltpu.roll(value, 2, 0))
                under = jnp.where(
                    even, pltpu.roll(value, 2 * K - 2, 0), pltpu.roll(value, 2 * K - 1, 0)
                )
                from_above.append(jnp.where(spot < 2, 0.0, over))
                from_below.append(jnp.where(spot >= 2 * K - 2, 0.0, under))
                inflow[h, j, 0] = from_above[j]
                inflow[h, j, 1] = from_below[j]
            nearby = near[step, h]
            for i in range(SWEEPS):
                m = SWEEPS - 1 - i
                nearby = nearby + (
                    answer_near[h, m, 0] * inflow[h, i, 0, mine, :]
                    + answer_near[h, m, 1] * inflow[h, i, 1, mine, :]
                )
            above, below = nearby[:1], nearby[1 + RD : 2 + RD]
            above = jnp.where(place == 0, inflow[h, SWEEPS, 0, mine, :], above)
            below = jnp.where(place == Q - 1, inflow[h, SWEEPS, 1, mine, :], below)
            halves.append((above, nearby[1 : 1 + RD], below))

        def joined(first, second):
            over = HC - cut
            lanes = lax.broadcasted_iota(jnp.int32, (first.shape[0], over), 1)
            both = jnp.where(lanes < over // 2, first[:, cut:], second[:, :over])
            return jnp.concatenate([first[:, :cut], both, second[:, over:]], axis=1)

        row_above, current, row_below = (joined(a, b) for a, b in zip(*halves))
        row_above = jnp.where(strip == 0, current[:1], row_above)
        row_below = jnp.where(strip == strips - 1, current[RD - 1 :], row_below)

    density_ref[...] = current
    last_send[0:1, :] = row_above
    last_send[1 : 1 + RD, :] = current
    last_send[1 + RD : 2 + RD, :] = row_below
    last_send[2 + RD : 8, :] = jnp.zeros((6 - RD, NC), f32)
    last_recv[cell] = last_send[...]
    for peer in cell_peers:
        send(12, last_send, last_recv.at[cell], peer)
    arrived(12, last_recv.at[0 : C - 1])
    field = jnp.concatenate([last_recv[c] for c in range(C)], axis=1)
    centre = field[1 : 1 + RD]
    spot = lax.broadcasted_iota(jnp.int32, (RD, C * NC), 1)
    left = jnp.where(spot == 0, centre, pltpu.roll(centre, 1, 1))
    right = jnp.where(spot == C * NC - 1, centre, pltpu.roll(centre, C * NC - 1, 1))
    scale = jnp.maximum(centre, floor_level)
    velocity_y = -(0.5 * (field[2 : 2 + RD] - field[:RD])) / scale
    velocity_x = -(0.5 * (right - left)) / scale
    tables = []
    for i, velocity in enumerate((velocity_y, velocity_x)):
        vel_bins[i, bins:, :] = jnp.zeros((128 - bins, 128), f32)
        for n in range(bins // RD):
            vel_bins[i, RD * n : RD * (n + 1), :] = velocity[:, 128 * n : 128 * (n + 1)]
        turned = jnp.transpose(vel_bins[i])
        past = jnp.broadcast_to(pltpu.roll(turned[:8], 128 - RD, 1)[:1], (8, 128))
        tables += [turned.astype(bf16), past.astype(bf16)]
    tables = jnp.concatenate(tables, axis=0)

    def sample(i, carry):
        sampled = jnp.dot(tables, look[i], preferred_element_type=f32)
        across = spread[i]
        out_y = jnp.sum(sampled[:136] * across, axis=0, keepdims=True)
        out_x = jnp.sum(sampled[136:] * across, axis=0, keepdims=True)
        span = pl.ds(pl.multiple_of(128 * i, 128), 128)
        pinv_ref[:, span] = jnp.concatenate([out_y, out_x], axis=0)
        return carry

    lax.fori_loop(0, chunks, sample, 0, unroll=4)
    for group, span in sent:
        pltpu.make_async_copy(span, span, send_sem.at[group]).wait()


def diffuse(pin_rows, pin_cols, pin_fracs, pin_weights, capacity, blockage, row_blocks, col_blocks):
    pins = pin_rows.shape[0]
    chunks = pins // 128
    strips = lax.axis_size("strip")
    C = lax.axis_size("cells")
    RD, NC = capacity.shape
    NB = row_blocks.shape[0]
    K, BL = col_blocks.shape[:2]
    Q = strips // K
    HC = 128 * ((NB + 1) // 2)
    vmem = pl.BlockSpec(memory_space=pltpu.VMEM)
    bins = RD * C * NC // 128
    shapes = [
        ((chunks, 128), jnp.int32),
        ((chunks, 128), jnp.int32),
        ((chunks, 128), f32),
        ((2, pins), f32),
        ((RD, NC), jnp.int32),
        ((RD, NC), f32),
        ((NB, 128, 128), f32),
        ((BL, BL), f32),
        ((bins, 128), f32),
        ((C, RD, NC), f32),
        ((chunks, 128, 128), bf16),
        ((chunks, 136, 128), f32),
        ((2, 128, 128), f32),
        ((2, C, 1, NC), f32),
        ((C, RD, NC), f32),
        ((2, C, 1, NC), f32),
        ((2, 1, NC), f32),
        ((2, 1, NC), f32),
        ((2, RD, HC), jnp.int16),
        ((Q, RD, HC), jnp.int16),
        ((BL, HC), f32),
        ((NB, 128, 384), bf16),
        ((BL, 3 * BL), bf16),
        ((STEPS, 2, RD, 128), f32),
        ((STEPS, 2, RD, 128), f32),
        ((STEPS, 2, RD, HC), f32),
        ((STEPS, Q, RD, HC), f32),
        ((BL, HC), f32),
        ((STEPS, 2, 1, 128), f32),
        ((STEPS, Q, 1, 128), f32),
        ((BL, 128), f32),
        ((SWEEPS, BL, HC), f32),
        ((BL + 16, HC), f32),
        ((SWEEPS, 2, 8, HC), f32),
        ((2, SWEEPS, 2, 8, HC), f32),
        ((STEPS, 8, HC), f32),
        ((STEPS, 2, 8, HC), f32),
        ((SWEEPS, 2, 2, HC), f32),
        ((2 * K, SWEEPS, 2, 2, HC), f32),
        ((2, SWEEPS, 2, 2 * K, HC), f32),
        ((STEPS, SWEEPS + 1, 2, HC), f32),
        ((STEPS, 2 * K, SWEEPS + 1, 2, HC), f32),
        ((2, SWEEPS + 1, 2 * K, HC), f32),
        ((2, SWEEPS + 1, 2, 2 * K, HC), f32),
        ((8, NC), f32),
        ((C, 8, NC), f32),
    ]
    results = pl.pallas_call(
        functools.partial(adi_kernel, (K, Q, C, RD, NC, BL)),
        out_shape=(
            jax.ShapeDtypeStruct((RD, NC), f32),
            jax.ShapeDtypeStruct((2, pins), f32),
        ),
        in_specs=[pl.BlockSpec(memory_space=pltpu.HBM)] * 8,
        out_specs=(vmem, vmem),
        scratch_shapes=[pltpu.VMEM(shape, dtype) for shape, dtype in shapes]
        + [pltpu.SemaphoreType.DMA((n,)) for n in (17, 17, 8)],
        compiler_params=pltpu.CompilerParams(
            collective_id=0, has_side_effects=True
        ),
        name="adi",
    )(
        pin_rows.reshape(chunks, 128),
        pin_cols.reshape(chunks, 128),
        pin_fracs,
        pin_weights.reshape(chunks, 128),
        capacity,
        blockage,
        row_blocks,
        col_blocks,
    )
    return pl.pallas_call(
        hand_over,
        out_shape=[jax.ShapeDtypeStruct(r.shape, r.dtype) for r in results],
        in_specs=[pl.BlockSpec(memory_space=pl.ANY)] * 2,
        out_specs=[pl.BlockSpec(memory_space=pl.ANY)] * 2,
        scratch_shapes=[pltpu.SemaphoreType.DMA((2,))],
        name="hand_over",
    )(*results)


def hand_over(first, second, first_out, second_out, sems):
    copies = [
        pltpu.make_async_copy(first, first_out, sems.at[0]),
        pltpu.make_async_copy(second, second_out, sems.at[1]),
    ]
    for copy in copies:
        copy.start()
    for copy in copies:
        copy.wait()


def solution(mesh):
    placed = (
        P(("strip", "cells")),
        P(("strip", "cells")),
        P(None, ("strip", "cells")),
        P(("strip", "cells")),
        P("strip", "cells"),
        P("strip", "cells"),
        P("cells", None, None),
        P(),
    )
    return jax.shard_map(
        diffuse,
        mesh=mesh,
        in_specs=placed,
        out_specs=(P("strip", "cells"), P(None, ("strip", "cells"))),
        check_vma=False,
    )
```

```python
import functools

import jax
import jax.numpy as jnp
from jax import lax
from jax.experimental import pallas as pl
from jax.experimental.pallas import tpu as pltpu
from jax.sharding import PartitionSpec as P

SWEEPS = 3
STEPS = 2
coupling = 2.0
floor_level = 0.5
w_steps = 8191.0
f32 = jnp.float32
bf16 = jnp.bfloat16


def exact_parts(values):
    high = values.astype(bf16)
    return high, (values - high.astype(f32)).astype(bf16)


def row_product(values, blocks_ref):
    pieces = []
    for n in range(blocks_ref.shape[0]):
        high, low = exact_parts(values[:, 128 * n : 128 * (n + 1)])
        pieces.append(
            lax.dot_general(
                jnp.concatenate([high, low, high], axis=1),
                blocks_ref[n],
                (((1,), (1,)), ((), ())),
                preferred_element_type=f32,
            )
        )
    return jnp.concatenate(pieces, axis=1)


def col_product(matrix_ref, values):
    high, low = exact_parts(values)
    parts = jnp.concatenate([high, low, high], axis=0)
    return jnp.dot(matrix_ref[...], parts, preferred_element_type=f32)


def table(index, first, second, count):
    spot = lax.broadcasted_iota(jnp.int32, (count, index.shape[1]), 0)
    return jnp.where(spot == index, first, jnp.where(spot == index + 1, second, 0.0))


def adi_kernel(
    sizes,
    rows_hbm,
    cols_hbm,
    fracs_hbm,
    pinw_hbm,
    cap_hbm,
    blk_hbm,
    rowb_hbm,
    colb_hbm,
    density_ref,
    pinv_ref,
    rows_ref,
    cols_ref,
    pinw_ref,
    fracs_ref,
    cap_ref,
    blk_ref,
    rowb_ref,
    colb_ref,
    bin_sums,
    part_ref,
    look,
    spread,
    vel_bins,
    edge_part,
    part_recv,
    edge_recv,
    wedge_send,
    wedge_recv,
    w_send,
    w_plane,
    w_block,
    rowb_parts,
    colb_parts,
    rim_send,
    rim_recv,
    field_send,
    field_plane,
    field_block,
    padded,
    answer_send,
    answer_near,
    near_send,
    near,
    still_send,
    still_recv,
    still_all,
    tops_send,
    tops_recv,
    tops_all,
    inflow,
    last_send,
    last_recv,
    send_sem,
    recv_sem,
    load_sem,
):
    K, Q, C, RD, NC, BL = sizes
    strips = K * Q
    HC = w_send.shape[2]
    cut = NC - HC
    strip = lax.axis_index("strip")
    cell = lax.axis_index("cells")
    plane = strip // Q
    place = strip % Q
    depth = Q // 2
    half = (place // 2) % 2
    strip_side = place % 2
    first_cell, last_cell = cell == 0, cell == C - 1
    first_plane, last_plane = plane == 0, plane == K - 1

    def at(strip_id, cell_id):
        return (strip_id, cell_id)

    cell_peers = [at(strip, (cell + d) % C) for d in range(1, C)]
    above_strip, below_strip = (strip + strips - 1) % strips, (strip + 1) % strips
    offsets = [(dz, dy) for dz in range(depth) for dy in range(2) if (dz, dy) != (0, 0)]
    offsets.sort(key=lambda o: -(min(o[0], depth - o[0]) + 2 * o[1]))
    plane_peers = []
    for dz, dy in offsets:
        other = ((place // 2 + dz) % depth) * 2 + (place % 2 + dy) % 2
        plane_peers.append((at(plane * Q + other, cell), (half + dz) % 2))
    partner = at(strip + 2 - 4 * half, cell)
    shifts = [(dk, dz) for dk in range(K) for dz in range(2) if (dk, dz) != (0, 0)]
    shifts.sort(key=lambda o: -(min(o[0], K - o[0]) + o[1]))
    plane_cross = [
        at(((plane + dk) % K) * Q + place + dz * (2 - 4 * half), cell) for dk, dz in shifts
    ]
    slot = 2 * plane + half
    row_peers = [at(s, (cell + d) % C) for s in (above_strip, below_strip) for d in range(C)]

    barrier = pltpu.get_barrier_semaphore()
    greeted = cell_peers + [p for p, _ in plane_peers] + plane_cross + row_peers
    for peer in greeted:
        pl.semaphore_signal(barrier, 1, device_id=peer, device_id_type=pl.DeviceIdType.MESH)

    sent = []

    def send(group, source, target, peer):
        pltpu.make_async_remote_copy(
            src_ref=source,
            dst_ref=target,
            send_sem=send_sem.at[group],
            recv_sem=recv_sem.at[group],
            device_id=peer,
            device_id_type=pl.DeviceIdType.MESH,
        ).start()

    def arrived(group, span):
        sent.append((group, span))
        pltpu.make_async_copy(span, span, recv_sem.at[group]).wait()

    loads = [
        pltpu.make_async_copy(source, target, load_sem.at[i])
        for i, (source, target) in enumerate(
            (
                (rows_hbm, rows_ref),
                (cols_hbm, cols_ref),
                (pinw_hbm, pinw_ref),
                (fracs_hbm, fracs_ref),
                (cap_hbm, cap_ref),
                (blk_hbm, blk_ref),
                (rowb_hbm, rowb_ref),
                (colb_hbm.at[plane], colb_ref),
            )
        )
    ]
    for load in loads:
        load.start()
    for load in loads:
        load.wait()

    chunks = rows_ref.shape[0]
    bins = bin_sums.shape[0]

    def pins_of(i):
        span = pl.ds(pl.multiple_of(128 * i, 128), 128)
        down, across = fracs_ref[0:1, span], fracs_ref[1:2, span]
        column = cols_ref[pl.ds(i, 1), :]
        tile = lax.shift_right_logical(column, 7)
        return down, across, tile * RD + rows_ref[pl.ds(i, 1), :], column - tile * 128

    def rounded(values):
        return values.astype(bf16).astype(f32)

    def add_pins(i, total):
        down, across, index, lane = pins_of(i)
        heavy = pinw_ref[pl.ds(i, 1), :]
        where_down = table(index, rounded(heavy * (1.0 - down)), rounded(heavy * down), bins)
        where_across = table(lane, rounded(1.0 - across), rounded(across), 136)
        return total + lax.dot_general(
            where_down.astype(bf16),
            where_across.astype(bf16),
            (((1,), (1,)), ((), ())),
            preferred_element_type=f32,
        )

    total = lax.fori_loop(0, chunks, add_pins, jnp.zeros((bins, 136), f32), unroll=4)
    spot = lax.broadcasted_iota(jnp.int32, (bins, 128), 1)
    past = jnp.where(spot == 0, total[:, 128:129], 0.0)
    bin_sums[...] = total[:, :128] + pltpu.roll(past, RD, 0)
    for c in range(C):
        for n in range(NC // 128):
            tile = c * (NC // 128) + n
            part_ref[c, :, 128 * n : 128 * (n + 1)] = bin_sums[RD * tile : RD * (tile + 1), :]

    weights = cap_ref[...].astype(f32) * (1.0 - blk_ref[...])
    whole = jnp.round(weights * w_steps).astype(jnp.int32).astype(jnp.int16)
    w_send[0] = whole[:, :HC]
    w_send[1] = whole[:, cut:]
    w_plane[place] = w_send[half]
    wedge_send[0] = weights[:1]
    wedge_send[1] = weights[RD - 1 :]
    for c in range(C):
        edge_part[0, c] = part_ref[c, :1]
        edge_part[1, c] = part_ref[c, RD - 1 :]
    pl.semaphore_wait(barrier, len(greeted))

    for d in range(C):
        other = (cell + d) % C
        send(1, edge_part.at[0, other], edge_recv.at[1, cell], at(above_strip, other))
        send(1, edge_part.at[1, other], edge_recv.at[0, cell], at(below_strip, other))
    send(2, wedge_send.at[0], wedge_recv.at[1], at(above_strip, cell))
    send(2, wedge_send.at[1], wedge_recv.at[0], at(below_strip, cell))
    for d in range(1, C):
        other = (cell + d) % C
        send(0, part_ref.at[other], part_recv.at[C - 1 - d], at(strip, other))
    for peer, other_half in plane_peers:
        send(3, w_send.at[other_half], w_plane.at[place], peer)

    for n in range(rowb_ref.shape[0]):
        high, low = exact_parts(rowb_ref[n])
        rowb_parts[n] = jnp.concatenate([high, high, low], axis=1)
    high, low = exact_parts(colb_ref[...])
    colb_parts[...] = jnp.concatenate([high, high, low], axis=1)

    end = lax.broadcasted_iota(jnp.int32, (RD, HC), 1)

    def along_inside(values):
        left = pltpu.roll(values, 1, 1)
        right = pltpu.roll(values, NC - 1, 1)
        spot = lax.broadcasted_iota(jnp.int32, values.shape, 1)
        left = jnp.where(spot == 0, jnp.where(first_cell, values, 0.0), left)
        right = jnp.where(spot == NC - 1, jnp.where(last_cell, values, 0.0), right)
        return 2.0 * values - left - right

    weights_two = jnp.concatenate([weights, weights], axis=0)
    spot = lax.broadcasted_iota(jnp.int32, (2 * RD, NC), 1)
    row = lax.broadcasted_iota(jnp.int32, (2 * RD, NC), 0)
    unit = jnp.where(spot == jnp.where(row < RD, 0, NC - 1), coupling, 0.0)
    pulse = row_product(unit, rowb_parts)
    pulses = [pulse]
    for _ in range(SWEEPS - 1):
        back = weights_two * pulse + coupling * along_inside(pulse)
        pulse = pulse - row_product(back, rowb_parts)
        pulses.append(pulse)

    arrived(1, edge_recv)
    arrived(2, wedge_recv)
    arrived(0, part_recv.at[0 : C - 1])
    density = part_ref[cell]
    for d in range(C - 1):
        density = density + part_recv[d]
    current = density / weights
    row_above = edge_recv[0, 0]
    row_below = edge_recv[1, 0]
    for c in range(1, C):
        row_above = row_above + edge_recv[0, c]
        row_below = row_below + edge_recv[1, c]
    row_above = row_above / wedge_recv[0]
    row_below = row_below / wedge_recv[1]
    row_above = jnp.where(strip == 0, current[:1], row_above)
    row_below = jnp.where(strip == strips - 1, current[RD - 1 :], row_below)

    def frame(pair):
        base = pl.multiple_of(RD * 2 * pair, 2 * RD)
        inner = padded[pl.ds(base + 8, 2 * RD), :]
        over = padded[pl.ds(base + 7, 1), :]
        under = padded[pl.ds(base + 8 + 2 * RD, 1), :]
        fill = jnp.zeros((6 - RD, HC), f32)
        upper = jnp.concatenate([over, inner[: RD + 1], fill], axis=0)
        lower = jnp.concatenate([inner[RD - 1 :], under, fill], axis=0)
        return jnp.where(strip_side == 0, upper, lower)

    def frames():
        return frame(place // 2), frame(place // 2 + 1 - 2 * half)

    small = lax.broadcasted_iota(jnp.int32, (RD, 128), 1)

    def clamp_rows(values):
        shape = values.shape
        spot = lax.broadcasted_iota(jnp.int32, shape, 0)
        up = pltpu.roll(values, 1, 0)
        down = pltpu.roll(values, shape[0] - 1, 0)
        up = jnp.where(spot == 0, jnp.where(first_plane, values, 0.0), up)
        down = jnp.where(spot == shape[0] - 1, jnp.where(last_plane, values, 0.0), down)
        return 2.0 * values - up - down

    for step in range(STEPS):
        up = jnp.concatenate([row_above, current[: RD - 1]], axis=0)
        down = jnp.concatenate([current[1:], row_below], axis=0)
        source = weights * current - coupling * (2.0 * current - up - down)
        iterate = current
        levels = [iterate]
        for _ in range(SWEEPS):
            left_over = source - (weights * iterate + coupling * along_inside(iterate))
            iterate = iterate + row_product(left_over, rowb_parts)
            levels.append(iterate)
        for side, column in ((0, 0), (1, NC - 1)):
            message = jnp.zeros((RD, 128), f32)
            for j in range(SWEEPS + 1):
                message = jnp.where(small == j, levels[j][:, column : column + 1], message)
            for m in range(SWEEPS):
                mine = pulses[m][side * RD : (side + 1) * RD, column : column + 1]
                message = jnp.where(small == SWEEPS + 1 + m, mine, message)
            rim_send[step, side] = message
        group = 4 + 4 * step
        send(group, rim_send.at[step, 0], rim_recv.at[step, 1], at(strip, (cell + C - 1) % C))
        send(group, rim_send.at[step, 1], rim_recv.at[step, 0], at(strip, (cell + 1) % C))

        arrived(group, rim_recv.at[step])
        edges = []
        for side in range(2):
            own = [rim_send[step, side][:, i : i + 1] for i in range(2 * SWEEPS + 1)]
            far = [rim_recv[step, side][:, i : i + 1] for i in range(2 * SWEEPS + 1)]
            mine, theirs = [], []
            for j in range(SWEEPS + 1):
                a, b = own[j], far[j]
                for i in range(j):
                    a = a + own[SWEEPS + j - i] * theirs[i]
                    b = b + far[SWEEPS + j - i] * mine[i]
                mine.append(a)
                theirs.append(b)
            edges.append(theirs)
        left_in = [jnp.where(first_cell, 0.0, e) for e in edges[0]]
        right_in = [jnp.where(last_cell, 0.0, e) for e in edges[1]]
        for i in range(SWEEPS):
            iterate = iterate + (
                pulses[SWEEPS - 1 - i][:RD] * left_in[i] + pulses[SWEEPS - 1 - i][RD:] * right_in[i]
            )
        halo_left = jnp.where(first_cell, iterate[:, :1], left_in[SWEEPS])
        halo_right = jnp.where(last_cell, iterate[:, NC - 1 :], right_in[SWEEPS])
        field_send[step, 0] = jnp.where(end == HC - 1, halo_left, iterate[:, :HC])
        field_send[step, 1] = jnp.where(end == 0, halo_right, iterate[:, cut:])
        field_plane[step, place] = field_send[step, half]
        for peer, other_half in plane_peers:
            send(group + 2, field_send.at[step, other_half], field_plane.at[step, place], peer)
        if step == 0:
            arrived(3, w_plane.at[0 : Q - 1])
            for i in range(Q):
                stepped = w_plane[i].astype(jnp.int32).astype(f32)
                w_block[RD * i : RD * (i + 1), :] = stepped * (1.0 / w_steps)
            padded[0:8, :] = jnp.zeros((8, HC), f32)
            padded[BL + 8 :, :] = jnp.zeros((8, HC), f32)
            for side, column in ((0, 0), (1, BL - 1)):
                answer = coupling * jnp.broadcast_to(
                    colb_ref[:, column : column + 1], (BL, HC)
                )
                for m in range(SWEEPS):
                    if m > 0:
                        back = w_block[...] * answer + coupling * clamp_rows(answer)
                        answer = answer - col_product(colb_parts, back)
                    padded[8 : BL + 8, :] = answer
                    own, other = frames()
                    answer_near[half, m, side] = own
                    answer_send[m, side] = other
                    still_send[m, side, 0:1, :] = answer[:1]
                    still_send[m, side, 1:2, :] = answer[BL - 1 :]
            still_recv[slot] = still_send[...]
        else:

            def prepare(i, carry):
                down, across, index, lane = pins_of(i)
                look[i] = table(index, rounded(1.0 - down), rounded(down), 128).astype(bf16)
                spread[i] = table(lane, rounded(1.0 - across), rounded(across), 136)
                return carry

            lax.fori_loop(0, chunks, prepare, 0, unroll=2)

        arrived(group + 2, field_plane.at[step, 0 : Q - 1])
        if step == 0:
            send(9, answer_send, answer_near.at[half], partner)
            for peer in plane_cross:
                send(5, still_send, still_recv.at[slot], peer)
        for i in range(Q):
            field_block[RD * i : RD * (i + 1), :] = field_plane[step, i]

        start = field_block[...]
        beside = pltpu.roll(start, 1, 1) + pltpu.roll(start, HC - 1, 1)
        middle = w_block[...] * start - coupling * (2.0 * start - beside)
        iterate = start
        for j in range(SWEEPS + 1):
            if j > 0:
                left_over = middle - (w_block[...] * iterate + coupling * clamp_rows(iterate))
                iterate = iterate + col_product(colb_parts, left_over)
            tops_send[step, j, 0:1, :] = iterate[:1]
            tops_send[step, j, 1:2, :] = iterate[BL - 1 :]
        for peer in plane_cross:
            send(group + 3, tops_send.at[step], tops_recv.at[step, slot], peer)
        padded[8 : BL + 8, :] = iterate
        own, other = frames()
        near_send[step] = other
        near[step, half] = own
        send(13 + step, near_send.at[step], near.at[step, half], partner)
        tops_recv[step, slot] = tops_send[step]

        if step == 0:
            arrived(5, still_recv.at[0 : 2 * K - 1])
            arrived(9, answer_near.at[0])
            for k in range(K):
                for m in range(SWEEPS):
                    for side in range(2):
                        for h in range(2):
                            still_all[h, m, side, 2 * k : 2 * k + 2, :] = still_recv[
                                2 * k + h, m, side
                            ]
        arrived(group + 3, tops_recv.at[step, 0 : 2 * K - 1])
        for k in range(K):
            for j in range(SWEEPS + 1):
                for h in range(2):
                    tops_all[h, j, 2 * k : 2 * k + 2, :] = tops_recv[step, 2 * k + h, j]
        arrived(13 + step, near.at[step, 0])
        spot = lax.broadcasted_iota(jnp.int32, (2 * K, HC), 0)
        even = spot % 2 == 0
        mine = pl.ds(2 * plane, 1)
        halves = []
        for h in range(2):
            from_above, from_below = [], []
            for j in range(SWEEPS + 1):
                value = tops_all[h, j]
                for i in range(j):
                    value = value + still_all[h, j - i - 1, 0] * from_above[i]
                    value = value + still_all[h, j - i - 1, 1] * from_below[i]
                over = jnp.where(even, pltpu.roll(value, 1, 0), pltpu.roll(value, 2, 0))
                under = jnp.where(
                    even, pltpu.roll(value, 2 * K - 2, 0), pltpu.roll(value, 2 * K - 1, 0)
                )
                from_above.append(jnp.where(spot < 2, 0.0, over))
                from_below.append(jnp.where(spot >= 2 * K - 2, 0.0, under))
                inflow[h, j, 0] = from_above[j]
                inflow[h, j, 1] = from_below[j]
            nearby = near[step, h]
            for i in range(SWEEPS):
                m = SWEEPS - 1 - i
                nearby = nearby + (
                    answer_near[h, m, 0] * inflow[h, i, 0, mine, :]
                    + answer_near[h, m, 1] * inflow[h, i, 1, mine, :]
                )
            above, below = nearby[:1], nearby[1 + RD : 2 + RD]
            above = jnp.where(place == 0, inflow[h, SWEEPS, 0, mine, :], above)
            below = jnp.where(place == Q - 1, inflow[h, SWEEPS, 1, mine, :], below)
            halves.append((above, nearby[1 : 1 + RD], below))

        def joined(first, second):
            over = HC - cut
            lanes = lax.broadcasted_iota(jnp.int32, (first.shape[0], over), 1)
            both = jnp.where(lanes < over // 2, first[:, cut:], second[:, :over])
            return jnp.concatenate([first[:, :cut], both, second[:, over:]], axis=1)

        row_above, current, row_below = (joined(a, b) for a, b in zip(*halves))
        row_above = jnp.where(strip == 0, current[:1], row_above)
        row_below = jnp.where(strip == strips - 1, current[RD - 1 :], row_below)

    density_ref[...] = current
    last_send[0:1, :] = row_above
    last_send[1 : 1 + RD, :] = current
    last_send[1 + RD : 2 + RD, :] = row_below
    last_send[2 + RD : 8, :] = jnp.zeros((6 - RD, NC), f32)
    last_recv[cell] = last_send[...]
    for peer in cell_peers:
        send(12, last_send, last_recv.at[cell], peer)
    arrived(12, last_recv.at[0 : C - 1])
    field = jnp.concatenate([last_recv[c] for c in range(C)], axis=1)
    centre = field[1 : 1 + RD]
    spot = lax.broadcasted_iota(jnp.int32, (RD, C * NC), 1)
    left = jnp.where(spot == 0, centre, pltpu.roll(centre, 1, 1))
    right = jnp.where(spot == C * NC - 1, centre, pltpu.roll(centre, C * NC - 1, 1))
    scale = jnp.maximum(centre, floor_level)
    velocity_y = -(0.5 * (field[2 : 2 + RD] - field[:RD])) / scale
    velocity_x = -(0.5 * (right - left)) / scale
    tables = []
    for i, velocity in enumerate((velocity_y, velocity_x)):
        vel_bins[i, bins:, :] = jnp.zeros((128 - bins, 128), f32)
        for n in range(bins // RD):
            vel_bins[i, RD * n : RD * (n + 1), :] = velocity[:, 128 * n : 128 * (n + 1)]
        turned = jnp.transpose(vel_bins[i])
        past = jnp.broadcast_to(pltpu.roll(turned[:8], 128 - RD, 1)[:1], (8, 128))
        tables += [turned.astype(bf16), past.astype(bf16)]
    tables = jnp.concatenate(tables, axis=0)

    def sample(i, carry):
        sampled = jnp.dot(tables, look[i], preferred_element_type=f32)
        across = spread[i]
        out_y = jnp.sum(sampled[:136] * across, axis=0, keepdims=True)
        out_x = jnp.sum(sampled[136:] * across, axis=0, keepdims=True)
        span = pl.ds(pl.multiple_of(128 * i, 128), 128)
        pinv_ref[:, span] = jnp.concatenate([out_y, out_x], axis=0)
        return carry

    lax.fori_loop(0, chunks, sample, 0, unroll=4)
    for group, span in sent:
        pltpu.make_async_copy(span, span, send_sem.at[group]).wait()


def diffuse(pin_rows, pin_cols, pin_fracs, pin_weights, capacity, blockage, row_blocks, col_blocks):
    pins = pin_rows.shape[0]
    chunks = pins // 128
    strips = lax.axis_size("strip")
    C = lax.axis_size("cells")
    RD, NC = capacity.shape
    NB = row_blocks.shape[0]
    K, BL = col_blocks.shape[:2]
    Q = strips // K
    HC = 128 * ((NB + 1) // 2)
    vmem = pl.BlockSpec(memory_space=pltpu.VMEM)
    bins = RD * C * NC // 128
    shapes = [
        ((chunks, 128), jnp.int32),
        ((chunks, 128), jnp.int32),
        ((chunks, 128), f32),
        ((2, pins), f32),
        ((RD, NC), jnp.int32),
        ((RD, NC), f32),
        ((NB, 128, 128), f32),
        ((BL, BL), f32),
        ((bins, 128), f32),
        ((C, RD, NC), f32),
        ((chunks, 128, 128), bf16),
        ((chunks, 136, 128), f32),
        ((2, 128, 128), f32),
        ((2, C, 1, NC), f32),
        ((C, RD, NC), f32),
        ((2, C, 1, NC), f32),
        ((2, 1, NC), f32),
        ((2, 1, NC), f32),
        ((2, RD, HC), jnp.int16),
        ((Q, RD, HC), jnp.int16),
        ((BL, HC), f32),
        ((NB, 128, 384), bf16),
        ((BL, 3 * BL), bf16),
        ((STEPS, 2, RD, 128), f32),
        ((STEPS, 2, RD, 128), f32),
        ((STEPS, 2, RD, HC), f32),
        ((STEPS, Q, RD, HC), f32),
        ((BL, HC), f32),
        ((BL + 16, HC), f32),
        ((SWEEPS, 2, 8, HC), f32),
        ((2, SWEEPS, 2, 8, HC), f32),
        ((STEPS, 8, HC), f32),
        ((STEPS, 2, 8, HC), f32),
        ((SWEEPS, 2, 2, HC), f32),
        ((2 * K, SWEEPS, 2, 2, HC), f32),
        ((2, SWEEPS, 2, 2 * K, HC), f32),
        ((STEPS, SWEEPS + 1, 2, HC), f32),
        ((STEPS, 2 * K, SWEEPS + 1, 2, HC), f32),
        ((2, SWEEPS + 1, 2 * K, HC), f32),
        ((2, SWEEPS + 1, 2, 2 * K, HC), f32),
        ((8, NC), f32),
        ((C, 8, NC), f32),
    ]
    results = pl.pallas_call(
        functools.partial(adi_kernel, (K, Q, C, RD, NC, BL)),
        out_shape=(
            jax.ShapeDtypeStruct((RD, NC), f32),
            jax.ShapeDtypeStruct((2, pins), f32),
        ),
        in_specs=[pl.BlockSpec(memory_space=pltpu.HBM)] * 8,
        out_specs=(vmem, vmem),
        scratch_shapes=[pltpu.VMEM(shape, dtype) for shape, dtype in shapes]
        + [pltpu.SemaphoreType.DMA((n,)) for n in (15, 15, 8)],
        compiler_params=pltpu.CompilerParams(
            collective_id=0, has_side_effects=True
        ),
        name="adi",
    )(
        pin_rows.reshape(chunks, 128),
        pin_cols.reshape(chunks, 128),
        pin_fracs,
        pin_weights.reshape(chunks, 128),
        capacity,
        blockage,
        row_blocks,
        col_blocks,
    )
    return pl.pallas_call(
        hand_over,
        out_shape=[jax.ShapeDtypeStruct(r.shape, r.dtype) for r in results],
        in_specs=[vmem] * 2,
        out_specs=[vmem] * 2,
        name="hand_over",
    )(*results)


def hand_over(first, second, first_out, second_out):
    first_out[...] = first[...]
    second_out[...] = second[...]


def solution(mesh):
    placed = (
        P(("strip", "cells")),
        P(("strip", "cells")),
        P(None, ("strip", "cells")),
        P(("strip", "cells")),
        P("strip", "cells"),
        P("strip", "cells"),
        P("cells", None, None),
        P(),
    )
    return jax.shard_map(
        diffuse,
        mesh=mesh,
        in_specs=placed,
        out_specs=(P("strip", "cells"), P(None, ("strip", "cells"))),
        check_vma=False,
    )
```

```python
import functools

import jax
import jax.numpy as jnp
from jax import lax
from jax.experimental import pallas as pl
from jax.experimental.pallas import tpu as pltpu
from jax.sharding import PartitionSpec as P

SWEEPS = 3
STEPS = 2
coupling = 2.0
floor_level = 0.5
w_steps = 8191.0
f32 = jnp.float32
bf16 = jnp.bfloat16


def exact_parts(values):
    high = values.astype(bf16)
    return high, (values - high.astype(f32)).astype(bf16)


def row_product(values, blocks_ref):
    pieces = []
    for n in range(blocks_ref.shape[0]):
        high, low = exact_parts(values[:, 128 * n : 128 * (n + 1)])
        pieces.append(
            lax.dot_general(
                jnp.concatenate([high, low, high], axis=1),
                blocks_ref[n],
                (((1,), (1,)), ((), ())),
                preferred_element_type=f32,
            )
        )
    return jnp.concatenate(pieces, axis=1)


def col_product(matrix_ref, values):
    high, low = exact_parts(values)
    parts = jnp.concatenate([high, low, high], axis=0)
    return jnp.dot(matrix_ref[...], parts, preferred_element_type=f32)


def table(index, first, second, count):
    spot = lax.broadcasted_iota(jnp.int32, (count, index.shape[1]), 0)
    return jnp.where(spot == index, first, jnp.where(spot == index + 1, second, 0.0))


def adi_kernel(
    sizes,
    rows_hbm,
    cols_hbm,
    fracs_hbm,
    pinw_hbm,
    cap_hbm,
    blk_hbm,
    rowb_hbm,
    colb_hbm,
    density_ref,
    pinv_ref,
    rows_ref,
    cols_ref,
    pinw_ref,
    fracs_ref,
    cap_ref,
    blk_ref,
    rowb_ref,
    colb_ref,
    bin_sums,
    part_ref,
    look,
    spread,
    vel_bins,
    edge_part,
    part_recv,
    edge_recv,
    wedge_send,
    wedge_recv,
    w_send,
    w_plane,
    w_block,
    rowb_parts,
    colb_parts,
    rim_send,
    rim_recv,
    field_send,
    field_plane,
    field_block,
    padded,
    answer_send,
    answer_near,
    near_send,
    near,
    still_send,
    still_recv,
    still_all,
    tops_send,
    tops_recv,
    tops_all,
    inflow,
    last_send,
    last_recv,
    send_sem,
    recv_sem,
    load_sem,
):
    K, Q, C, RD, NC, BL = sizes
    strips = K * Q
    HC = w_send.shape[2]
    cut = NC - HC
    strip = lax.axis_index("strip")
    cell = lax.axis_index("cells")
    plane = strip // Q
    place = strip % Q
    depth = Q // 2
    half = (place // 2) % 2
    strip_side = place % 2
    first_cell, last_cell = cell == 0, cell == C - 1
    first_plane, last_plane = plane == 0, plane == K - 1

    def at(strip_id, cell_id):
        return (strip_id, cell_id)

    cell_peers = [at(strip, (cell + d) % C) for d in range(1, C)]
    above_strip, below_strip = (strip + strips - 1) % strips, (strip + 1) % strips
    offsets = [(dz, dy) for dz in range(depth) for dy in range(2) if (dz, dy) != (0, 0)]
    offsets.sort(key=lambda o: -(min(o[0], depth - o[0]) + 2 * o[1]))
    plane_peers = []
    for dz, dy in offsets:
        other = ((place // 2 + dz) % depth) * 2 + (place % 2 + dy) % 2
        plane_peers.append((at(plane * Q + other, cell), (half + dz) % 2))
    partner = at(strip + 2 - 4 * half, cell)
    shifts = [(dk, dz) for dk in range(K) for dz in range(2) if (dk, dz) != (0, 0)]
    shifts.sort(key=lambda o: -(min(o[0], K - o[0]) + o[1]))
    plane_cross = [
        at(((plane + dk) % K) * Q + place + dz * (2 - 4 * half), cell) for dk, dz in shifts
    ]
    slot = 2 * plane + half
    row_peers = [at(s, (cell + d) % C) for s in (above_strip, below_strip) for d in range(C)]

    barrier = pltpu.get_barrier_semaphore()
    greeted = cell_peers + [p for p, _ in plane_peers] + plane_cross + row_peers
    for peer in greeted:
        pl.semaphore_signal(barrier, 1, device_id=peer, device_id_type=pl.DeviceIdType.MESH)

    sent = []

    def send(group, source, target, peer):
        pltpu.make_async_remote_copy(
            src_ref=source,
            dst_ref=target,
            send_sem=send_sem.at[group],
            recv_sem=recv_sem.at[group],
            device_id=peer,
            device_id_type=pl.DeviceIdType.MESH,
        ).start()

    def arrived(group, span):
        sent.append((group, span))
        pltpu.make_async_copy(span, span, recv_sem.at[group]).wait()

    loads = [
        pltpu.make_async_copy(source, target, load_sem.at[i])
        for i, (source, target) in enumerate(
            (
                (rows_hbm, rows_ref),
                (cols_hbm, cols_ref),
                (pinw_hbm, pinw_ref),
                (fracs_hbm, fracs_ref),
                (cap_hbm, cap_ref),
                (blk_hbm, blk_ref),
                (rowb_hbm, rowb_ref),
                (colb_hbm.at[plane], colb_ref),
            )
        )
    ]
    for load in loads:
        load.start()
    for load in loads:
        load.wait()

    chunks = rows_ref.shape[0]
    bins = bin_sums.shape[0]

    def pins_of(i):
        span = pl.ds(pl.multiple_of(128 * i, 128), 128)
        down, across = fracs_ref[0:1, span], fracs_ref[1:2, span]
        column = cols_ref[pl.ds(i, 1), :]
        tile = lax.shift_right_logical(column, 7)
        return down, across, tile * RD + rows_ref[pl.ds(i, 1), :], column - tile * 128

    def rounded(values):
        return values.astype(bf16).astype(f32)

    def add_pins(i, total):
        down, across, index, lane = pins_of(i)
        heavy = pinw_ref[pl.ds(i, 1), :]
        where_down = table(index, rounded(heavy * (1.0 - down)), rounded(heavy * down), bins)
        where_across = table(lane, rounded(1.0 - across), rounded(across), 136)
        return total + lax.dot_general(
            where_down.astype(bf16),
            where_across.astype(bf16),
            (((1,), (1,)), ((), ())),
            preferred_element_type=f32,
        )

    total = lax.fori_loop(0, chunks, add_pins, jnp.zeros((bins, 136), f32), unroll=4)
    spot = lax.broadcasted_iota(jnp.int32, (bins, 128), 1)
    past = jnp.where(spot == 0, total[:, 128:129], 0.0)
    bin_sums[...] = total[:, :128] + pltpu.roll(past, RD, 0)
    for c in range(C):
        for n in range(NC // 128):
            tile = c * (NC // 128) + n
            part_ref[c, :, 128 * n : 128 * (n + 1)] = bin_sums[RD * tile : RD * (tile + 1), :]

    weights = cap_ref[...].astype(f32) * (1.0 - blk_ref[...])
    whole = jnp.round(weights * w_steps).astype(jnp.int32).astype(jnp.int16)
    w_send[0] = whole[:, :HC]
    w_send[1] = whole[:, cut:]
    w_plane[place] = w_send[half]
    wedge_send[0] = weights[:1]
    wedge_send[1] = weights[RD - 1 :]
    for c in range(C):
        edge_part[0, c] = part_ref[c, :1]
        edge_part[1, c] = part_ref[c, RD - 1 :]
    pl.semaphore_wait(barrier, len(greeted))

    for d in range(C):
        other = (cell + d) % C
        send(1, edge_part.at[0, other], edge_recv.at[1, cell], at(above_strip, other))
        send(1, edge_part.at[1, other], edge_recv.at[0, cell], at(below_strip, other))
    send(2, wedge_send.at[0], wedge_recv.at[1], at(above_strip, cell))
    send(2, wedge_send.at[1], wedge_recv.at[0], at(below_strip, cell))
    for d in range(1, C):
        other = (cell + d) % C
        send(0, part_ref.at[other], part_recv.at[C - 1 - d], at(strip, other))
    for peer, other_half in plane_peers:
        send(3, w_send.at[other_half], w_plane.at[place], peer)

    for n in range(rowb_ref.shape[0]):
        high, low = exact_parts(rowb_ref[n])
        rowb_parts[n] = jnp.concatenate([high, high, low], axis=1)
    high, low = exact_parts(colb_ref[...])
    colb_parts[...] = jnp.concatenate([high, high, low], axis=1)

    end = lax.broadcasted_iota(jnp.int32, (RD, HC), 1)

    def along_inside(values):
        left = pltpu.roll(values, 1, 1)
        right = pltpu.roll(values, NC - 1, 1)
        spot = lax.broadcasted_iota(jnp.int32, values.shape, 1)
        left = jnp.where(spot == 0, jnp.where(first_cell, values, 0.0), left)
        right = jnp.where(spot == NC - 1, jnp.where(last_cell, values, 0.0), right)
        return 2.0 * values - left - right

    weights_two = jnp.concatenate([weights, weights], axis=0)
    spot = lax.broadcasted_iota(jnp.int32, (2 * RD, NC), 1)
    row = lax.broadcasted_iota(jnp.int32, (2 * RD, NC), 0)
    unit = jnp.where(spot == jnp.where(row < RD, 0, NC - 1), coupling, 0.0)
    pulse = row_product(unit, rowb_parts)
    pulses = [pulse]
    for _ in range(SWEEPS - 1):
        back = weights_two * pulse + coupling * along_inside(pulse)
        pulse = pulse - row_product(back, rowb_parts)
        pulses.append(pulse)

    arrived(1, edge_recv)
    arrived(2, wedge_recv)
    arrived(0, part_recv.at[0 : C - 1])
    density = part_ref[cell]
    for d in range(C - 1):
        density = density + part_recv[d]
    current = density / weights
    row_above = edge_recv[0, 0]
    row_below = edge_recv[1, 0]
    for c in range(1, C):
        row_above = row_above + edge_recv[0, c]
        row_below = row_below + edge_recv[1, c]
    row_above = row_above / wedge_recv[0]
    row_below = row_below / wedge_recv[1]
    row_above = jnp.where(strip == 0, current[:1], row_above)
    row_below = jnp.where(strip == strips - 1, current[RD - 1 :], row_below)

    def frame(pair):
        base = pl.multiple_of(RD * 2 * pair, 2 * RD)
        inner = padded[pl.ds(base + 8, 2 * RD), :]
        over = padded[pl.ds(base + 7, 1), :]
        under = padded[pl.ds(base + 8 + 2 * RD, 1), :]
        fill = jnp.zeros((6 - RD, HC), f32)
        upper = jnp.concatenate([over, inner[: RD + 1], fill], axis=0)
        lower = jnp.concatenate([inner[RD - 1 :], under, fill], axis=0)
        return jnp.where(strip_side == 0, upper, lower)

    def frames():
        return frame(place // 2), frame(place // 2 + 1 - 2 * half)

    small = lax.broadcasted_iota(jnp.int32, (RD, 128), 1)

    def clamp_rows(values):
        shape = values.shape
        spot = lax.broadcasted_iota(jnp.int32, shape, 0)
        up = pltpu.roll(values, 1, 0)
        down = pltpu.roll(values, shape[0] - 1, 0)
        up = jnp.where(spot == 0, jnp.where(first_plane, values, 0.0), up)
        down = jnp.where(spot == shape[0] - 1, jnp.where(last_plane, values, 0.0), down)
        return 2.0 * values - up - down

    for step in range(STEPS):
        up = jnp.concatenate([row_above, current[: RD - 1]], axis=0)
        down = jnp.concatenate([current[1:], row_below], axis=0)
        source = weights * current - coupling * (2.0 * current - up - down)
        iterate = current
        levels = [iterate]
        for _ in range(SWEEPS):
            left_over = source - (weights * iterate + coupling * along_inside(iterate))
            iterate = iterate + row_product(left_over, rowb_parts)
            levels.append(iterate)
        for side, column in ((0, 0), (1, NC - 1)):
            message = jnp.zeros((RD, 128), f32)
            for j in range(SWEEPS + 1):
                message = jnp.where(small == j, levels[j][:, column : column + 1], message)
            for m in range(SWEEPS):
                mine = pulses[m][side * RD : (side + 1) * RD, column : column + 1]
                message = jnp.where(small == SWEEPS + 1 + m, mine, message)
            rim_send[step, side] = message
        group = 4 + 4 * step
        send(group, rim_send.at[step, 0], rim_recv.at[step, 1], at(strip, (cell + C - 1) % C))
        send(group, rim_send.at[step, 1], rim_recv.at[step, 0], at(strip, (cell + 1) % C))

        arrived(group, rim_recv.at[step])
        edges = []
        for side in range(2):
            own = [rim_send[step, side][:, i : i + 1] for i in range(2 * SWEEPS + 1)]
            far = [rim_recv[step, side][:, i : i + 1] for i in range(2 * SWEEPS + 1)]
            mine, theirs = [], []
            for j in range(SWEEPS + 1):
                a, b = own[j], far[j]
                for i in range(j):
                    a = a + own[SWEEPS + j - i] * theirs[i]
                    b = b + far[SWEEPS + j - i] * mine[i]
                mine.append(a)
                theirs.append(b)
            edges.append(theirs)
        left_in = [jnp.where(first_cell, 0.0, e) for e in edges[0]]
        right_in = [jnp.where(last_cell, 0.0, e) for e in edges[1]]
        for i in range(SWEEPS):
            iterate = iterate + (
                pulses[SWEEPS - 1 - i][:RD] * left_in[i] + pulses[SWEEPS - 1 - i][RD:] * right_in[i]
            )
        halo_left = jnp.where(first_cell, iterate[:, :1], left_in[SWEEPS])
        halo_right = jnp.where(last_cell, iterate[:, NC - 1 :], right_in[SWEEPS])
        field_send[step, 0] = jnp.where(end == HC - 1, halo_left, iterate[:, :HC])
        field_send[step, 1] = jnp.where(end == 0, halo_right, iterate[:, cut:])
        field_plane[step, place] = field_send[step, half]
        for peer, other_half in plane_peers:
            send(group + 2, field_send.at[step, other_half], field_plane.at[step, place], peer)
        if step == 0:
            arrived(3, w_plane.at[0 : Q - 1])
            for i in range(Q):
                stepped = w_plane[i].astype(jnp.int32).astype(f32)
                w_block[RD * i : RD * (i + 1), :] = stepped * (1.0 / w_steps)
            padded[0:8, :] = jnp.zeros((8, HC), f32)
            padded[BL + 8 :, :] = jnp.zeros((8, HC), f32)
            for side, column in ((0, 0), (1, BL - 1)):
                answer = coupling * jnp.broadcast_to(
                    colb_ref[:, column : column + 1], (BL, HC)
                )
                for m in range(SWEEPS):
                    if m > 0:
                        back = w_block[...] * answer + coupling * clamp_rows(answer)
                        answer = answer - col_product(colb_parts, back)
                    padded[8 : BL + 8, :] = answer
                    own, other = frames()
                    answer_near[half, m, side] = own
                    answer_send[m, side] = other
                    still_send[m, side, 0:1, :] = answer[:1]
                    still_send[m, side, 1:2, :] = answer[BL - 1 :]
            still_recv[slot] = still_send[...]
            for peer in plane_cross:
                send(5, still_send, still_recv.at[slot], peer)
            send(9, answer_send, answer_near.at[half], partner)
        else:

            def prepare(i, carry):
                for k in range(2):
                    down, across, index, lane = pins_of(2 * i + k)
                    part = slice(128 * k, 128 * (k + 1))
                    nearer, farther = rounded(1.0 - down), rounded(down)
                    look[i, :, part] = table(index, nearer, farther, 128).astype(bf16)
                    spread[i, :, part] = table(lane, rounded(1.0 - across), rounded(across), 136)
                return carry

            lax.fori_loop(0, chunks // 2, prepare, 0)

        arrived(group + 2, field_plane.at[step, 0 : Q - 1])
        for i in range(Q):
            field_block[RD * i : RD * (i + 1), :] = field_plane[step, i]

        start = field_block[...]
        beside = pltpu.roll(start, 1, 1) + pltpu.roll(start, HC - 1, 1)
        middle = w_block[...] * start - coupling * (2.0 * start - beside)
        iterate = start
        for j in range(SWEEPS + 1):
            if j > 0:
                left_over = middle - (w_block[...] * iterate + coupling * clamp_rows(iterate))
                iterate = iterate + col_product(colb_parts, left_over)
            tops_send[step, j, 0:1, :] = iterate[:1]
            tops_send[step, j, 1:2, :] = iterate[BL - 1 :]
        for peer in plane_cross:
            send(group + 3, tops_send.at[step], tops_recv.at[step, slot], peer)
        padded[8 : BL + 8, :] = iterate
        own, other = frames()
        near_send[step] = other
        near[step, half] = own
        send(13 + step, near_send.at[step], near.at[step, half], partner)
        tops_recv[step, slot] = tops_send[step]

        if step == 0:
            arrived(5, still_recv.at[0 : 2 * K - 1])
            arrived(9, answer_near.at[0])
            for k in range(K):
                for m in range(SWEEPS):
                    for side in range(2):
                        for h in range(2):
                            still_all[h, m, side, 2 * k : 2 * k + 2, :] = still_recv[
                                2 * k + h, m, side
                            ]
        arrived(group + 3, tops_recv.at[step, 0 : 2 * K - 1])
        for k in range(K):
            for j in range(SWEEPS + 1):
                for h in range(2):
                    tops_all[h, j, 2 * k : 2 * k + 2, :] = tops_recv[step, 2 * k + h, j]
        arrived(13 + step, near.at[step, 0])
        spot = lax.broadcasted_iota(jnp.int32, (2 * K, HC), 0)
        even = spot % 2 == 0
        mine = pl.ds(2 * plane, 1)
        halves = []
        for h in range(2):
            from_above, from_below = [], []
            for j in range(SWEEPS + 1):
                value = tops_all[h, j]
                for i in range(j):
                    value = value + still_all[h, j - i - 1, 0] * from_above[i]
                    value = value + still_all[h, j - i - 1, 1] * from_below[i]
                over = jnp.where(even, pltpu.roll(value, 1, 0), pltpu.roll(value, 2, 0))
                under = jnp.where(
                    even, pltpu.roll(value, 2 * K - 2, 0), pltpu.roll(value, 2 * K - 1, 0)
                )
                from_above.append(jnp.where(spot < 2, 0.0, over))
                from_below.append(jnp.where(spot >= 2 * K - 2, 0.0, under))
                inflow[h, j, 0] = from_above[j]
                inflow[h, j, 1] = from_below[j]
            nearby = near[step, h]
            for i in range(SWEEPS):
                m = SWEEPS - 1 - i
                nearby = nearby + (
                    answer_near[h, m, 0] * inflow[h, i, 0, mine, :]
                    + answer_near[h, m, 1] * inflow[h, i, 1, mine, :]
                )
            above, below = nearby[:1], nearby[1 + RD : 2 + RD]
            above = jnp.where(place == 0, inflow[h, SWEEPS, 0, mine, :], above)
            below = jnp.where(place == Q - 1, inflow[h, SWEEPS, 1, mine, :], below)
            halves.append((above, nearby[1 : 1 + RD], below))

        def joined(first, second):
            over = HC - cut
            lanes = lax.broadcasted_iota(jnp.int32, (first.shape[0], over), 1)
            both = jnp.where(lanes < over // 2, first[:, cut:], second[:, :over])
            return jnp.concatenate([first[:, :cut], both, second[:, over:]], axis=1)

        row_above, current, row_below = (joined(a, b) for a, b in zip(*halves))
        row_above = jnp.where(strip == 0, current[:1], row_above)
        row_below = jnp.where(strip == strips - 1, current[RD - 1 :], row_below)

    density_ref[...] = current
    last_send[0:1, :] = row_above
    last_send[1 : 1 + RD, :] = current
    last_send[1 + RD : 2 + RD, :] = row_below
    last_send[2 + RD : 8, :] = jnp.zeros((6 - RD, NC), f32)
    last_recv[cell] = last_send[...]
    for peer in cell_peers:
        send(12, last_send, last_recv.at[cell], peer)
    arrived(12, last_recv.at[0 : C - 1])
    field = jnp.concatenate([last_recv[c] for c in range(C)], axis=1)
    centre = field[1 : 1 + RD]
    spot = lax.broadcasted_iota(jnp.int32, (RD, C * NC), 1)
    left = jnp.where(spot == 0, centre, pltpu.roll(centre, 1, 1))
    right = jnp.where(spot == C * NC - 1, centre, pltpu.roll(centre, C * NC - 1, 1))
    scale = jnp.maximum(centre, floor_level)
    velocity_y = -(0.5 * (field[2 : 2 + RD] - field[:RD])) / scale
    velocity_x = -(0.5 * (right - left)) / scale
    tables = []
    for i, velocity in enumerate((velocity_y, velocity_x)):
        vel_bins[i, bins:, :] = jnp.zeros((128 - bins, 128), f32)
        for n in range(bins // RD):
            vel_bins[i, RD * n : RD * (n + 1), :] = velocity[:, 128 * n : 128 * (n + 1)]
        turned = jnp.transpose(vel_bins[i])
        past = jnp.broadcast_to(pltpu.roll(turned[:8], 128 - RD, 1)[:1], (8, 128))
        tables += [turned.astype(bf16), past.astype(bf16)]
    tables = jnp.concatenate(tables, axis=0)

    def sample(i, carry):
        sampled = jnp.dot(tables, look[i], preferred_element_type=f32)
        across = spread[i]
        out_y = jnp.sum(sampled[:136] * across, axis=0, keepdims=True)
        out_x = jnp.sum(sampled[136:] * across, axis=0, keepdims=True)
        span = pl.ds(pl.multiple_of(256 * i, 256), 256)
        pinv_ref[:, span] = jnp.concatenate([out_y, out_x], axis=0)
        return carry

    lax.fori_loop(0, chunks // 2, sample, 0, unroll=4)
    for group, span in sent:
        pltpu.make_async_copy(span, span, send_sem.at[group]).wait()


def diffuse(pin_rows, pin_cols, pin_fracs, pin_weights, capacity, blockage, row_blocks, col_blocks):
    pins = pin_rows.shape[0]
    chunks = pins // 128
    strips = lax.axis_size("strip")
    C = lax.axis_size("cells")
    RD, NC = capacity.shape
    NB = row_blocks.shape[0]
    K, BL = col_blocks.shape[:2]
    Q = strips // K
    HC = 128 * ((NB + 1) // 2)
    vmem = pl.BlockSpec(memory_space=pltpu.VMEM)
    bins = RD * C * NC // 128
    shapes = [
        ((chunks, 128), jnp.int32),
        ((chunks, 128), jnp.int32),
        ((chunks, 128), f32),
        ((2, pins), f32),
        ((RD, NC), jnp.int32),
        ((RD, NC), f32),
        ((NB, 128, 128), f32),
        ((BL, BL), f32),
        ((bins, 128), f32),
        ((C, RD, NC), f32),
        ((chunks // 2, 128, 256), bf16),
        ((chunks // 2, 136, 256), f32),
        ((2, 128, 128), f32),
        ((2, C, 1, NC), f32),
        ((C, RD, NC), f32),
        ((2, C, 1, NC), f32),
        ((2, 1, NC), f32),
        ((2, 1, NC), f32),
        ((2, RD, HC), jnp.int16),
        ((Q, RD, HC), jnp.int16),
        ((BL, HC), f32),
        ((NB, 128, 384), bf16),
        ((BL, 3 * BL), bf16),
        ((STEPS, 2, RD, 128), f32),
        ((STEPS, 2, RD, 128), f32),
        ((STEPS, 2, RD, HC), f32),
        ((STEPS, Q, RD, HC), f32),
        ((BL, HC), f32),
        ((BL + 16, HC), f32),
        ((SWEEPS, 2, 8, HC), f32),
        ((2, SWEEPS, 2, 8, HC), f32),
        ((STEPS, 8, HC), f32),
        ((STEPS, 2, 8, HC), f32),
        ((SWEEPS, 2, 2, HC), f32),
        ((2 * K, SWEEPS, 2, 2, HC), f32),
        ((2, SWEEPS, 2, 2 * K, HC), f32),
        ((STEPS, SWEEPS + 1, 2, HC), f32),
        ((STEPS, 2 * K, SWEEPS + 1, 2, HC), f32),
        ((2, SWEEPS + 1, 2 * K, HC), f32),
        ((2, SWEEPS + 1, 2, 2 * K, HC), f32),
        ((8, NC), f32),
        ((C, 8, NC), f32),
    ]
    results = pl.pallas_call(
        functools.partial(adi_kernel, (K, Q, C, RD, NC, BL)),
        out_shape=(
            jax.ShapeDtypeStruct((RD, NC), f32),
            jax.ShapeDtypeStruct((2, pins), f32),
        ),
        in_specs=[pl.BlockSpec(memory_space=pltpu.HBM)] * 8,
        out_specs=(vmem, vmem),
        scratch_shapes=[pltpu.VMEM(shape, dtype) for shape, dtype in shapes]
        + [pltpu.SemaphoreType.DMA((n,)) for n in (15, 15, 8)],
        compiler_params=pltpu.CompilerParams(collective_id=0, has_side_effects=True),
        name="adi",
    )(
        pin_rows.reshape(chunks, 128),
        pin_cols.reshape(chunks, 128),
        pin_fracs,
        pin_weights.reshape(chunks, 128),
        capacity,
        blockage,
        row_blocks,
        col_blocks,
    )
    return pl.pallas_call(
        hand_over,
        out_shape=[jax.ShapeDtypeStruct(r.shape, r.dtype) for r in results],
        in_specs=[vmem] * 2,
        out_specs=[vmem] * 2,
        name="hand_over",
    )(*results)


def hand_over(first, second, first_out, second_out):
    first_out[...] = first[...]
    second_out[...] = second[...]


def solution(mesh):
    placed = (
        P(("strip", "cells")),
        P(("strip", "cells")),
        P(None, ("strip", "cells")),
        P(("strip", "cells")),
        P("strip", "cells"),
        P("strip", "cells"),
        P("cells", None, None),
        P(),
    )
    return jax.shard_map(
        diffuse,
        mesh=mesh,
        in_specs=placed,
        out_specs=(P("strip", "cells"), P(None, ("strip", "cells"))),
        check_vma=False,
    )
```

```python
import functools

import jax
import jax.numpy as jnp
from jax import lax
from jax.experimental import pallas as pl
from jax.experimental.pallas import tpu as pltpu
from jax.sharding import PartitionSpec as P

SWEEPS = 3
STEPS = 2
coupling = 2.0
floor_level = 0.5
w_steps = 8191.0
f32 = jnp.float32
bf16 = jnp.bfloat16


def exact_parts(values):
    high = values.astype(bf16)
    return high, (values - high.astype(f32)).astype(bf16)


def row_product(values, blocks_ref):
    pieces = []
    for n in range(blocks_ref.shape[0]):
        high, low = exact_parts(values[:, 128 * n : 128 * (n + 1)])
        pieces.append(
            lax.dot_general(
                jnp.concatenate([high, low, high], axis=1),
                blocks_ref[n],
                (((1,), (1,)), ((), ())),
                preferred_element_type=f32,
            )
        )
    return jnp.concatenate(pieces, axis=1)


def col_product(matrix_ref, values):
    high, low = exact_parts(values)
    parts = jnp.concatenate([high, low, high], axis=0)
    return jnp.dot(matrix_ref[...], parts, preferred_element_type=f32)


def table(index, first, second, count):
    spot = lax.broadcasted_iota(jnp.int32, (count, index.shape[1]), 0)
    return jnp.where(spot == index, first, jnp.where(spot == index + 1, second, 0.0))


def adi_kernel(
    sizes,
    rows_hbm,
    cols_hbm,
    fracs_hbm,
    pinw_hbm,
    cap_hbm,
    blk_hbm,
    rowb_hbm,
    colb_hbm,
    density_ref,
    pinv_ref,
    rows_ref,
    cols_ref,
    pinw_ref,
    fracs_ref,
    cap_ref,
    blk_ref,
    rowb_ref,
    colb_ref,
    bin_sums,
    part_ref,
    look,
    spread,
    vel_bins,
    edge_part,
    part_recv,
    edge_recv,
    wedge_send,
    wedge_recv,
    w_send,
    w_plane,
    w_block,
    rowb_parts,
    colb_parts,
    rim_send,
    rim_recv,
    field_send,
    field_plane,
    field_block,
    padded,
    answer_send,
    answer_near,
    near_send,
    near,
    still_send,
    still_recv,
    still_all,
    tops_send,
    tops_recv,
    tops_all,
    inflow,
    last_send,
    last_recv,
    send_sem,
    recv_sem,
    load_sem,
):
    K, Q, C, RD, NC, BL = sizes
    strips = K * Q
    HC = w_send.shape[2]
    cut = NC - HC
    strip = lax.axis_index("strip")
    cell = lax.axis_index("cells")
    plane = strip // Q
    place = strip % Q
    depth = Q // 2
    half = (place // 2) % 2
    strip_side = place % 2
    first_cell, last_cell = cell == 0, cell == C - 1
    first_plane, last_plane = plane == 0, plane == K - 1

    def at(strip_id, cell_id):
        return (strip_id, cell_id)

    cell_peers = [at(strip, (cell + d) % C) for d in range(1, C)]
    above_strip, below_strip = (strip + strips - 1) % strips, (strip + 1) % strips
    offsets = [(dz, dy) for dz in range(depth) for dy in range(2) if (dz, dy) != (0, 0)]
    offsets.sort(key=lambda o: -(min(o[0], depth - o[0]) + 2 * o[1]))
    plane_peers = []
    for dz, dy in offsets:
        other = ((place // 2 + dz) % depth) * 2 + (place % 2 + dy) % 2
        plane_peers.append((at(plane * Q + other, cell), (half + dz) % 2))
    partner = at(strip + 2 - 4 * half, cell)
    shifts = [(dk, dz) for dk in range(K) for dz in range(2) if (dk, dz) != (0, 0)]
    shifts.sort(key=lambda o: -(min(o[0], K - o[0]) + o[1]))
    plane_cross = [
        at(((plane + dk) % K) * Q + place + dz * (2 - 4 * half), cell) for dk, dz in shifts
    ]
    slot = 2 * plane + half
    plane_next = [
        at(((plane + dk) % K) * Q + place + dz * (2 - 4 * half), cell)
        for dk, dz in shifts
        if dk in (1, K - 1)
    ]
    row_peers = [at(s, (cell + d) % C) for s in (above_strip, below_strip) for d in range(C)]

    barrier = pltpu.get_barrier_semaphore()
    greeted = cell_peers + [p for p, _ in plane_peers] + plane_cross + row_peers
    for peer in greeted:
        pl.semaphore_signal(barrier, 1, device_id=peer, device_id_type=pl.DeviceIdType.MESH)

    sent = []

    def send(group, source, target, peer):
        pltpu.make_async_remote_copy(
            src_ref=source,
            dst_ref=target,
            send_sem=send_sem.at[group],
            recv_sem=recv_sem.at[group],
            device_id=peer,
            device_id_type=pl.DeviceIdType.MESH,
        ).start()

    def arrived(group, span):
        sent.append((group, span))
        pltpu.make_async_copy(span, span, recv_sem.at[group]).wait()

    loads = [
        pltpu.make_async_copy(source, target, load_sem.at[i])
        for i, (source, target) in enumerate(
            (
                (rows_hbm, rows_ref),
                (cols_hbm, cols_ref),
                (pinw_hbm, pinw_ref),
                (fracs_hbm, fracs_ref),
                (cap_hbm, cap_ref),
                (blk_hbm, blk_ref),
                (rowb_hbm, rowb_ref),
                (colb_hbm.at[plane], colb_ref),
            )
        )
    ]
    for load in loads:
        load.start()
    for load in loads:
        load.wait()

    chunks = rows_ref.shape[0]
    bins = bin_sums.shape[0]

    def pins_of(i):
        span = pl.ds(pl.multiple_of(128 * i, 128), 128)
        down, across = fracs_ref[0:1, span], fracs_ref[1:2, span]
        column = cols_ref[pl.ds(i, 1), :]
        tile = lax.shift_right_logical(column, 7)
        return down, across, tile * RD + rows_ref[pl.ds(i, 1), :], column - tile * 128

    def rounded(values):
        return values.astype(bf16).astype(f32)

    def add_pins(i, total):
        down, across, index, lane = pins_of(i)
        heavy = pinw_ref[pl.ds(i, 1), :]
        where_down = table(index, rounded(heavy * (1.0 - down)), rounded(heavy * down), bins)
        where_across = table(lane, rounded(1.0 - across), rounded(across), 136)
        return total + lax.dot_general(
            where_down.astype(bf16),
            where_across.astype(bf16),
            (((1,), (1,)), ((), ())),
            preferred_element_type=f32,
        )

    total = lax.fori_loop(0, chunks, add_pins, jnp.zeros((bins, 136), f32), unroll=4)
    spot = lax.broadcasted_iota(jnp.int32, (bins, 128), 1)
    past = jnp.where(spot == 0, total[:, 128:129], 0.0)
    bin_sums[...] = total[:, :128] + pltpu.roll(past, RD, 0)
    for c in range(C):
        for n in range(NC // 128):
            tile = c * (NC // 128) + n
            part_ref[c, :, 128 * n : 128 * (n + 1)] = bin_sums[RD * tile : RD * (tile + 1), :]

    weights = cap_ref[...].astype(f32) * (1.0 - blk_ref[...])
    whole = jnp.round(weights * w_steps).astype(jnp.int32).astype(jnp.int16)
    w_send[0] = whole[:, :HC]
    w_send[1] = whole[:, cut:]
    w_plane[place] = w_send[half]
    wedge_send[0] = weights[:1]
    wedge_send[1] = weights[RD - 1 :]
    for c in range(C):
        edge_part[0, c] = part_ref[c, :1]
        edge_part[1, c] = part_ref[c, RD - 1 :]
    pl.semaphore_wait(barrier, len(greeted))

    for d in range(C):
        other = (cell + d) % C
        send(1, edge_part.at[0, other], edge_recv.at[1, cell], at(above_strip, other))
        send(1, edge_part.at[1, other], edge_recv.at[0, cell], at(below_strip, other))
    send(2, wedge_send.at[0], wedge_recv.at[1], at(above_strip, cell))
    send(2, wedge_send.at[1], wedge_recv.at[0], at(below_strip, cell))
    for d in range(1, C):
        other = (cell + d) % C
        send(0, part_ref.at[other], part_recv.at[C - 1 - d], at(strip, other))
    for peer, other_half in plane_peers:
        send(3, w_send.at[other_half], w_plane.at[place], peer)

    for n in range(rowb_ref.shape[0]):
        high, low = exact_parts(rowb_ref[n])
        rowb_parts[n] = jnp.concatenate([high, high, low], axis=1)
    high, low = exact_parts(colb_ref[...])
    colb_parts[...] = jnp.concatenate([high, high, low], axis=1)

    end = lax.broadcasted_iota(jnp.int32, (RD, HC), 1)

    def along_inside(values):
        left = pltpu.roll(values, 1, 1)
        right = pltpu.roll(values, NC - 1, 1)
        spot = lax.broadcasted_iota(jnp.int32, values.shape, 1)
        left = jnp.where(spot == 0, jnp.where(first_cell, values, 0.0), left)
        right = jnp.where(spot == NC - 1, jnp.where(last_cell, values, 0.0), right)
        return 2.0 * values - left - right

    weights_two = jnp.concatenate([weights, weights], axis=0)
    spot = lax.broadcasted_iota(jnp.int32, (2 * RD, NC), 1)
    row = lax.broadcasted_iota(jnp.int32, (2 * RD, NC), 0)
    unit = jnp.where(spot == jnp.where(row < RD, 0, NC - 1), coupling, 0.0)
    pulse = row_product(unit, rowb_parts)
    pulses = [pulse]
    for _ in range(SWEEPS - 1):
        back = weights_two * pulse + coupling * along_inside(pulse)
        pulse = pulse - row_product(back, rowb_parts)
        pulses.append(pulse)

    arrived(1, edge_recv)
    arrived(2, wedge_recv)
    arrived(0, part_recv.at[0 : C - 1])
    density = part_ref[cell]
    for d in range(C - 1):
        density = density + part_recv[d]
    current = density / weights
    row_above = edge_recv[0, 0]
    row_below = edge_recv[1, 0]
    for c in range(1, C):
        row_above = row_above + edge_recv[0, c]
        row_below = row_below + edge_recv[1, c]
    row_above = row_above / wedge_recv[0]
    row_below = row_below / wedge_recv[1]
    row_above = jnp.where(strip == 0, current[:1], row_above)
    row_below = jnp.where(strip == strips - 1, current[RD - 1 :], row_below)

    def frame(pair):
        base = pl.multiple_of(RD * 2 * pair, 2 * RD)
        inner = padded[pl.ds(base + 8, 2 * RD), :]
        over = padded[pl.ds(base + 7, 1), :]
        under = padded[pl.ds(base + 8 + 2 * RD, 1), :]
        fill = jnp.zeros((6 - RD, HC), f32)
        upper = jnp.concatenate([over, inner[: RD + 1], fill], axis=0)
        lower = jnp.concatenate([inner[RD - 1 :], under, fill], axis=0)
        return jnp.where(strip_side == 0, upper, lower)

    def frames():
        return frame(place // 2), frame(place // 2 + 1 - 2 * half)

    small = lax.broadcasted_iota(jnp.int32, (RD, 128), 1)

    def clamp_rows(values):
        shape = values.shape
        spot = lax.broadcasted_iota(jnp.int32, shape, 0)
        up = pltpu.roll(values, 1, 0)
        down = pltpu.roll(values, shape[0] - 1, 0)
        up = jnp.where(spot == 0, jnp.where(first_plane, values, 0.0), up)
        down = jnp.where(spot == shape[0] - 1, jnp.where(last_plane, values, 0.0), down)
        return 2.0 * values - up - down

    for step in range(STEPS):
        up = jnp.concatenate([row_above, current[: RD - 1]], axis=0)
        down = jnp.concatenate([current[1:], row_below], axis=0)
        source = weights * current - coupling * (2.0 * current - up - down)
        iterate = current
        levels = [iterate]
        for _ in range(SWEEPS):
            left_over = source - (weights * iterate + coupling * along_inside(iterate))
            iterate = iterate + row_product(left_over, rowb_parts)
            levels.append(iterate)
        for side, column in ((0, 0), (1, NC - 1)):
            message = jnp.zeros((RD, 128), f32)
            for j in range(SWEEPS + 1):
                message = jnp.where(small == j, levels[j][:, column : column + 1], message)
            for m in range(SWEEPS):
                mine = pulses[m][side * RD : (side + 1) * RD, column : column + 1]
                message = jnp.where(small == SWEEPS + 1 + m, mine, message)
            rim_send[step, side] = message
        group = 4 + 4 * step
        send(group, rim_send.at[step, 0], rim_recv.at[step, 1], at(strip, (cell + C - 1) % C))
        send(group, rim_send.at[step, 1], rim_recv.at[step, 0], at(strip, (cell + 1) % C))

        arrived(group, rim_recv.at[step])
        edges = []
        for side in range(2):
            own = [rim_send[step, side][:, i : i + 1] for i in range(2 * SWEEPS + 1)]
            far = [rim_recv[step, side][:, i : i + 1] for i in range(2 * SWEEPS + 1)]
            mine, theirs = [], []
            for j in range(SWEEPS + 1):
                a, b = own[j], far[j]
                for i in range(j):
                    a = a + own[SWEEPS + j - i] * theirs[i]
                    b = b + far[SWEEPS + j - i] * mine[i]
                mine.append(a)
                theirs.append(b)
            edges.append(theirs)
        left_in = [jnp.where(first_cell, 0.0, e) for e in edges[0]]
        right_in = [jnp.where(last_cell, 0.0, e) for e in edges[1]]
        for i in range(SWEEPS):
            iterate = iterate + (
                pulses[SWEEPS - 1 - i][:RD] * left_in[i] + pulses[SWEEPS - 1 - i][RD:] * right_in[i]
            )
        halo_left = jnp.where(first_cell, iterate[:, :1], left_in[SWEEPS])
        halo_right = jnp.where(last_cell, iterate[:, NC - 1 :], right_in[SWEEPS])
        field_send[step, 0] = jnp.where(end == HC - 1, halo_left, iterate[:, :HC])
        field_send[step, 1] = jnp.where(end == 0, halo_right, iterate[:, cut:])
        field_plane[step, place] = field_send[step, half]
        for peer, other_half in plane_peers:
            send(group + 2, field_send.at[step, other_half], field_plane.at[step, place], peer)
        if step == 0:
            arrived(3, w_plane.at[0 : Q - 1])
            for i in range(Q):
                stepped = w_plane[i].astype(jnp.int32).astype(f32)
                w_block[RD * i : RD * (i + 1), :] = stepped * (1.0 / w_steps)
            padded[0:8, :] = jnp.zeros((8, HC), f32)
            padded[BL + 8 :, :] = jnp.zeros((8, HC), f32)
            for side, column in ((0, 0), (1, BL - 1)):
                answer = coupling * jnp.broadcast_to(
                    colb_ref[:, column : column + 1], (BL, HC)
                )
                for m in range(SWEEPS):
                    if m > 0:
                        back = w_block[...] * answer + coupling * clamp_rows(answer)
                        answer = answer - col_product(colb_parts, back)
                    padded[8 : BL + 8, :] = answer
                    own, other = frames()
                    answer_near[half, m, side] = own
                    answer_send[m, side] = other
                    still_send[m, side, 0:1, :] = answer[:1]
                    still_send[m, side, 1:2, :] = answer[BL - 1 :]
            still_recv[slot] = still_send[...]
            for peer in plane_cross:
                send(5, still_send, still_recv.at[slot], peer)
            send(9, answer_send, answer_near.at[half], partner)
        else:

            def prepare(i, carry):
                for k in range(2):
                    down, across, index, lane = pins_of(2 * i + k)
                    part = slice(128 * k, 128 * (k + 1))
                    nearer, farther = rounded(1.0 - down), rounded(down)
                    look[i, :, part] = table(index, nearer, farther, 128).astype(bf16)
                    spread[i, :, part] = table(lane, rounded(1.0 - across), rounded(across), 136)
                return carry

            lax.fori_loop(0, chunks // 2, prepare, 0)

        arrived(group + 2, field_plane.at[step, 0 : Q - 1])
        for i in range(Q):
            field_block[RD * i : RD * (i + 1), :] = field_plane[step, i]

        start = field_block[...]
        beside = pltpu.roll(start, 1, 1) + pltpu.roll(start, HC - 1, 1)
        middle = w_block[...] * start - coupling * (2.0 * start - beside)
        iterate = start
        for j in range(SWEEPS + 1):
            if j == SWEEPS:
                for peer in plane_cross:
                    send(
                        group + 3,
                        tops_send.at[step, 0:SWEEPS],
                        tops_recv.at[step, slot, 0:SWEEPS],
                        peer,
                    )
            if j > 0:
                left_over = middle - (w_block[...] * iterate + coupling * clamp_rows(iterate))
                iterate = iterate + col_product(colb_parts, left_over)
            tops_send[step, j, 0:1, :] = iterate[:1]
            tops_send[step, j, 1:2, :] = iterate[BL - 1 :]
        for peer in plane_next:
            send(
                15 + step,
                tops_send.at[step, SWEEPS],
                tops_recv.at[step, slot, SWEEPS],
                peer,
            )
        padded[8 : BL + 8, :] = iterate
        own, other = frames()
        near_send[step] = other
        near[step, half] = own
        send(13 + step, near_send.at[step], near.at[step, half], partner)
        tops_recv[step, slot] = tops_send[step]

        if step == 0:
            arrived(5, still_recv.at[0 : 2 * K - 1])
            arrived(9, answer_near.at[0])
            for k in range(K):
                for m in range(SWEEPS):
                    for side in range(2):
                        for h in range(2):
                            still_all[h, m, side, 2 * k : 2 * k + 2, :] = still_recv[
                                2 * k + h, m, side
                            ]
        arrived(group + 3, tops_recv.at[step, 0 : 2 * K - 1, 0:SWEEPS])
        arrived(15 + step, tops_recv.at[step, 0 : len(plane_next), SWEEPS])
        for k in range(K):
            for j in range(SWEEPS + 1):
                for h in range(2):
                    tops_all[h, j, 2 * k : 2 * k + 2, :] = tops_recv[step, 2 * k + h, j]
        arrived(13 + step, near.at[step, 0])
        spot = lax.broadcasted_iota(jnp.int32, (2 * K, HC), 0)
        even = spot % 2 == 0
        mine = pl.ds(2 * plane, 1)
        halves = []
        for h in range(2):
            from_above, from_below = [], []
            for j in range(SWEEPS + 1):
                value = tops_all[h, j]
                for i in range(j):
                    value = value + still_all[h, j - i - 1, 0] * from_above[i]
                    value = value + still_all[h, j - i - 1, 1] * from_below[i]
                over = jnp.where(even, pltpu.roll(value, 1, 0), pltpu.roll(value, 2, 0))
                under = jnp.where(
                    even, pltpu.roll(value, 2 * K - 2, 0), pltpu.roll(value, 2 * K - 1, 0)
                )
                from_above.append(jnp.where(spot < 2, 0.0, over))
                from_below.append(jnp.where(spot >= 2 * K - 2, 0.0, under))
                inflow[h, j, 0] = from_above[j]
                inflow[h, j, 1] = from_below[j]
            nearby = near[step, h]
            for i in range(SWEEPS):
                m = SWEEPS - 1 - i
                nearby = nearby + (
                    answer_near[h, m, 0] * inflow[h, i, 0, mine, :]
                    + answer_near[h, m, 1] * inflow[h, i, 1, mine, :]
                )
            above, below = nearby[:1], nearby[1 + RD : 2 + RD]
            above = jnp.where(place == 0, inflow[h, SWEEPS, 0, mine, :], above)
            below = jnp.where(place == Q - 1, inflow[h, SWEEPS, 1, mine, :], below)
            halves.append((above, nearby[1 : 1 + RD], below))

        def joined(first, second):
            over = HC - cut
            lanes = lax.broadcasted_iota(jnp.int32, (first.shape[0], over), 1)
            both = jnp.where(lanes < over // 2, first[:, cut:], second[:, :over])
            return jnp.concatenate([first[:, :cut], both, second[:, over:]], axis=1)

        row_above, current, row_below = (joined(a, b) for a, b in zip(*halves))
        row_above = jnp.where(strip == 0, current[:1], row_above)
        row_below = jnp.where(strip == strips - 1, current[RD - 1 :], row_below)

    density_ref[...] = current
    last_send[0:1, :] = row_above
    last_send[1 : 1 + RD, :] = current
    last_send[1 + RD : 2 + RD, :] = row_below
    last_send[2 + RD : 8, :] = jnp.zeros((6 - RD, NC), f32)
    last_recv[cell] = last_send[...]
    for peer in cell_peers:
        send(12, last_send, last_recv.at[cell], peer)
    arrived(12, last_recv.at[0 : C - 1])
    field = jnp.concatenate([last_recv[c] for c in range(C)], axis=1)
    centre = field[1 : 1 + RD]
    spot = lax.broadcasted_iota(jnp.int32, (RD, C * NC), 1)
    left = jnp.where(spot == 0, centre, pltpu.roll(centre, 1, 1))
    right = jnp.where(spot == C * NC - 1, centre, pltpu.roll(centre, C * NC - 1, 1))
    scale = jnp.maximum(centre, floor_level)
    velocity_y = -(0.5 * (field[2 : 2 + RD] - field[:RD])) / scale
    velocity_x = -(0.5 * (right - left)) / scale
    tables = []
    for i, velocity in enumerate((velocity_y, velocity_x)):
        vel_bins[i, bins:, :] = jnp.zeros((128 - bins, 128), f32)
        for n in range(bins // RD):
            vel_bins[i, RD * n : RD * (n + 1), :] = velocity[:, 128 * n : 128 * (n + 1)]
        turned = jnp.transpose(vel_bins[i])
        past = jnp.broadcast_to(pltpu.roll(turned[:8], 128 - RD, 1)[:1], (8, 128))
        tables += [turned.astype(bf16), past.astype(bf16)]
    tables = jnp.concatenate(tables, axis=0)

    def sample(i, carry):
        sampled = jnp.dot(tables, look[i], preferred_element_type=f32)
        across = spread[i]
        out_y = jnp.sum(sampled[:136] * across, axis=0, keepdims=True)
        out_x = jnp.sum(sampled[136:] * across, axis=0, keepdims=True)
        span = pl.ds(pl.multiple_of(256 * i, 256), 256)
        pinv_ref[:, span] = jnp.concatenate([out_y, out_x], axis=0)
        return carry

    lax.fori_loop(0, chunks // 2, sample, 0, unroll=4)
    for group, span in sent:
        pltpu.make_async_copy(span, span, send_sem.at[group]).wait()


def diffuse(pin_rows, pin_cols, pin_fracs, pin_weights, capacity, blockage, row_blocks, col_blocks):
    pins = pin_rows.shape[0]
    chunks = pins // 128
    strips = lax.axis_size("strip")
    C = lax.axis_size("cells")
    RD, NC = capacity.shape
    NB = row_blocks.shape[0]
    K, BL = col_blocks.shape[:2]
    Q = strips // K
    HC = 128 * ((NB + 1) // 2)
    vmem = pl.BlockSpec(memory_space=pltpu.VMEM)
    bins = RD * C * NC // 128
    shapes = [
        ((chunks, 128), jnp.int32),
        ((chunks, 128), jnp.int32),
        ((chunks, 128), f32),
        ((2, pins), f32),
        ((RD, NC), jnp.int32),
        ((RD, NC), f32),
        ((NB, 128, 128), f32),
        ((BL, BL), f32),
        ((bins, 128), f32),
        ((C, RD, NC), f32),
        ((chunks // 2, 128, 256), bf16),
        ((chunks // 2, 136, 256), f32),
        ((2, 128, 128), f32),
        ((2, C, 1, NC), f32),
        ((C, RD, NC), f32),
        ((2, C, 1, NC), f32),
        ((2, 1, NC), f32),
        ((2, 1, NC), f32),
        ((2, RD, HC), jnp.int16),
        ((Q, RD, HC), jnp.int16),
        ((BL, HC), f32),
        ((NB, 128, 384), bf16),
        ((BL, 3 * BL), bf16),
        ((STEPS, 2, RD, 128), f32),
        ((STEPS, 2, RD, 128), f32),
        ((STEPS, 2, RD, HC), f32),
        ((STEPS, Q, RD, HC), f32),
        ((BL, HC), f32),
        ((BL + 16, HC), f32),
        ((SWEEPS, 2, 8, HC), f32),
        ((2, SWEEPS, 2, 8, HC), f32),
        ((STEPS, 8, HC), f32),
        ((STEPS, 2, 8, HC), f32),
        ((SWEEPS, 2, 2, HC), f32),
        ((2 * K, SWEEPS, 2, 2, HC), f32),
        ((2, SWEEPS, 2, 2 * K, HC), f32),
        ((STEPS, SWEEPS + 1, 2, HC), f32),
        ((STEPS, 2 * K, SWEEPS + 1, 2, HC), f32),
        ((2, SWEEPS + 1, 2 * K, HC), f32),
        ((2, SWEEPS + 1, 2, 2 * K, HC), f32),
        ((8, NC), f32),
        ((C, 8, NC), f32),
    ]
    results = pl.pallas_call(
        functools.partial(adi_kernel, (K, Q, C, RD, NC, BL)),
        out_shape=(
            jax.ShapeDtypeStruct((RD, NC), f32),
            jax.ShapeDtypeStruct((2, pins), f32),
        ),
        in_specs=[pl.BlockSpec(memory_space=pltpu.HBM)] * 8,
        out_specs=(vmem, vmem),
        scratch_shapes=[pltpu.VMEM(shape, dtype) for shape, dtype in shapes]
        + [pltpu.SemaphoreType.DMA((n,)) for n in (17, 17, 8)],
        compiler_params=pltpu.CompilerParams(collective_id=0, has_side_effects=True),
        name="adi",
    )(
        pin_rows.reshape(chunks, 128),
        pin_cols.reshape(chunks, 128),
        pin_fracs,
        pin_weights.reshape(chunks, 128),
        capacity,
        blockage,
        row_blocks,
        col_blocks,
    )
    return pl.pallas_call(
        hand_over,
        out_shape=[jax.ShapeDtypeStruct(r.shape, r.dtype) for r in results],
        in_specs=[vmem] * 2,
        out_specs=[vmem] * 2,
        name="hand_over",
    )(*results)


def hand_over(first, second, first_out, second_out):
    first_out[...] = first[...]
    second_out[...] = second[...]


def solution(mesh):
    placed = (
        P(("strip", "cells")),
        P(("strip", "cells")),
        P(None, ("strip", "cells")),
        P(("strip", "cells")),
        P("strip", "cells"),
        P("strip", "cells"),
        P("cells", None, None),
        P(),
    )
    return jax.shard_map(
        diffuse,
        mesh=mesh,
        in_specs=placed,
        out_specs=(P("strip", "cells"), P(None, ("strip", "cells"))),
        check_vma=False,
    )
```

```python
import functools

import jax
import jax.numpy as jnp
from jax import lax
from jax.experimental import pallas as pl
from jax.experimental.pallas import tpu as pltpu
from jax.sharding import PartitionSpec as P

SWEEPS = 3
STEPS = 2
coupling = 2.0
floor_level = 0.5
w_steps = 8191.0
f32 = jnp.float32
bf16 = jnp.bfloat16


def exact_parts(values):
    high = values.astype(bf16)
    return high, (values - high.astype(f32)).astype(bf16)


def row_product(values, blocks_ref):
    pieces = []
    for n in range(blocks_ref.shape[0]):
        high, low = exact_parts(values[:, 128 * n : 128 * (n + 1)])
        pieces.append(
            lax.dot_general(
                jnp.concatenate([high, low, high], axis=1),
                blocks_ref[n],
                (((1,), (1,)), ((), ())),
                preferred_element_type=f32,
            )
        )
    return jnp.concatenate(pieces, axis=1)


def col_product(matrix_ref, values):
    high, low = exact_parts(values)
    parts = jnp.concatenate([high, low, high], axis=0)
    return jnp.dot(matrix_ref[...], parts, preferred_element_type=f32)


def table(index, first, second, count):
    spot = lax.broadcasted_iota(jnp.int32, (count, index.shape[1]), 0)
    return jnp.where(spot == index, first, jnp.where(spot == index + 1, second, 0.0))


def adi_kernel(
    sizes,
    rows_hbm,
    cols_hbm,
    fracs_hbm,
    pinw_hbm,
    cap_hbm,
    blk_hbm,
    rowb_hbm,
    colb_hbm,
    density_ref,
    pinv_ref,
    rows_ref,
    cols_ref,
    pinw_ref,
    fracs_ref,
    cap_ref,
    blk_ref,
    rowb_ref,
    colb_ref,
    bin_sums,
    part_ref,
    look,
    spread,
    vel_bins,
    edge_part,
    part_recv,
    edge_recv,
    wedge_send,
    wedge_recv,
    w_send,
    w_plane,
    w_block,
    rowb_parts,
    colb_parts,
    rim_send,
    rim_recv,
    field_send,
    field_plane,
    field_block,
    padded,
    answer_send,
    answer_near,
    near_send,
    near,
    still_send,
    still_recv,
    still_all,
    tops_send,
    tops_recv,
    tops_all,
    inflow,
    last_send,
    last_recv,
    send_sem,
    recv_sem,
    load_sem,
):
    K, Q, C, RD, NC, BL = sizes
    strips = K * Q
    HC = w_send.shape[2]
    cut = NC - HC
    strip = lax.axis_index("strip")
    cell = lax.axis_index("cells")
    plane = strip // Q
    place = strip % Q
    depth = Q // 2
    half = (place // 2) % 2
    strip_side = place % 2
    first_cell, last_cell = cell == 0, cell == C - 1
    first_plane, last_plane = plane == 0, plane == K - 1

    def at(strip_id, cell_id):
        return (strip_id, cell_id)

    cell_peers = [at(strip, (cell + d) % C) for d in range(1, C)]
    above_strip, below_strip = (strip + strips - 1) % strips, (strip + 1) % strips
    offsets = [(dz, dy) for dz in range(depth) for dy in range(2) if (dz, dy) != (0, 0)]
    offsets.sort(key=lambda o: -(min(o[0], depth - o[0]) + 2 * o[1]))
    plane_peers = []
    for dz, dy in offsets:
        other = ((place // 2 + dz) % depth) * 2 + (place % 2 + dy) % 2
        plane_peers.append((at(plane * Q + other, cell), (half + dz) % 2))
    partner = at(strip + 2 - 4 * half, cell)
    shifts = [(dk, dz) for dk in range(K) for dz in range(2) if (dk, dz) != (0, 0)]
    shifts.sort(key=lambda o: -(min(o[0], K - o[0]) + o[1]))
    plane_cross = [
        at(((plane + dk) % K) * Q + place + dz * (2 - 4 * half), cell) for dk, dz in shifts
    ]
    slot = 2 * plane + half
    plane_next = [
        at(((plane + dk) % K) * Q + place + dz * (2 - 4 * half), cell)
        for dk, dz in shifts
        if dk in (1, K - 1)
    ]
    row_peers = [at(s, (cell + d) % C) for s in (above_strip, below_strip) for d in range(C)]

    barrier = pltpu.get_barrier_semaphore()
    greeted = cell_peers + [p for p, _ in plane_peers] + plane_cross + row_peers
    for peer in greeted:
        pl.semaphore_signal(barrier, 1, device_id=peer, device_id_type=pl.DeviceIdType.MESH)

    sent = []

    def send(group, source, target, peer):
        pltpu.make_async_remote_copy(
            src_ref=source,
            dst_ref=target,
            send_sem=send_sem.at[group],
            recv_sem=recv_sem.at[group],
            device_id=peer,
            device_id_type=pl.DeviceIdType.MESH,
        ).start()

    def arrived(group, span):
        sent.append((group, span))
        pltpu.make_async_copy(span, span, recv_sem.at[group]).wait()

    loads = [
        pltpu.make_async_copy(source, target, load_sem.at[i])
        for i, (source, target) in enumerate(
            (
                (rows_hbm, rows_ref),
                (cols_hbm, cols_ref),
                (pinw_hbm, pinw_ref),
                (fracs_hbm, fracs_ref),
                (cap_hbm, cap_ref),
                (blk_hbm, blk_ref),
                (rowb_hbm, rowb_ref),
                (colb_hbm, colb_ref),
            )
        )
    ]
    for load in loads:
        load.start()
    for load in loads:
        load.wait()

    chunks = rows_ref.shape[0]
    bins = bin_sums.shape[0]

    def pins_of(i):
        span = pl.ds(pl.multiple_of(128 * i, 128), 128)
        down, across = fracs_ref[0:1, span], fracs_ref[1:2, span]
        column = cols_ref[pl.ds(i, 1), :]
        tile = lax.shift_right_logical(column, 7)
        return down, across, tile * RD + rows_ref[pl.ds(i, 1), :], column - tile * 128

    def rounded(values):
        return values.astype(bf16).astype(f32)

    def add_pins(i, total):
        down, across, index, lane = pins_of(i)
        heavy = pinw_ref[pl.ds(i, 1), :]
        where_down = table(index, rounded(heavy * (1.0 - down)), rounded(heavy * down), bins)
        where_across = table(lane, rounded(1.0 - across), rounded(across), 136)
        return total + lax.dot_general(
            where_down.astype(bf16),
            where_across.astype(bf16),
            (((1,), (1,)), ((), ())),
            preferred_element_type=f32,
        )

    total = lax.fori_loop(0, chunks, add_pins, jnp.zeros((bins, 136), f32), unroll=4)
    spot = lax.broadcasted_iota(jnp.int32, (bins, 128), 1)
    past = jnp.where(spot == 0, total[:, 128:129], 0.0)
    bin_sums[...] = total[:, :128] + pltpu.roll(past, RD, 0)
    for c in range(C):
        for n in range(NC // 128):
            tile = c * (NC // 128) + n
            part_ref[c, :, 128 * n : 128 * (n + 1)] = bin_sums[RD * tile : RD * (tile + 1), :]

    weights = cap_ref[...].astype(f32) * (1.0 - blk_ref[...])
    whole = jnp.round(weights * w_steps).astype(jnp.int32).astype(jnp.int16)
    w_send[0] = whole[:, :HC]
    w_send[1] = whole[:, cut:]
    w_plane[place] = w_send[half]
    wedge_send[0] = weights[:1]
    wedge_send[1] = weights[RD - 1 :]
    for c in range(C):
        edge_part[0, c] = part_ref[c, :1]
        edge_part[1, c] = part_ref[c, RD - 1 :]
    pl.semaphore_wait(barrier, len(greeted))

    for d in range(C):
        other = (cell + d) % C
        send(1, edge_part.at[0, other], edge_recv.at[1, cell], at(above_strip, other))
        send(1, edge_part.at[1, other], edge_recv.at[0, cell], at(below_strip, other))
    send(2, wedge_send.at[0], wedge_recv.at[1], at(above_strip, cell))
    send(2, wedge_send.at[1], wedge_recv.at[0], at(below_strip, cell))
    for d in range(1, C):
        other = (cell + d) % C
        send(0, part_ref.at[other], part_recv.at[C - 1 - d], at(strip, other))
    for peer, other_half in plane_peers:
        send(3, w_send.at[other_half], w_plane.at[place], peer)

    for n in range(rowb_ref.shape[0]):
        high, low = exact_parts(rowb_ref[n])
        rowb_parts[n] = jnp.concatenate([high, high, low], axis=1)
    high, low = exact_parts(colb_ref[plane])
    colb_parts[...] = jnp.concatenate([high, high, low], axis=1)

    end = lax.broadcasted_iota(jnp.int32, (RD, HC), 1)

    def along_inside(values):
        left = pltpu.roll(values, 1, 1)
        right = pltpu.roll(values, NC - 1, 1)
        spot = lax.broadcasted_iota(jnp.int32, values.shape, 1)
        left = jnp.where(spot == 0, jnp.where(first_cell, values, 0.0), left)
        right = jnp.where(spot == NC - 1, jnp.where(last_cell, values, 0.0), right)
        return 2.0 * values - left - right

    weights_two = jnp.concatenate([weights, weights], axis=0)
    spot = lax.broadcasted_iota(jnp.int32, (2 * RD, NC), 1)
    row = lax.broadcasted_iota(jnp.int32, (2 * RD, NC), 0)
    unit = jnp.where(spot == jnp.where(row < RD, 0, NC - 1), coupling, 0.0)
    pulse = row_product(unit, rowb_parts)
    pulses = [pulse]
    for _ in range(SWEEPS - 1):
        back = weights_two * pulse + coupling * along_inside(pulse)
        pulse = pulse - row_product(back, rowb_parts)
        pulses.append(pulse)

    arrived(1, edge_recv)
    arrived(2, wedge_recv)
    arrived(0, part_recv.at[0 : C - 1])
    density = part_ref[cell]
    for d in range(C - 1):
        density = density + part_recv[d]
    current = density / weights
    row_above = edge_recv[0, 0]
    row_below = edge_recv[1, 0]
    for c in range(1, C):
        row_above = row_above + edge_recv[0, c]
        row_below = row_below + edge_recv[1, c]
    row_above = row_above / wedge_recv[0]
    row_below = row_below / wedge_recv[1]
    row_above = jnp.where(strip == 0, current[:1], row_above)
    row_below = jnp.where(strip == strips - 1, current[RD - 1 :], row_below)

    def frame(pair):
        base = pl.multiple_of(RD * 2 * pair, 2 * RD)
        inner = padded[pl.ds(base + 8, 2 * RD), :]
        over = padded[pl.ds(base + 7, 1), :]
        under = padded[pl.ds(base + 8 + 2 * RD, 1), :]
        fill = jnp.zeros((6 - RD, HC), f32)
        upper = jnp.concatenate([over, inner[: RD + 1], fill], axis=0)
        lower = jnp.concatenate([inner[RD - 1 :], under, fill], axis=0)
        return jnp.where(strip_side == 0, upper, lower)

    def frames():
        return frame(place // 2), frame(place // 2 + 1 - 2 * half)

    small = lax.broadcasted_iota(jnp.int32, (RD, 128), 1)

    def clamp_rows(values):
        shape = values.shape
        spot = lax.broadcasted_iota(jnp.int32, shape, 0)
        up = pltpu.roll(values, 1, 0)
        down = pltpu.roll(values, shape[0] - 1, 0)
        up = jnp.where(spot == 0, jnp.where(first_plane, values, 0.0), up)
        down = jnp.where(spot == shape[0] - 1, jnp.where(last_plane, values, 0.0), down)
        return 2.0 * values - up - down

    for step in range(STEPS):
        up = jnp.concatenate([row_above, current[: RD - 1]], axis=0)
        down = jnp.concatenate([current[1:], row_below], axis=0)
        source = weights * current - coupling * (2.0 * current - up - down)
        iterate = current
        levels = [iterate]
        for _ in range(SWEEPS):
            left_over = source - (weights * iterate + coupling * along_inside(iterate))
            iterate = iterate + row_product(left_over, rowb_parts)
            levels.append(iterate)
        for side, column in ((0, 0), (1, NC - 1)):
            message = jnp.zeros((RD, 128), f32)
            for j in range(SWEEPS + 1):
                message = jnp.where(small == j, levels[j][:, column : column + 1], message)
            for m in range(SWEEPS):
                mine = pulses[m][side * RD : (side + 1) * RD, column : column + 1]
                message = jnp.where(small == SWEEPS + 1 + m, mine, message)
            rim_send[step, side] = message
        group = 4 + 4 * step
        send(group, rim_send.at[step, 0], rim_recv.at[step, 1], at(strip, (cell + C - 1) % C))
        send(group, rim_send.at[step, 1], rim_recv.at[step, 0], at(strip, (cell + 1) % C))

        arrived(group, rim_recv.at[step])
        edges = []
        for side in range(2):
            own = [rim_send[step, side][:, i : i + 1] for i in range(2 * SWEEPS + 1)]
            far = [rim_recv[step, side][:, i : i + 1] for i in range(2 * SWEEPS + 1)]
            mine, theirs = [], []
            for j in range(SWEEPS + 1):
                a, b = own[j], far[j]
                for i in range(j):
                    a = a + own[SWEEPS + j - i] * theirs[i]
                    b = b + far[SWEEPS + j - i] * mine[i]
                mine.append(a)
                theirs.append(b)
            edges.append(theirs)
        left_in = [jnp.where(first_cell, 0.0, e) for e in edges[0]]
        right_in = [jnp.where(last_cell, 0.0, e) for e in edges[1]]
        for i in range(SWEEPS):
            iterate = iterate + (
                pulses[SWEEPS - 1 - i][:RD] * left_in[i] + pulses[SWEEPS - 1 - i][RD:] * right_in[i]
            )
        halo_left = jnp.where(first_cell, iterate[:, :1], left_in[SWEEPS])
        halo_right = jnp.where(last_cell, iterate[:, NC - 1 :], right_in[SWEEPS])
        field_send[step, 0] = jnp.where(end == HC - 1, halo_left, iterate[:, :HC])
        field_send[step, 1] = jnp.where(end == 0, halo_right, iterate[:, cut:])
        field_plane[step, place] = field_send[step, half]
        for peer, other_half in plane_peers:
            send(group + 2, field_send.at[step, other_half], field_plane.at[step, place], peer)
        if step == 0:
            arrived(3, w_plane.at[0 : Q - 1])
            for i in range(Q):
                stepped = w_plane[i].astype(jnp.int32).astype(f32)
                w_block[RD * i : RD * (i + 1), :] = stepped * (1.0 / w_steps)
            padded[0:8, :] = jnp.zeros((8, HC), f32)
            padded[BL + 8 :, :] = jnp.zeros((8, HC), f32)
            for side, column in ((0, 0), (1, BL - 1)):
                answer = coupling * jnp.broadcast_to(
                    colb_ref[plane][:, column : column + 1], (BL, HC)
                )
                for m in range(SWEEPS):
                    if m > 0:
                        back = w_block[...] * answer + coupling * clamp_rows(answer)
                        answer = answer - col_product(colb_parts, back)
                    padded[8 : BL + 8, :] = answer
                    own, other = frames()
                    answer_near[half, m, side] = own
                    if m == 0:
                        answer_near[1 - half, m, side] = own
                    else:
                        answer_send[m - 1, side] = other
                        still_send[m - 1, side, 0:1, :] = answer[:1]
                        still_send[m - 1, side, 1:2, :] = answer[BL - 1 :]
            still_recv[slot] = still_send[...]
            for peer in plane_cross:
                send(5, still_send, still_recv.at[slot], peer)
            send(9, answer_send, answer_near.at[half, 1:SWEEPS], partner)
        else:

            def prepare(i, carry):
                for k in range(2):
                    down, across, index, lane = pins_of(2 * i + k)
                    part = slice(128 * k, 128 * (k + 1))
                    nearer, farther = rounded(1.0 - down), rounded(down)
                    look[i, :, part] = table(index, nearer, farther, 128).astype(bf16)
                    spread[i, :, part] = table(lane, rounded(1.0 - across), rounded(across), 136)
                return carry

            lax.fori_loop(0, chunks // 2, prepare, 0)

        arrived(group + 2, field_plane.at[step, 0 : Q - 1])
        for i in range(Q):
            field_block[RD * i : RD * (i + 1), :] = field_plane[step, i]

        start = field_block[...]
        beside = pltpu.roll(start, 1, 1) + pltpu.roll(start, HC - 1, 1)
        middle = w_block[...] * start - coupling * (2.0 * start - beside)
        iterate = start
        for j in range(SWEEPS + 1):
            if j == SWEEPS:
                for peer in plane_cross:
                    send(
                        group + 3,
                        tops_send.at[step, 0:SWEEPS],
                        tops_recv.at[step, slot, 0:SWEEPS],
                        peer,
                    )
            if j > 0:
                left_over = middle - (w_block[...] * iterate + coupling * clamp_rows(iterate))
                iterate = iterate + col_product(colb_parts, left_over)
            tops_send[step, j, 0:1, :] = iterate[:1]
            tops_send[step, j, 1:2, :] = iterate[BL - 1 :]
        for peer in plane_next:
            send(
                15 + step,
                tops_send.at[step, SWEEPS],
                tops_recv.at[step, slot, SWEEPS],
                peer,
            )
        padded[8 : BL + 8, :] = iterate
        own, other = frames()
        near_send[step] = other
        near[step, half] = own
        send(13 + step, near_send.at[step], near.at[step, half], partner)
        tops_recv[step, slot] = tops_send[step]

        if step == 0:
            for k in range(K):
                for side, column in ((0, 0), (1, BL - 1)):
                    for t, line in ((0, 0), (1, BL - 1)):
                        corner = coupling * colb_ref[k][line : line + 1, column : column + 1]
                        corner = jnp.broadcast_to(corner, (1, HC))
                        for h in range(2):
                            still_all[h, 0, side, 2 * k + t : 2 * k + t + 1, :] = corner
            arrived(5, still_recv.at[0 : 2 * K - 1])
            arrived(9, answer_near.at[0, 1:SWEEPS])
            for k in range(K):
                for side in range(2):
                    for h in range(2):
                        for m in range(1, SWEEPS):
                            still_all[h, m, side, 2 * k : 2 * k + 2, :] = still_recv[
                                2 * k + h, m - 1, side
                            ]
        arrived(group + 3, tops_recv.at[step, 0 : 2 * K - 1, 0:SWEEPS])
        arrived(15 + step, tops_recv.at[step, 0 : len(plane_next), SWEEPS])
        for k in range(K):
            for j in range(SWEEPS + 1):
                for h in range(2):
                    tops_all[h, j, 2 * k : 2 * k + 2, :] = tops_recv[step, 2 * k + h, j]
        arrived(13 + step, near.at[step, 0])
        spot = lax.broadcasted_iota(jnp.int32, (2 * K, HC), 0)
        even = spot % 2 == 0
        mine = pl.ds(2 * plane, 1)
        halves = []
        for h in range(2):
            from_above, from_below = [], []
            for j in range(SWEEPS + 1):
                value = tops_all[h, j]
                for i in range(j):
                    value = value + still_all[h, j - i - 1, 0] * from_above[i]
                    value = value + still_all[h, j - i - 1, 1] * from_below[i]
                over = jnp.where(even, pltpu.roll(value, 1, 0), pltpu.roll(value, 2, 0))
                under = jnp.where(
                    even, pltpu.roll(value, 2 * K - 2, 0), pltpu.roll(value, 2 * K - 1, 0)
                )
                from_above.append(jnp.where(spot < 2, 0.0, over))
                from_below.append(jnp.where(spot >= 2 * K - 2, 0.0, under))
                inflow[h, j, 0] = from_above[j]
                inflow[h, j, 1] = from_below[j]
            nearby = near[step, h]
            for i in range(SWEEPS):
                m = SWEEPS - 1 - i
                nearby = nearby + (
                    answer_near[h, m, 0] * inflow[h, i, 0, mine, :]
                    + answer_near[h, m, 1] * inflow[h, i, 1, mine, :]
                )
            above, below = nearby[:1], nearby[1 + RD : 2 + RD]
            above = jnp.where(place == 0, inflow[h, SWEEPS, 0, mine, :], above)
            below = jnp.where(place == Q - 1, inflow[h, SWEEPS, 1, mine, :], below)
            halves.append((above, nearby[1 : 1 + RD], below))

        def joined(first, second):
            over = HC - cut
            lanes = lax.broadcasted_iota(jnp.int32, (first.shape[0], over), 1)
            both = jnp.where(lanes < over // 2, first[:, cut:], second[:, :over])
            return jnp.concatenate([first[:, :cut], both, second[:, over:]], axis=1)

        row_above, current, row_below = (joined(a, b) for a, b in zip(*halves))
        row_above = jnp.where(strip == 0, current[:1], row_above)
        row_below = jnp.where(strip == strips - 1, current[RD - 1 :], row_below)

    density_ref[...] = current
    last_send[0:1, :] = row_above
    last_send[1 : 1 + RD, :] = current
    last_send[1 + RD : 2 + RD, :] = row_below
    last_send[2 + RD : 8, :] = jnp.zeros((6 - RD, NC), f32)
    last_recv[cell] = last_send[...]
    for peer in cell_peers:
        send(12, last_send, last_recv.at[cell], peer)
    arrived(12, last_recv.at[0 : C - 1])
    field = jnp.concatenate([last_recv[c] for c in range(C)], axis=1)
    centre = field[1 : 1 + RD]
    spot = lax.broadcasted_iota(jnp.int32, (RD, C * NC), 1)
    left = jnp.where(spot == 0, centre, pltpu.roll(centre, 1, 1))
    right = jnp.where(spot == C * NC - 1, centre, pltpu.roll(centre, C * NC - 1, 1))
    scale = jnp.maximum(centre, floor_level)
    velocity_y = -(0.5 * (field[2 : 2 + RD] - field[:RD])) / scale
    velocity_x = -(0.5 * (right - left)) / scale
    tables = []
    for i, velocity in enumerate((velocity_y, velocity_x)):
        vel_bins[i, bins:, :] = jnp.zeros((128 - bins, 128), f32)
        for n in range(bins // RD):
            vel_bins[i, RD * n : RD * (n + 1), :] = velocity[:, 128 * n : 128 * (n + 1)]
        turned = jnp.transpose(vel_bins[i])
        past = jnp.broadcast_to(pltpu.roll(turned[:8], 128 - RD, 1)[:1], (8, 128))
        tables += [turned.astype(bf16), past.astype(bf16)]
    tables = jnp.concatenate(tables, axis=0)

    def sample(i, carry):
        sampled = jnp.dot(tables, look[i], preferred_element_type=f32)
        across = spread[i]
        out_y = jnp.sum(sampled[:136] * across, axis=0, keepdims=True)
        out_x = jnp.sum(sampled[136:] * across, axis=0, keepdims=True)
        span = pl.ds(pl.multiple_of(256 * i, 256), 256)
        pinv_ref[:, span] = jnp.concatenate([out_y, out_x], axis=0)
        return carry

    lax.fori_loop(0, chunks // 2, sample, 0, unroll=4)
    for group, span in sent:
        pltpu.make_async_copy(span, span, send_sem.at[group]).wait()


def diffuse(pin_rows, pin_cols, pin_fracs, pin_weights, capacity, blockage, row_blocks, col_blocks):
    pins = pin_rows.shape[0]
    chunks = pins // 128
    strips = lax.axis_size("strip")
    C = lax.axis_size("cells")
    RD, NC = capacity.shape
    NB = row_blocks.shape[0]
    K, BL = col_blocks.shape[:2]
    Q = strips // K
    HC = 128 * ((NB + 1) // 2)
    vmem = pl.BlockSpec(memory_space=pltpu.VMEM)
    bins = RD * C * NC // 128
    shapes = [
        ((chunks, 128), jnp.int32),
        ((chunks, 128), jnp.int32),
        ((chunks, 128), f32),
        ((2, pins), f32),
        ((RD, NC), jnp.int32),
        ((RD, NC), f32),
        ((NB, 128, 128), f32),
        ((K, BL, BL), f32),
        ((bins, 128), f32),
        ((C, RD, NC), f32),
        ((chunks // 2, 128, 256), bf16),
        ((chunks // 2, 136, 256), f32),
        ((2, 128, 128), f32),
        ((2, C, 1, NC), f32),
        ((C, RD, NC), f32),
        ((2, C, 1, NC), f32),
        ((2, 1, NC), f32),
        ((2, 1, NC), f32),
        ((2, RD, HC), jnp.int16),
        ((Q, RD, HC), jnp.int16),
        ((BL, HC), f32),
        ((NB, 128, 384), bf16),
        ((BL, 3 * BL), bf16),
        ((STEPS, 2, RD, 128), f32),
        ((STEPS, 2, RD, 128), f32),
        ((STEPS, 2, RD, HC), f32),
        ((STEPS, Q, RD, HC), f32),
        ((BL, HC), f32),
        ((BL + 16, HC), f32),
        ((SWEEPS - 1, 2, 8, HC), f32),
        ((2, SWEEPS, 2, 8, HC), f32),
        ((STEPS, 8, HC), f32),
        ((STEPS, 2, 8, HC), f32),
        ((SWEEPS - 1, 2, 2, HC), f32),
        ((2 * K, SWEEPS - 1, 2, 2, HC), f32),
        ((2, SWEEPS, 2, 2 * K, HC), f32),
        ((STEPS, SWEEPS + 1, 2, HC), f32),
        ((STEPS, 2 * K, SWEEPS + 1, 2, HC), f32),
        ((2, SWEEPS + 1, 2 * K, HC), f32),
        ((2, SWEEPS + 1, 2, 2 * K, HC), f32),
        ((8, NC), f32),
        ((C, 8, NC), f32),
    ]
    results = pl.pallas_call(
        functools.partial(adi_kernel, (K, Q, C, RD, NC, BL)),
        out_shape=(
            jax.ShapeDtypeStruct((RD, NC), f32),
            jax.ShapeDtypeStruct((2, pins), f32),
        ),
        in_specs=[pl.BlockSpec(memory_space=pltpu.HBM)] * 8,
        out_specs=(vmem, vmem),
        scratch_shapes=[pltpu.VMEM(shape, dtype) for shape, dtype in shapes]
        + [pltpu.SemaphoreType.DMA((n,)) for n in (17, 17, 8)],
        compiler_params=pltpu.CompilerParams(collective_id=0, has_side_effects=True),
        name="adi",
    )(
        pin_rows.reshape(chunks, 128),
        pin_cols.reshape(chunks, 128),
        pin_fracs,
        pin_weights.reshape(chunks, 128),
        capacity,
        blockage,
        row_blocks,
        col_blocks,
    )
    return pl.pallas_call(
        hand_over,
        out_shape=[jax.ShapeDtypeStruct(r.shape, r.dtype) for r in results],
        in_specs=[vmem] * 2,
        out_specs=[vmem] * 2,
        name="hand_over",
    )(*results)


def hand_over(first, second, first_out, second_out):
    first_out[...] = first[...]
    second_out[...] = second[...]


def solution(mesh):
    placed = (
        P(("strip", "cells")),
        P(("strip", "cells")),
        P(None, ("strip", "cells")),
        P(("strip", "cells")),
        P("strip", "cells"),
        P("strip", "cells"),
        P("cells", None, None),
        P(),
    )
    return jax.shard_map(
        diffuse,
        mesh=mesh,
        in_specs=placed,
        out_specs=(P("strip", "cells"), P(None, ("strip", "cells"))),
        check_vma=False,
    )
```

```python
import functools

import jax
import jax.numpy as jnp
from jax import lax
from jax.experimental import pallas as pl
from jax.experimental.pallas import tpu as pltpu
from jax.sharding import PartitionSpec as P

SWEEPS = 3
STEPS = 2
coupling = 2.0
floor_level = 0.5
w_steps = 8191.0
f32 = jnp.float32
bf16 = jnp.bfloat16


def exact_parts(values):
    high = values.astype(bf16)
    return high, (values - high.astype(f32)).astype(bf16)


def row_product(values, blocks_ref):
    pieces = []
    for n in range(blocks_ref.shape[0]):
        high, low = exact_parts(values[:, 128 * n : 128 * (n + 1)])
        pieces.append(
            lax.dot_general(
                jnp.concatenate([high, low, high], axis=1),
                blocks_ref[n],
                (((1,), (1,)), ((), ())),
                preferred_element_type=f32,
            )
        )
    return jnp.concatenate(pieces, axis=1)


def col_product(matrix_ref, values):
    high, low = exact_parts(values)
    parts = jnp.concatenate([high, low, high], axis=0)
    return jnp.dot(matrix_ref[...], parts, preferred_element_type=f32)


def table(index, first, second, count):
    spot = lax.broadcasted_iota(jnp.int32, (count, index.shape[1]), 0)
    return jnp.where(spot == index, first, jnp.where(spot == index + 1, second, 0.0))


def adi_kernel(
    sizes,
    rows_hbm,
    cols_hbm,
    fracs_hbm,
    pinw_hbm,
    cap_hbm,
    blk_hbm,
    rowb_hbm,
    colb_hbm,
    density_ref,
    pinv_ref,
    rows_ref,
    cols_ref,
    pinw_ref,
    fracs_ref,
    cap_ref,
    blk_ref,
    rowb_ref,
    colb_ref,
    bin_sums,
    part_ref,
    look,
    spread,
    vel_bins,
    edge_part,
    part_recv,
    edge_recv,
    wedge_send,
    wedge_recv,
    w_send,
    w_plane,
    w_block,
    rowb_parts,
    colb_parts,
    rim_send,
    rim_recv,
    field_send,
    field_plane,
    field_block,
    padded,
    answer_send,
    answer_near,
    near_send,
    near,
    still_send,
    still_recv,
    still_all,
    tops_send,
    tops_recv,
    tops_all,
    inflow,
    last_send,
    last_recv,
    send_sem,
    recv_sem,
    load_sem,
):
    K, Q, C, RD, NC, BL = sizes
    strips = K * Q
    HC = w_send.shape[2]
    cut = NC - HC
    strip = lax.axis_index("strip")
    cell = lax.axis_index("cells")
    plane = strip // Q
    place = strip % Q
    depth = Q // 2
    half = (place // 2) % 2
    strip_side = place % 2
    first_cell, last_cell = cell == 0, cell == C - 1
    first_plane, last_plane = plane == 0, plane == K - 1

    def at(strip_id, cell_id):
        return (strip_id, cell_id)

    cell_peers = [at(strip, (cell + d) % C) for d in range(1, C)]
    above_strip, below_strip = (strip + strips - 1) % strips, (strip + 1) % strips
    offsets = [(dz, dy) for dz in range(depth) for dy in range(2) if (dz, dy) != (0, 0)]
    offsets.sort(key=lambda o: -(min(o[0], depth - o[0]) + 2 * o[1]))
    plane_peers = []
    for dz, dy in offsets:
        other = ((place // 2 + dz) % depth) * 2 + (place % 2 + dy) % 2
        plane_peers.append((at(plane * Q + other, cell), (half + dz) % 2))
    partner = at(strip + 2 - 4 * half, cell)
    shifts = [(dk, dz) for dk in range(K) for dz in range(2) if (dk, dz) != (0, 0)]
    shifts.sort(key=lambda o: -(min(o[0], K - o[0]) + o[1]))
    plane_cross = [
        at(((plane + dk) % K) * Q + place + dz * (2 - 4 * half), cell) for dk, dz in shifts
    ]
    slot = 2 * plane + half
    plane_next = [
        at(((plane + dk) % K) * Q + place + dz * (2 - 4 * half), cell)
        for dk, dz in shifts
        if dk in (1, K - 1)
    ]
    row_peers = [at(s, (cell + d) % C) for s in (above_strip, below_strip) for d in range(C)]

    barrier = pltpu.get_barrier_semaphore()
    greeted = cell_peers + [p for p, _ in plane_peers] + plane_cross + row_peers
    for peer in greeted:
        pl.semaphore_signal(barrier, 1, device_id=peer, device_id_type=pl.DeviceIdType.MESH)

    sent = []

    def send(group, source, target, peer):
        pltpu.make_async_remote_copy(
            src_ref=source,
            dst_ref=target,
            send_sem=send_sem.at[group],
            recv_sem=recv_sem.at[group],
            device_id=peer,
            device_id_type=pl.DeviceIdType.MESH,
        ).start()

    def arrived(group, span):
        sent.append((group, span))
        pltpu.make_async_copy(span, span, recv_sem.at[group]).wait()

    loads = [
        pltpu.make_async_copy(source, target, load_sem.at[i])
        for i, (source, target) in enumerate(
            (
                (rows_hbm, rows_ref),
                (cols_hbm, cols_ref),
                (pinw_hbm, pinw_ref),
                (fracs_hbm, fracs_ref),
                (cap_hbm, cap_ref),
                (blk_hbm, blk_ref),
                (rowb_hbm, rowb_ref),
                (colb_hbm, colb_ref),
            )
        )
    ]
    for load in loads:
        load.start()
    for load in loads:
        load.wait()

    chunks = rows_ref.shape[0]
    bins = bin_sums.shape[0]

    def pins_of(i):
        span = pl.ds(pl.multiple_of(128 * i, 128), 128)
        down, across = fracs_ref[0:1, span], fracs_ref[1:2, span]
        column = cols_ref[pl.ds(i, 1), :]
        tile = lax.shift_right_logical(column, 7)
        return down, across, tile * RD + rows_ref[pl.ds(i, 1), :], column - tile * 128

    def rounded(values):
        return values.astype(bf16).astype(f32)

    def add_pins(i, total):
        down, across, index, lane = pins_of(i)
        heavy = pinw_ref[pl.ds(i, 1), :]
        where_down = table(index, rounded(heavy * (1.0 - down)), rounded(heavy * down), bins)
        where_across = table(lane, rounded(1.0 - across), rounded(across), 136)
        return total + lax.dot_general(
            where_down.astype(bf16),
            where_across.astype(bf16),
            (((1,), (1,)), ((), ())),
            preferred_element_type=f32,
        )

    total = lax.fori_loop(0, chunks, add_pins, jnp.zeros((bins, 136), f32), unroll=4)
    spot = lax.broadcasted_iota(jnp.int32, (bins, 128), 1)
    past = jnp.where(spot == 0, total[:, 128:129], 0.0)
    bin_sums[...] = total[:, :128] + pltpu.roll(past, RD, 0)
    for c in range(C):
        for n in range(NC // 128):
            tile = c * (NC // 128) + n
            part_ref[c, :, 128 * n : 128 * (n + 1)] = bin_sums[RD * tile : RD * (tile + 1), :]

    weights = cap_ref[...].astype(f32) * (1.0 - blk_ref[...])
    whole = jnp.round(weights * w_steps).astype(jnp.int32).astype(jnp.int16)
    w_send[0] = whole[:, :HC]
    w_send[1] = whole[:, cut:]
    w_plane[place] = w_send[half]
    wedge_send[0] = weights[:1]
    wedge_send[1] = weights[RD - 1 :]
    for c in range(C):
        edge_part[0, c] = part_ref[c, :1]
        edge_part[1, c] = part_ref[c, RD - 1 :]
    pl.semaphore_wait(barrier, len(greeted))

    for d in range(C):
        other = (cell + d) % C
        send(1, edge_part.at[0, other], edge_recv.at[1, cell], at(above_strip, other))
        send(1, edge_part.at[1, other], edge_recv.at[0, cell], at(below_strip, other))
    send(2, wedge_send.at[0], wedge_recv.at[1], at(above_strip, cell))
    send(2, wedge_send.at[1], wedge_recv.at[0], at(below_strip, cell))
    for d in range(1, C):
        other = (cell + d) % C
        send(0, part_ref.at[other], part_recv.at[C - 1 - d], at(strip, other))
    for peer, other_half in plane_peers:
        send(3, w_send.at[other_half], w_plane.at[place], peer)

    for n in range(rowb_ref.shape[0]):
        high, low = exact_parts(rowb_ref[n])
        rowb_parts[n] = jnp.concatenate([high, high, low], axis=1)
    high, low = exact_parts(colb_ref[plane])
    colb_parts[...] = jnp.concatenate([high, high, low], axis=1)

    end = lax.broadcasted_iota(jnp.int32, (RD, HC), 1)

    def along_inside(values):
        left = pltpu.roll(values, 1, 1)
        right = pltpu.roll(values, NC - 1, 1)
        spot = lax.broadcasted_iota(jnp.int32, values.shape, 1)
        left = jnp.where(spot == 0, jnp.where(first_cell, values, 0.0), left)
        right = jnp.where(spot == NC - 1, jnp.where(last_cell, values, 0.0), right)
        return 2.0 * values - left - right

    weights_two = jnp.concatenate([weights, weights], axis=0)
    spot = lax.broadcasted_iota(jnp.int32, (2 * RD, NC), 1)
    row = lax.broadcasted_iota(jnp.int32, (2 * RD, NC), 0)
    unit = jnp.where(spot == jnp.where(row < RD, 0, NC - 1), coupling, 0.0)
    pulse = row_product(unit, rowb_parts)
    pulses = [pulse]
    for _ in range(SWEEPS - 1):
        back = weights_two * pulse + coupling * along_inside(pulse)
        pulse = pulse - row_product(back, rowb_parts)
        pulses.append(pulse)

    arrived(1, edge_recv)
    arrived(2, wedge_recv)
    arrived(0, part_recv.at[0 : C - 1])
    density = part_ref[cell]
    for d in range(C - 1):
        density = density + part_recv[d]
    current = density / weights
    row_above = edge_recv[0, 0]
    row_below = edge_recv[1, 0]
    for c in range(1, C):
        row_above = row_above + edge_recv[0, c]
        row_below = row_below + edge_recv[1, c]
    row_above = row_above / wedge_recv[0]
    row_below = row_below / wedge_recv[1]
    row_above = jnp.where(strip == 0, current[:1], row_above)
    row_below = jnp.where(strip == strips - 1, current[RD - 1 :], row_below)

    def frame(pair):
        base = pl.multiple_of(RD * 2 * pair, 2 * RD)
        inner = padded[pl.ds(base + 8, 2 * RD), :]
        over = padded[pl.ds(base + 7, 1), :]
        under = padded[pl.ds(base + 8 + 2 * RD, 1), :]
        fill = jnp.zeros((6 - RD, HC), f32)
        upper = jnp.concatenate([over, inner[: RD + 1], fill], axis=0)
        lower = jnp.concatenate([inner[RD - 1 :], under, fill], axis=0)
        return jnp.where(strip_side == 0, upper, lower)

    def frames():
        return frame(place // 2), frame(place // 2 + 1 - 2 * half)

    small = lax.broadcasted_iota(jnp.int32, (RD, 128), 1)

    def clamp_rows(values):
        shape = values.shape
        spot = lax.broadcasted_iota(jnp.int32, shape, 0)
        up = pltpu.roll(values, 1, 0)
        down = pltpu.roll(values, shape[0] - 1, 0)
        up = jnp.where(spot == 0, jnp.where(first_plane, values, 0.0), up)
        down = jnp.where(spot == shape[0] - 1, jnp.where(last_plane, values, 0.0), down)
        return 2.0 * values - up - down

    for step in range(STEPS):
        up = jnp.concatenate([row_above, current[: RD - 1]], axis=0)
        down = jnp.concatenate([current[1:], row_below], axis=0)
        source = weights * current - coupling * (2.0 * current - up - down)
        iterate = current
        levels = [iterate]
        for _ in range(SWEEPS):
            left_over = source - (weights * iterate + coupling * along_inside(iterate))
            iterate = iterate + row_product(left_over, rowb_parts)
            levels.append(iterate)
        for side, column in ((0, 0), (1, NC - 1)):
            message = jnp.zeros((RD, 128), f32)
            for j in range(SWEEPS + 1):
                message = jnp.where(small == j, levels[j][:, column : column + 1], message)
            for m in range(SWEEPS):
                mine = pulses[m][side * RD : (side + 1) * RD, column : column + 1]
                message = jnp.where(small == SWEEPS + 1 + m, mine, message)
            rim_send[step, side] = message
        group = 4 + 4 * step
        send(group, rim_send.at[step, 0], rim_recv.at[step, 1], at(strip, (cell + C - 1) % C))
        send(group, rim_send.at[step, 1], rim_recv.at[step, 0], at(strip, (cell + 1) % C))

        arrived(group, rim_recv.at[step])
        edges = []
        for side in range(2):
            own = [rim_send[step, side][:, i : i + 1] for i in range(2 * SWEEPS + 1)]
            far = [rim_recv[step, side][:, i : i + 1] for i in range(2 * SWEEPS + 1)]
            mine, theirs = [], []
            for j in range(SWEEPS + 1):
                a, b = own[j], far[j]
                for i in range(j):
                    a = a + own[SWEEPS + j - i] * theirs[i]
                    b = b + far[SWEEPS + j - i] * mine[i]
                mine.append(a)
                theirs.append(b)
            edges.append(theirs)
        left_in = [jnp.where(first_cell, 0.0, e) for e in edges[0]]
        right_in = [jnp.where(last_cell, 0.0, e) for e in edges[1]]
        for i in range(SWEEPS):
            iterate = iterate + (
                pulses[SWEEPS - 1 - i][:RD] * left_in[i] + pulses[SWEEPS - 1 - i][RD:] * right_in[i]
            )
        halo_left = jnp.where(first_cell, iterate[:, :1], left_in[SWEEPS])
        halo_right = jnp.where(last_cell, iterate[:, NC - 1 :], right_in[SWEEPS])
        field_send[step, 0] = jnp.where(end == HC - 1, halo_left, iterate[:, :HC])
        field_send[step, 1] = jnp.where(end == 0, halo_right, iterate[:, cut:])
        field_plane[step, place] = field_send[step, half]
        for peer, other_half in plane_peers:
            send(group + 2, field_send.at[step, other_half], field_plane.at[step, place], peer)
        if step == 0:
            arrived(3, w_plane.at[0 : Q - 1])
            for i in range(Q):
                stepped = w_plane[i].astype(jnp.int32).astype(f32)
                w_block[RD * i : RD * (i + 1), :] = stepped * (1.0 / w_steps)
            padded[0:8, :] = jnp.zeros((8, HC), f32)
            padded[BL + 8 :, :] = jnp.zeros((8, HC), f32)
            for side, column in ((0, 0), (1, BL - 1)):
                answer = coupling * jnp.broadcast_to(
                    colb_ref[plane][:, column : column + 1], (BL, HC)
                )
                for m in range(SWEEPS):
                    if m > 0:
                        back = w_block[...] * answer + coupling * clamp_rows(answer)
                        answer = answer - col_product(colb_parts, back)
                    padded[8 : BL + 8, :] = answer
                    own, other = frames()
                    answer_near[half, m, side] = own
                    if m == 0:
                        answer_near[1 - half, m, side] = own
                    else:
                        answer_send[m - 1, side] = other
                        still_send[m - 1, side, 0:1, :] = answer[:1]
                        still_send[m - 1, side, 1:2, :] = answer[BL - 1 :]
            still_recv[slot] = still_send[...]
            for peer in plane_cross:
                send(5, still_send, still_recv.at[slot], peer)
        else:

            def prepare(i, carry):
                for k in range(2):
                    down, across, index, lane = pins_of(2 * i + k)
                    part = slice(128 * k, 128 * (k + 1))
                    nearer, farther = rounded(1.0 - down), rounded(down)
                    look[i, :, part] = table(index, nearer, farther, 128).astype(bf16)
                    spread[i, :, part] = table(lane, rounded(1.0 - across), rounded(across), 136)
                return carry

            lax.fori_loop(0, chunks // 2, prepare, 0)

        arrived(group + 2, field_plane.at[step, 0 : Q - 1])
        if step == 0:
            send(9, answer_send, answer_near.at[half, 1:SWEEPS], partner)
        for i in range(Q):
            field_block[RD * i : RD * (i + 1), :] = field_plane[step, i]

        start = field_block[...]
        beside = pltpu.roll(start, 1, 1) + pltpu.roll(start, HC - 1, 1)
        middle = w_block[...] * start - coupling * (2.0 * start - beside)
        iterate = start
        for j in range(SWEEPS + 1):
            if j == SWEEPS:
                for peer in plane_cross:
                    send(
                        group + 3,
                        tops_send.at[step, 0:SWEEPS],
                        tops_recv.at[step, slot, 0:SWEEPS],
                        peer,
                    )
            if j > 0:
                left_over = middle - (w_block[...] * iterate + coupling * clamp_rows(iterate))
                iterate = iterate + col_product(colb_parts, left_over)
            tops_send[step, j, 0:1, :] = iterate[:1]
            tops_send[step, j, 1:2, :] = iterate[BL - 1 :]
        for peer in plane_next:
            send(
                15 + step,
                tops_send.at[step, SWEEPS],
                tops_recv.at[step, slot, SWEEPS],
                peer,
            )
        padded[8 : BL + 8, :] = iterate
        own, other = frames()
        near_send[step] = other
        near[step, half] = own
        send(13 + step, near_send.at[step], near.at[step, half], partner)
        tops_recv[step, slot] = tops_send[step]

        if step == 0:
            for k in range(K):
                for side, column in ((0, 0), (1, BL - 1)):
                    for t, line in ((0, 0), (1, BL - 1)):
                        corner = coupling * colb_ref[k][line : line + 1, column : column + 1]
                        corner = jnp.broadcast_to(corner, (1, HC))
                        for h in range(2):
                            still_all[h, 0, side, 2 * k + t : 2 * k + t + 1, :] = corner
            arrived(5, still_recv.at[0 : 2 * K - 1])
            arrived(9, answer_near.at[0, 1:SWEEPS])
            for k in range(K):
                for side in range(2):
                    for h in range(2):
                        for m in range(1, SWEEPS):
                            still_all[h, m, side, 2 * k : 2 * k + 2, :] = still_recv[
                                2 * k + h, m - 1, side
                            ]
        arrived(group + 3, tops_recv.at[step, 0 : 2 * K - 1, 0:SWEEPS])
        arrived(15 + step, tops_recv.at[step, 0 : len(plane_next), SWEEPS])
        for k in range(K):
            for j in range(SWEEPS + 1):
                for h in range(2):
                    tops_all[h, j, 2 * k : 2 * k + 2, :] = tops_recv[step, 2 * k + h, j]
        arrived(13 + step, near.at[step, 0])
        spot = lax.broadcasted_iota(jnp.int32, (2 * K, HC), 0)
        even = spot % 2 == 0
        mine = pl.ds(2 * plane, 1)
        halves = []
        for h in range(2):
            from_above, from_below = [], []
            for j in range(SWEEPS + 1):
                value = tops_all[h, j]
                for i in range(j):
                    value = value + still_all[h, j - i - 1, 0] * from_above[i]
                    value = value + still_all[h, j - i - 1, 1] * from_below[i]
                over = jnp.where(even, pltpu.roll(value, 1, 0), pltpu.roll(value, 2, 0))
                under = jnp.where(
                    even, pltpu.roll(value, 2 * K - 2, 0), pltpu.roll(value, 2 * K - 1, 0)
                )
                from_above.append(jnp.where(spot < 2, 0.0, over))
                from_below.append(jnp.where(spot >= 2 * K - 2, 0.0, under))
                inflow[h, j, 0] = from_above[j]
                inflow[h, j, 1] = from_below[j]
            nearby = near[step, h]
            for i in range(SWEEPS):
                m = SWEEPS - 1 - i
                nearby = nearby + (
                    answer_near[h, m, 0] * inflow[h, i, 0, mine, :]
                    + answer_near[h, m, 1] * inflow[h, i, 1, mine, :]
                )
            above, below = nearby[:1], nearby[1 + RD : 2 + RD]
            above = jnp.where(place == 0, inflow[h, SWEEPS, 0, mine, :], above)
            below = jnp.where(place == Q - 1, inflow[h, SWEEPS, 1, mine, :], below)
            halves.append((above, nearby[1 : 1 + RD], below))

        def joined(first, second):
            over = HC - cut
            lanes = lax.broadcasted_iota(jnp.int32, (first.shape[0], over), 1)
            both = jnp.where(lanes < over // 2, first[:, cut:], second[:, :over])
            return jnp.concatenate([first[:, :cut], both, second[:, over:]], axis=1)

        row_above, current, row_below = (joined(a, b) for a, b in zip(*halves))
        row_above = jnp.where(strip == 0, current[:1], row_above)
        row_below = jnp.where(strip == strips - 1, current[RD - 1 :], row_below)

    density_ref[...] = current
    last_send[0:1, :] = row_above
    last_send[1 : 1 + RD, :] = current
    last_send[1 + RD : 2 + RD, :] = row_below
    last_send[2 + RD : 8, :] = jnp.zeros((6 - RD, NC), f32)
    last_recv[cell] = last_send[...]
    for peer in cell_peers:
        send(12, last_send, last_recv.at[cell], peer)
    arrived(12, last_recv.at[0 : C - 1])
    field = jnp.concatenate([last_recv[c] for c in range(C)], axis=1)
    centre = field[1 : 1 + RD]
    spot = lax.broadcasted_iota(jnp.int32, (RD, C * NC), 1)
    left = jnp.where(spot == 0, centre, pltpu.roll(centre, 1, 1))
    right = jnp.where(spot == C * NC - 1, centre, pltpu.roll(centre, C * NC - 1, 1))
    scale = jnp.maximum(centre, floor_level)
    velocity_y = -(0.5 * (field[2 : 2 + RD] - field[:RD])) / scale
    velocity_x = -(0.5 * (right - left)) / scale
    tables = []
    for i, velocity in enumerate((velocity_y, velocity_x)):
        vel_bins[i, bins:, :] = jnp.zeros((128 - bins, 128), f32)
        for n in range(bins // RD):
            vel_bins[i, RD * n : RD * (n + 1), :] = velocity[:, 128 * n : 128 * (n + 1)]
        turned = jnp.transpose(vel_bins[i])
        past = jnp.broadcast_to(pltpu.roll(turned[:8], 128 - RD, 1)[:1], (8, 128))
        tables += [turned.astype(bf16), past.astype(bf16)]
    tables = jnp.concatenate(tables, axis=0)

    def sample(i, carry):
        sampled = jnp.dot(tables, look[i], preferred_element_type=f32)
        across = spread[i]
        out_y = jnp.sum(sampled[:136] * across, axis=0, keepdims=True)
        out_x = jnp.sum(sampled[136:] * across, axis=0, keepdims=True)
        span = pl.ds(pl.multiple_of(256 * i, 256), 256)
        pinv_ref[:, span] = jnp.concatenate([out_y, out_x], axis=0)
        return carry

    lax.fori_loop(0, chunks // 2, sample, 0, unroll=4)
    for group, span in sent:
        pltpu.make_async_copy(span, span, send_sem.at[group]).wait()


def diffuse(pin_rows, pin_cols, pin_fracs, pin_weights, capacity, blockage, row_blocks, col_blocks):
    pins = pin_rows.shape[0]
    chunks = pins // 128
    strips = lax.axis_size("strip")
    C = lax.axis_size("cells")
    RD, NC = capacity.shape
    NB = row_blocks.shape[0]
    K, BL = col_blocks.shape[:2]
    Q = strips // K
    HC = 128 * ((NB + 1) // 2)
    vmem = pl.BlockSpec(memory_space=pltpu.VMEM)
    bins = RD * C * NC // 128
    shapes = [
        ((chunks, 128), jnp.int32),
        ((chunks, 128), jnp.int32),
        ((chunks, 128), f32),
        ((2, pins), f32),
        ((RD, NC), jnp.int32),
        ((RD, NC), f32),
        ((NB, 128, 128), f32),
        ((K, BL, BL), f32),
        ((bins, 128), f32),
        ((C, RD, NC), f32),
        ((chunks // 2, 128, 256), bf16),
        ((chunks // 2, 136, 256), f32),
        ((2, 128, 128), f32),
        ((2, C, 1, NC), f32),
        ((C, RD, NC), f32),
        ((2, C, 1, NC), f32),
        ((2, 1, NC), f32),
        ((2, 1, NC), f32),
        ((2, RD, HC), jnp.int16),
        ((Q, RD, HC), jnp.int16),
        ((BL, HC), f32),
        ((NB, 128, 384), bf16),
        ((BL, 3 * BL), bf16),
        ((STEPS, 2, RD, 128), f32),
        ((STEPS, 2, RD, 128), f32),
        ((STEPS, 2, RD, HC), f32),
        ((STEPS, Q, RD, HC), f32),
        ((BL, HC), f32),
        ((BL + 16, HC), f32),
        ((SWEEPS - 1, 2, 8, HC), f32),
        ((2, SWEEPS, 2, 8, HC), f32),
        ((STEPS, 8, HC), f32),
        ((STEPS, 2, 8, HC), f32),
        ((SWEEPS - 1, 2, 2, HC), f32),
        ((2 * K, SWEEPS - 1, 2, 2, HC), f32),
        ((2, SWEEPS, 2, 2 * K, HC), f32),
        ((STEPS, SWEEPS + 1, 2, HC), f32),
        ((STEPS, 2 * K, SWEEPS + 1, 2, HC), f32),
        ((2, SWEEPS + 1, 2 * K, HC), f32),
        ((2, SWEEPS + 1, 2, 2 * K, HC), f32),
        ((8, NC), f32),
        ((C, 8, NC), f32),
    ]
    results = pl.pallas_call(
        functools.partial(adi_kernel, (K, Q, C, RD, NC, BL)),
        out_shape=(
            jax.ShapeDtypeStruct((RD, NC), f32),
            jax.ShapeDtypeStruct((2, pins), f32),
        ),
        in_specs=[pl.BlockSpec(memory_space=pltpu.HBM)] * 8,
        out_specs=(vmem, vmem),
        scratch_shapes=[pltpu.VMEM(shape, dtype) for shape, dtype in shapes]
        + [pltpu.SemaphoreType.DMA((n,)) for n in (17, 17, 8)],
        compiler_params=pltpu.CompilerParams(collective_id=0, has_side_effects=True),
        name="adi",
    )(
        pin_rows.reshape(chunks, 128),
        pin_cols.reshape(chunks, 128),
        pin_fracs,
        pin_weights.reshape(chunks, 128),
        capacity,
        blockage,
        row_blocks,
        col_blocks,
    )
    return pl.pallas_call(
        hand_over,
        out_shape=[jax.ShapeDtypeStruct(r.shape, r.dtype) for r in results],
        in_specs=[vmem] * 2,
        out_specs=[vmem] * 2,
        name="hand_over",
    )(*results)


def hand_over(first, second, first_out, second_out):
    first_out[...] = first[...]
    second_out[...] = second[...]


def solution(mesh):
    placed = (
        P(("strip", "cells")),
        P(("strip", "cells")),
        P(None, ("strip", "cells")),
        P(("strip", "cells")),
        P("strip", "cells"),
        P("strip", "cells"),
        P("cells", None, None),
        P(),
    )
    return jax.shard_map(
        diffuse,
        mesh=mesh,
        in_specs=placed,
        out_specs=(P("strip", "cells"), P(None, ("strip", "cells"))),
        check_vma=False,
    )
```
